32 devices in a mesh: narrow: 4 (over y, core), wide: 8 (over z, x).
Axes of the slice: x: 2, y: 2, z: 4, core: 2. Of those that a mesh axis runs over, the one named last changes fastest.
Arguments:
- tokens: bfloat16 [16384, 768], P(('narrow', 'wide')), may hold values from -6 to 6
- attn_gain: bfloat16 [768], replicated, may hold values from 0.5 to 1.5
- attn_shift: bfloat16 [768], replicated, may hold values from -2 to 2
- in_weight: bfloat16 [768, 2304], replicated, may hold values from -0.21875 to 0.21875
- query_value_bias: bfloat16 [2, 768], replicated, may hold values from -3 to 3
- proj_weight: bfloat16 [768, 768], replicated, may hold values from -1.75 to 1.75
- proj_bias: bfloat16 [768], replicated, may hold values from -2 to 2
- attn_scale: bfloat16 [768], replicated, may hold values from 0.5 to 1.5
- mlp_gain: bfloat16 [768], replicated, may hold values from 0.5 to 1.5
- mlp_shift: bfloat16 [768], replicated, may hold values from -2 to 2
- up_weight: bfloat16 [768, 3072], replicated, may hold values from -0.21875 to 0.21875
- up_bias: bfloat16 [3072], replicated, may hold values from -2 to 2
- down_weight: bfloat16 [3072, 768], replicated, may hold values from -0.109375 to 0.109375
- down_bias: bfloat16 [768], replicated, may hold values from -2 to 2
- mlp_scale: bfloat16 [768], replicated, may hold values from 0.5 to 1.5
- crop_lengths: int32 [16, 10], P('narrow'), may hold values from 24 to 261, as said below
- out_grad: bfloat16 [16384, 768], P(('narrow', 'wide')), may hold values from -6 to 6
Outputs:
- output: bfloat16 [16384, 768], P(('narrow', 'wide'))
- input_grad: bfloat16 [16384, 768], P(('narrow', 'wide'))
- grad_attn_gain: float32 [768], P('wide')
- grad_attn_shift: float32 [768], P('wide')
- grad_in_weight: float32 [768, 2304], P('wide')
- grad_query_value_bias: float32 [2, 768], P(None, 'wide')
- grad_proj_weight: float32 [768, 768], P('wide')
- grad_proj_bias: float32 [768], P('wide')
- grad_attn_scale: float32 [768], P('wide')
- grad_mlp_gain: float32 [768], P('wide')
- grad_mlp_shift: float32 [768], P('wide')
- grad_up_weight: float32 [768, 3072], P('wide')
- grad_up_bias: float32 [3072], P('wide')
- grad_down_weight: float32 [3072, 768], P('wide')
- grad_down_bias: float32 [768], P('wide')
- grad_mlp_scale: float32 [768], P('wide')
The draws below stay inside these ranges and needn't reach their ends.
Inputs may be any that keep to these rules, and one draw needn't show every extreme that they name: `crop_lengths`: columns 0 and 1 lie in 160 to 261, columns 2 to 9 in 24 to 54.
All inputs are finite; a program needn't handle non-finite values.
Results may differ from the reference program's by a relative error of at most 0.017.
Values may be sent and summed in bfloat16 or wider, within the bound.
A program may use at most 128 MiB of HBM per device.

```python
import jax
import jax.numpy as jnp
from jax import lax

D = 768
FF = 3072
HEADS = 12
HEAD_DIM = 64
GSLOT = 288
LSLOT = 56
GLEN = 261
LLEN = 54
GMIN = 160
LMIN = 24
GROUP_IMG = 2
IMG_ROWS = 1024
STREAM = 2048
CROP_GROUPS = 2
BLK = 256
IMAGES = 16
TOKENS = 16384
N_NARROW = 4
N_WIDE = 8


def draw_crop_lengths(key, part):
    first_key, second_key = jax.random.split(jax.random.fold_in(key, 17))
    global_lengths = jax.random.randint(first_key, (IMAGES, 2), GMIN, GLEN + 1)
    local_lengths = jax.random.randint(second_key, (IMAGES, 8), LMIN, LLEN + 1)
    lengths = jnp.concatenate([global_lengths, local_lengths], axis=1)
    lengths = lengths.at[0, 0].set(GLEN).at[0, 1].set(GMIN).at[0, 2].set(LLEN).at[0, 9].set(LMIN)
    return lengths.astype(jnp.int32)


def steps_of(stream_key, shape, shards, least, high):
    loudness, own = 1.0, jax.random.fold_in(stream_key, 6)
    for position, shards_of in shards:
        steps = jnp.exp(jax.random.uniform(jax.random.fold_in(own, position), (shards_of,), jnp.float32, least / len(shards), high / len(shards)))
        loudness = loudness * jnp.repeat(steps, shape[position] // shards_of).reshape([-1 if axis == position else 1 for axis in range(len(shape))])
    return loudness


def bell_draw(key, extent, spread, limit, cuts=(), held_as=jnp.bfloat16):
    values = spread * jax.random.normal(key, extent, jnp.float32)
    if cuts:
        values = values * steps_of(key, extent, cuts, -0.22, 0.18)
    return jnp.clip(values, -limit, limit).astype(held_as)


def setup_inputs(seed: int = 0) -> dict:
    splits = jax.random.split(jax.random.key(seed), 18)
    tokens = bell_draw(splits[0], (TOKENS, D), 1.0, 6.0, ((0, 32),))
    attn_gain = jnp.clip(1.0 + 0.1 * jax.random.normal(splits[1], (D,), jnp.float32), 0.5, 1.5).astype(jnp.bfloat16)
    attn_shift = bell_draw(splits[2], (D,), 0.3, 2.0)
    in_weight = bell_draw(splits[3], (D, 3 * D), D ** -0.5, 0.21875)
    query_value_bias = bell_draw(splits[4], (2, D), 0.5, 3.0)
    proj_weight = bell_draw(splits[5], (D, D), (max(D // 64, 4)) ** -0.5, 1.75)
    proj_bias = bell_draw(splits[6], (D,), 0.3, 2.0)
    attn_scale = jnp.clip(1.0 + 0.1 * jax.random.normal(splits[7], (D,), jnp.float32), 0.5, 1.5).astype(jnp.bfloat16)
    mlp_gain = jnp.clip(1.0 + 0.1 * jax.random.normal(splits[8], (D,), jnp.float32), 0.5, 1.5).astype(jnp.bfloat16)
    mlp_shift = bell_draw(splits[9], (D,), 0.3, 2.0)
    up_weight = bell_draw(splits[10], (D, FF), D ** -0.5, 0.21875)
    up_bias = bell_draw(splits[11], (FF,), 0.3, 2.0)
    down_weight = bell_draw(splits[12], (FF, D), FF ** -0.5, 0.109375)
    down_bias = bell_draw(splits[13], (D,), 0.3, 2.0)
    mlp_scale = jnp.clip(1.0 + 0.1 * jax.random.normal(splits[14], (D,), jnp.float32), 0.5, 1.5).astype(jnp.bfloat16)
    crop_lengths = draw_crop_lengths(jax.random.fold_in(splits[17], 71), 0)
    out_grad = bell_draw(splits[16], (TOKENS, D), 1.0, 6.0, ((0, 32),))
    return dict(tokens=tokens, attn_gain=attn_gain, attn_shift=attn_shift, in_weight=in_weight, query_value_bias=query_value_bias, proj_weight=proj_weight, proj_bias=proj_bias, attn_scale=attn_scale, mlp_gain=mlp_gain, mlp_shift=mlp_shift, up_weight=up_weight, up_bias=up_bias, down_weight=down_weight, down_bias=down_bias, mlp_scale=mlp_scale, crop_lengths=crop_lengths, out_grad=out_grad)


NORM_EPSILON = 1e-06
MASKED = -1e+30
HIGHEST = lax.Precision.HIGHEST

@jax.custom_vjp
def low(v):
    return lax.optimization_barrier(v.astype(jnp.bfloat16)).astype(jnp.float32)

@jax.custom_vjp
def low_back(v):
    return v

def low_keep(v):
    return (low(v), None)

def low_pass(kept, grad):
    return (grad,)

def back_keep(v):
    return (v, None)

def back_low(kept, grad):
    return (low(grad),)
low.defvjp(low_keep, low_pass)
low_back.defvjp(back_keep, back_low)

def layer_norm(values, gain_row, shift_row):
    row_mean = lax.optimization_barrier(jnp.mean(values, axis=-1, keepdims=True))
    centered = values - row_mean
    variance = lax.optimization_barrier(jnp.mean(centered * centered, axis=-1, keepdims=True))
    return centered * lax.rsqrt(variance + NORM_EPSILON) * gain_row + shift_row

def gelu_exact(values):
    return 0.5 * values * (1.0 + jax.scipy.special.erf(values * 0.7071067811865476))

def key_masks(lengths):
    positions = jnp.arange(GSLOT, dtype=jnp.int32)
    global_valid = positions[None, None, :] < lengths[:, :2, None]
    global_valid = global_valid.reshape(GROUP_IMG * 2, 1, 1, GSLOT)
    row_ids = jnp.arange(8 * LSLOT, dtype=jnp.int32)
    crop_ids = row_ids // LSLOT
    offsets = row_ids % LSLOT
    local_lengths = jnp.repeat(lengths[:, 2:], LSLOT, axis=1)
    same_crop = crop_ids[:, None] == crop_ids[None, :]
    local_valid = same_crop[None] & (offsets[None, None, :] < local_lengths[:, None, :])
    return (global_valid, local_valid[:, None])

def split_crops(values):
    global_part = values[:, :2 * GSLOT].reshape(GROUP_IMG * 2, GSLOT, values.shape[2], values.shape[3])
    return (global_part, values[:, 2 * GSLOT:])

def join_crops(global_part, local_part):
    widened = global_part.reshape(GROUP_IMG, 2 * GSLOT, local_part.shape[2], local_part.shape[3])
    return jnp.concatenate([widened, local_part], axis=1)

def attend_tile(queries, key_rows, values, key_mask, score_scale):
    logits = low_back(jnp.einsum('bqhk,bshk->bhqs', queries, key_rows, precision=HIGHEST) * score_scale)
    logits = jnp.where(key_mask, logits, MASKED)
    row_max = lax.optimization_barrier(jnp.max(logits, axis=-1, keepdims=True))
    exponent = jnp.exp(logits - row_max)
    weights = low(exponent / lax.optimization_barrier(jnp.sum(exponent, axis=-1, keepdims=True)))
    return jnp.einsum('bhqs,bshk->bqhk', weights, values, precision=HIGHEST)

def group_layer(rows, params, lengths):
    attn_gain, attn_shift, in_weight, qv_bias, proj_weight, proj_bias, attn_scale, mlp_gain, mlp_shift, up_weight, up_bias, down_weight, down_bias, mlp_scale = params
    score_scale = HEAD_DIM ** (-0.5)
    normed = low(layer_norm(rows, attn_gain, attn_shift))
    full_bias = jnp.concatenate([qv_bias[0], jnp.zeros((D,), jnp.float32), qv_bias[1]])
    projected = low_back(low(jnp.dot(normed, in_weight, precision=HIGHEST) + full_bias))
    projected = projected.reshape(GROUP_IMG, IMG_ROWS, 3, HEADS, HEAD_DIM)
    masks = key_masks(lengths)
    members = [split_crops(projected[:, :, which]) for which in range(3)]
    tiles = [attend_tile(members[0][which], members[1][which], members[2][which], masks[which], score_scale) for which in range(2)]
    attended = join_crops(tiles[0], tiles[1]).reshape(STREAM, D)
    attended = low_back(low(attended))
    branch = low_back(jnp.dot(attended, proj_weight, precision=HIGHEST) + proj_bias)
    middle = rows + attn_scale * branch
    second = low(layer_norm(middle, mlp_gain, mlp_shift))
    hidden = low_back(jnp.dot(second, up_weight, precision=HIGHEST) + up_bias)
    activated = low(gelu_exact(hidden))
    outcome = low_back(jnp.dot(activated, down_weight, precision=HIGHEST) + down_bias)
    return middle + mlp_scale * outcome

def reference(tokens, attn_gain, attn_shift, in_weight, query_value_bias, proj_weight, proj_bias, attn_scale, mlp_gain, mlp_shift, up_weight, up_bias, down_weight, down_bias, mlp_scale, crop_lengths, out_grad):
    params = tuple((weight.astype(jnp.float32) for weight in (attn_gain, attn_shift, in_weight, query_value_bias, proj_weight, proj_bias, attn_scale, mlp_gain, mlp_shift, up_weight, up_bias, down_weight, down_bias, mlp_scale)))

    def to_groups(array):
        shaped = array.astype(jnp.float32).reshape(N_NARROW, N_WIDE, CROP_GROUPS, BLK, D)
        return shaped.transpose(0, 2, 1, 3, 4).reshape(N_NARROW * CROP_GROUPS, STREAM, D)

    def from_groups(array):
        shaped = array.reshape(N_NARROW, CROP_GROUPS, N_WIDE, BLK, D)
        return shaped.transpose(0, 2, 1, 3, 4).reshape(TOKENS, D)
    lengths = crop_lengths.reshape(N_NARROW * CROP_GROUPS, GROUP_IMG, 10)

    def advance(sums, entry):
        rows, cotangent, group_lengths = entry
        result, pullback = jax.vjp(lambda row_values, weights: group_layer(row_values, weights, group_lengths), rows, params)
        row_grads, weight_grads = pullback(cotangent)
        new_sums = tuple((left + right for left, right in zip(sums, weight_grads)))
        return (new_sums, (result.astype(jnp.bfloat16), row_grads.astype(jnp.bfloat16)))
    start_sums = tuple((jnp.zeros_like(weight) for weight in params))
    sums, (results, row_grads) = lax.scan(advance, start_sums, (to_groups(tokens), to_groups(out_grad), lengths))
    return (from_groups(results), from_groups(row_grads), sums[0], sums[1], sums[2], sums[3], sums[4], sums[5], sums[6], sums[7], sums[8], sums[9], sums[10], sums[11], sums[12], sums[13])
```

```python
import jax
import jax.numpy as jnp
from jax import lax
from jax.experimental import pallas as pl
from jax.experimental.pallas import tpu as pltpu
from jax.sharding import PartitionSpec as P

D = 768
HEAD_DIM = 64
HEAD_GROUPS = 4
GSLOT = 288
LSLOT = 56
GROUP_IMG = 2
IMG_ROWS = 1024
STREAM = 2048
TOK_DEV = 512


NORM_EPSILON = 1e-06
MASKED = -1e30


def layer_norm(values, gain_row, shift_row):
    row_mean = jnp.mean(values, axis=-1, keepdims=True)
    centered = values - row_mean
    variance = jnp.mean(centered * centered, axis=-1, keepdims=True)
    return centered * lax.rsqrt(variance + NORM_EPSILON) * gain_row + shift_row


def gelu_exact(values):
    return 0.5 * values * (1.0 + jax.scipy.special.erf(values * 0.7071067811865476))


def key_masks(lengths):
    positions = jnp.arange(GSLOT, dtype=jnp.int32)
    global_valid = positions[None, None, :] < lengths[:, :2, None]
    global_valid = global_valid.reshape(GROUP_IMG * 2, 1, 1, GSLOT)
    row_ids = jnp.arange(8 * LSLOT, dtype=jnp.int32)
    crop_ids = row_ids // LSLOT
    offsets = row_ids % LSLOT
    local_lengths = jnp.repeat(lengths[:, 2:], LSLOT, axis=1)
    same_crop = crop_ids[:, None] == crop_ids[None, :]
    local_valid = same_crop[None] & (offsets[None, None, :] < local_lengths[:, None, :])
    return (global_valid, local_valid[:, None])


def split_crops(values):
    global_part = values[:, : 2 * GSLOT].reshape(
        GROUP_IMG * 2, GSLOT, values.shape[2], values.shape[3]
    )
    return (global_part, values[:, 2 * GSLOT :])


def join_crops(global_part, local_part):
    widened = global_part.reshape(GROUP_IMG, 2 * GSLOT, local_part.shape[2], local_part.shape[3])
    return jnp.concatenate([widened, local_part], axis=1)


def unpack_heads(packed):
    per_group = packed.shape[2] // HEAD_DIM
    return [packed[which].reshape(GROUP_IMG, IMG_ROWS, per_group, HEAD_DIM) for which in range(3)]


def tile_logits(queries, key_rows, key_mask, score_scale):
    raw = (
        jnp.einsum("bqhk,bshk->bhqs", queries, key_rows, preferred_element_type=jnp.float32)
        * score_scale
    )
    return jnp.where(key_mask, raw, MASKED)


def forward_tile(queries, key_rows, values, key_mask, score_scale):
    logits = tile_logits(queries, key_rows, key_mask, score_scale)
    row_max = jnp.max(logits, axis=-1, keepdims=True)
    exponent = jnp.exp(logits - row_max)
    row_total = jnp.sum(exponent, axis=-1, keepdims=True)
    weights = (exponent / row_total).astype(jnp.bfloat16)
    result = jnp.einsum("bhqs,bshk->bqhk", weights, values, preferred_element_type=jnp.float32)
    return (result.astype(jnp.bfloat16), row_max + jnp.log(row_total))


def backward_tile(queries, key_rows, values, grad_out, key_mask, logsum, score_scale):
    logits = tile_logits(queries, key_rows, key_mask, score_scale)
    probabilities = jnp.exp(logits - logsum)
    grad_probs = jnp.einsum("bqhk,bshk->bhqs", grad_out, values, preferred_element_type=jnp.float32)
    inner = jnp.sum(probabilities * grad_probs, axis=-1, keepdims=True)
    grad_logits = (probabilities * (grad_probs - inner)).astype(jnp.bfloat16)
    grad_queries = (
        jnp.einsum("bhqs,bshk->bqhk", grad_logits, key_rows, preferred_element_type=jnp.float32)
        * score_scale
    )
    grad_keys = (
        jnp.einsum("bhqs,bqhk->bshk", grad_logits, queries, preferred_element_type=jnp.float32)
        * score_scale
    )
    grad_values = jnp.einsum(
        "bhqs,bqhk->bshk",
        probabilities.astype(jnp.bfloat16),
        grad_out,
        preferred_element_type=jnp.float32,
    )
    return (
        grad_queries.astype(jnp.bfloat16),
        grad_keys.astype(jnp.bfloat16),
        grad_values.astype(jnp.bfloat16),
    )


def attention_forward(packed, masks, score_scale):
    members = [split_crops(member) for member in unpack_heads(packed)]
    results = []
    logsums = []
    for which in range(2):
        result, logsum = forward_tile(
            members[0][which], members[1][which], members[2][which], masks[which], score_scale
        )
        results.append(result)
        logsums.append(logsum)
    return (join_crops(results[0], results[1]).reshape(STREAM, packed.shape[2]), logsums)


def attention_backward(packed, grad_attended, logsums, masks, score_scale):
    members = [split_crops(member) for member in unpack_heads(packed)]
    grad_parts = split_crops(grad_attended.reshape(GROUP_IMG, IMG_ROWS, -1, HEAD_DIM))
    tile_grads = [
        backward_tile(
            members[0][which],
            members[1][which],
            members[2][which],
            grad_parts[which],
            masks[which],
            logsums[which],
            score_scale,
        )
        for which in range(2)
    ]
    joined = [
        join_crops(tile_grads[0][member], tile_grads[1][member]).reshape(STREAM, packed.shape[2])
        for member in range(3)
    ]
    return jnp.stack(joined)


def on_device(
    tokens,
    attn_gain,
    attn_shift,
    in_weight,
    query_value_bias,
    proj_weight,
    proj_bias,
    attn_scale,
    mlp_gain,
    mlp_shift,
    up_weight,
    up_bias,
    down_weight,
    down_bias,
    mlp_scale,
    crop_lengths,
    out_grad,
):
    wide_size = lax.axis_size("wide")
    crop_groups = wide_size // HEAD_GROUPS
    block_rows = TOK_DEV // crop_groups
    head_width = D // HEAD_GROUPS
    score_scale = HEAD_DIM ** (-0.5)
    own_group = lax.axis_index("wide") // HEAD_GROUPS
    own_lengths = lax.dynamic_slice_in_dim(crop_lengths, own_group * GROUP_IMG, GROUP_IMG, 0)
    masks = key_masks(own_lengths)
    inputs = tokens.astype(jnp.float32)
    first_gain = attn_gain.astype(jnp.float32)
    first_shift = attn_shift.astype(jnp.float32)
    normed, first_back = jax.vjp(layer_norm, inputs, first_gain, first_shift)
    normed_low = normed.astype(jnp.bfloat16)
    normed_blocks = normed_low.reshape(crop_groups, block_rows, D)
    weight_in = in_weight.reshape(D, 3, HEAD_GROUPS, head_width)
    qv_rows = query_value_bias.astype(jnp.float32)
    full_bias = jnp.stack([qv_rows[0], jnp.zeros_like(qv_rows[0]), qv_rows[1]]).reshape(
        3, 1, HEAD_GROUPS, 1, head_width
    )
    projected = (
        jnp.einsum("gbd,dchk->cghbk", normed_blocks, weight_in, preferred_element_type=jnp.float32)
        + full_bias
    )
    send_heads = projected.astype(jnp.bfloat16).reshape(3, wide_size, block_rows, head_width)
    arrived = lax.all_to_all(send_heads, "wide", split_axis=1, concat_axis=1, tiled=True)
    packed = arrived.reshape(3, STREAM, head_width)
    attended, logsums = attention_forward(packed, masks, score_scale)
    returned = lax.all_to_all(
        attended.reshape(wide_size, block_rows, head_width),
        "wide",
        split_axis=0,
        concat_axis=0,
        tiled=True,
    )
    mixed_rows = returned.reshape(crop_groups, HEAD_GROUPS, block_rows, head_width)
    weight_proj = proj_weight.reshape(HEAD_GROUPS, head_width, D)
    branch = jnp.einsum(
        "ghbk,hkd->gbd", mixed_rows, weight_proj, preferred_element_type=jnp.float32
    )
    branch = branch.reshape(TOK_DEV, D) + proj_bias.astype(jnp.float32)
    first_scale = attn_scale.astype(jnp.float32)
    middle = inputs + first_scale * branch
    second, second_back = jax.vjp(
        layer_norm, middle, mlp_gain.astype(jnp.float32), mlp_shift.astype(jnp.float32)
    )
    second_low = second.astype(jnp.bfloat16)
    hidden = jnp.dot(second_low, up_weight, preferred_element_type=jnp.float32) + up_bias.astype(
        jnp.float32
    )
    activated, gelu_back = jax.vjp(gelu_exact, hidden)
    activated_low = activated.astype(jnp.bfloat16)
    outcome = jnp.dot(
        activated_low, down_weight, preferred_element_type=jnp.float32
    ) + down_bias.astype(jnp.float32)
    second_scale = mlp_scale.astype(jnp.float32)
    output = (middle + second_scale * outcome).astype(jnp.bfloat16)
    cotangent = out_grad.astype(jnp.float32)
    grad_mlp_scale = jnp.sum(cotangent * outcome, axis=0)
    grad_outcome = (cotangent * second_scale).astype(jnp.bfloat16)
    grad_down_weight = jnp.einsum(
        "tf,td->fd", activated_low, grad_outcome, preferred_element_type=jnp.float32
    )
    grad_down_bias = jnp.sum(grad_outcome.astype(jnp.float32), axis=0)
    grad_activated = jnp.einsum(
        "td,fd->tf", grad_outcome, down_weight, preferred_element_type=jnp.float32
    )
    grad_hidden = gelu_back(grad_activated)[0].astype(jnp.bfloat16)
    grad_up_weight = jnp.einsum(
        "td,tf->df", second_low, grad_hidden, preferred_element_type=jnp.float32
    )
    grad_up_bias = jnp.sum(grad_hidden.astype(jnp.float32), axis=0)
    grad_second = jnp.einsum(
        "tf,df->td", grad_hidden, up_weight, preferred_element_type=jnp.float32
    )
    grad_middle, grad_mlp_gain, grad_mlp_shift = second_back(grad_second)
    grad_middle = grad_middle + cotangent
    grad_attn_scale = jnp.sum(grad_middle * branch, axis=0)
    grad_branch = (grad_middle * first_scale).astype(jnp.bfloat16)
    branch_blocks = grad_branch.reshape(crop_groups, block_rows, D)
    grad_proj_weight = jnp.einsum(
        "ghbk,gbd->hkd", mixed_rows, branch_blocks, preferred_element_type=jnp.float32
    ).reshape(D, D)
    grad_proj_bias = jnp.sum(grad_branch.astype(jnp.float32), axis=0)
    grad_mixed = jnp.einsum(
        "gbd,hkd->ghbk", branch_blocks, weight_proj, preferred_element_type=jnp.float32
    )
    grad_mixed = grad_mixed.astype(jnp.bfloat16).reshape(wide_size, block_rows, head_width)
    again, grad_arrived = (
        lax.all_to_all(send_heads, "wide", split_axis=1, concat_axis=1, tiled=True),
        lax.all_to_all(grad_mixed[None], "wide", split_axis=1, concat_axis=1, tiled=True),
    )
    packed_back = again.reshape(3, STREAM, head_width)
    grad_attended = grad_arrived.reshape(STREAM, head_width)
    grad_packed = attention_backward(packed_back, grad_attended, logsums, masks, score_scale)
    grad_sent = lax.all_to_all(
        grad_packed.reshape(3, wide_size, block_rows, head_width),
        "wide",
        split_axis=1,
        concat_axis=1,
        tiled=True,
    )
    grad_heads = grad_sent.reshape(3, crop_groups, HEAD_GROUPS, block_rows, head_width)
    grad_in_weight = jnp.einsum(
        "gbd,cghbk->dchk", normed_blocks, grad_heads, preferred_element_type=jnp.float32
    ).reshape(D, 3 * D)
    bias_sums = jnp.sum(grad_heads.astype(jnp.float32), axis=(1, 3)).reshape(3, D)
    grad_query_value_bias = jnp.stack([bias_sums[0], bias_sums[2]])
    grad_normed = jnp.einsum(
        "cghbk,dchk->gbd", grad_heads, weight_in, preferred_element_type=jnp.float32
    ).reshape(TOK_DEV, D)
    grad_inputs, grad_attn_gain, grad_attn_shift = first_back(grad_normed)
    input_grad = (grad_inputs + grad_middle).astype(jnp.bfloat16)
    shares = (
        lax.psum_scatter(
            grad_attn_gain.astype(jnp.bfloat16), "wide", scatter_dimension=0, tiled=True
        ).astype(jnp.float32),
        lax.psum_scatter(
            grad_attn_shift.astype(jnp.bfloat16), "wide", scatter_dimension=0, tiled=True
        ).astype(jnp.float32),
        lax.psum_scatter(
            grad_in_weight.astype(jnp.bfloat16), "wide", scatter_dimension=0, tiled=True
        ).astype(jnp.float32),
        lax.psum_scatter(
            grad_query_value_bias.astype(jnp.bfloat16), "wide", scatter_dimension=1, tiled=True
        ).astype(jnp.float32),
        lax.psum_scatter(
            grad_proj_weight.astype(jnp.bfloat16), "wide", scatter_dimension=0, tiled=True
        ).astype(jnp.float32),
        lax.psum_scatter(
            grad_proj_bias.astype(jnp.bfloat16), "wide", scatter_dimension=0, tiled=True
        ).astype(jnp.float32),
        lax.psum_scatter(
            grad_attn_scale.astype(jnp.bfloat16), "wide", scatter_dimension=0, tiled=True
        ).astype(jnp.float32),
        lax.psum_scatter(
            grad_mlp_gain.astype(jnp.bfloat16), "wide", scatter_dimension=0, tiled=True
        ).astype(jnp.float32),
        lax.psum_scatter(
            grad_mlp_shift.astype(jnp.bfloat16), "wide", scatter_dimension=0, tiled=True
        ).astype(jnp.float32),
        lax.psum_scatter(
            grad_up_weight.astype(jnp.bfloat16), "wide", scatter_dimension=0, tiled=True
        ).astype(jnp.float32),
        lax.psum_scatter(
            grad_up_bias.astype(jnp.bfloat16), "wide", scatter_dimension=0, tiled=True
        ).astype(jnp.float32),
        lax.psum_scatter(
            grad_down_weight.astype(jnp.bfloat16), "wide", scatter_dimension=0, tiled=True
        ).astype(jnp.float32),
        lax.psum_scatter(
            grad_down_bias.astype(jnp.bfloat16), "wide", scatter_dimension=0, tiled=True
        ).astype(jnp.float32),
        lax.psum_scatter(
            grad_mlp_scale.astype(jnp.bfloat16), "wide", scatter_dimension=0, tiled=True
        ).astype(jnp.float32),
    )
    results = (
        lax.psum(shares[0].astype(jnp.bfloat16), "narrow").astype(jnp.float32),
        lax.psum(shares[1].astype(jnp.bfloat16), "narrow").astype(jnp.float32),
        lax.psum(shares[2].astype(jnp.bfloat16), "narrow").astype(jnp.float32),
        lax.psum(shares[3].astype(jnp.bfloat16), "narrow").astype(jnp.float32),
        lax.psum(shares[4].astype(jnp.bfloat16), "narrow").astype(jnp.float32),
        lax.psum(shares[5].astype(jnp.bfloat16), "narrow").astype(jnp.float32),
        lax.psum(shares[6].astype(jnp.bfloat16), "narrow").astype(jnp.float32),
        lax.psum(shares[7].astype(jnp.bfloat16), "narrow").astype(jnp.float32),
        lax.psum(shares[8].astype(jnp.bfloat16), "narrow").astype(jnp.float32),
        lax.psum(shares[9].astype(jnp.bfloat16), "narrow").astype(jnp.float32),
        lax.psum(shares[10].astype(jnp.bfloat16), "narrow").astype(jnp.float32),
        lax.psum(shares[11].astype(jnp.bfloat16), "narrow").astype(jnp.float32),
        lax.psum(shares[12].astype(jnp.bfloat16), "narrow").astype(jnp.float32),
        lax.psum(shares[13].astype(jnp.bfloat16), "narrow").astype(jnp.float32),
    )
    return (
        output,
        input_grad,
        results[0],
        results[1],
        results[2],
        results[3],
        results[4],
        results[5],
        results[6],
        results[7],
        results[8],
        results[9],
        results[10],
        results[11],
        results[12],
        results[13],
    )


MESH = pl.DeviceIdType.MESH
UNITS = 18
PAIRS = 9
ROWS = 576
F32 = jnp.float32
BF16 = jnp.bfloat16


def wgrad_kernel(
    g_ref, dm_ref, h2_ref, du_ref, o_ref, da_ref, h1_ref, dqkv_ref, vec_ref,
    win_ref, wproj_ref, wup_ref, wdown_ref, vout_ref,
    gbuf, r0, r1, r2, r3, r4, fin, gt, h2t, ot, h1t, vbuf, vrecv,
    ssem, rsem, vssem, vrsem,
):
    n = lax.axis_index("narrow")
    w = lax.axis_index("wide")
    c = n % 2
    y = n // 2
    x = w % 2
    z1 = (w // 2) % 2
    z2 = w // 4
    partner = {
        "core": (n + 1 - 2 * c, w),
        "y": (n + 2 - 4 * y, w),
        "x": (n, w + 1 - 2 * x),
        "z1": (n, w + 2 - 4 * z1),
        "z2": (n, w + 4 - 8 * z2),
    }
    barrier = pltpu.get_barrier_semaphore()
    for target in partner.values():
        pl.semaphore_signal(barrier, inc=1, device_id=target, device_id_type=MESH)
    pl.semaphore_wait(barrier, 5)

    def copy(src, dst, unit, stage, axis):
        return pltpu.make_async_remote_copy(
            src_ref=src, dst_ref=dst, send_sem=ssem.at[unit, stage], recv_sem=rsem.at[unit, stage],
            device_id=partner[axis], device_id_type=MESH,
        )

    def even(u, k):
        if k == 0:
            return copy(gbuf.at[u, 1 - c], r0.at[u], u, 0, "core")
        if k == 1:
            return copy(gbuf.at[u, c, :, 1 - x], r1.at[u], u, 1, "x")
        if k == 2:
            return copy(gbuf.at[u, c, :, x, 1 - z1], r2.at[u], u, 2, "z1")
        if k == 3:
            return copy(gbuf.at[u, c, :, x, z1, 1 - z2], r3.at[u], u, 3, "z2")
        if k == 4:
            return copy(gbuf.at[u, c, :, x, z1, z2], r4.at[u], u, 4, "y")
        return copy(fin.at[u, c], fin.at[u, c], u, 5, "core")

    def odd(u, k):
        if k == 0:
            return copy(gbuf.at[u, 1 - c], r0.at[u], u, 0, "core")
        if k == 1:
            return copy(gbuf.at[u, c, 1 - y], r1.at[u], u, 1, "y")
        if k == 2:
            return copy(gbuf.at[u, c, y, 1 - x], r2.at[u], u, 2, "x")
        if k == 3:
            return copy(gbuf.at[u, c, y, x, 1 - z1], r3.at[u], u, 3, "z1")
        if k == 4:
            return copy(gbuf.at[u, c, y, x, z1, 1 - z2], r4.at[u, 0], u, 4, "z2")
        if k == 5:
            return copy(fin.at[u, c, y], fin.at[u, c, y], u, 5, "y")
        return copy(fin.at[u, c], fin.at[u, c], u, 6, "core")

    def add(dst, src):
        dst[...] = (dst[...].astype(F32) + src[...].astype(F32)).astype(BF16)

    def even_land(u, k):
        if k == 0:
            for yy in range(2):
                for xx in range(2):
                    add(gbuf.at[u, c, yy, xx], r0.at[u, yy, xx])
        elif k == 1:
            for yy in range(2):
                add(gbuf.at[u, c, yy, x], r1.at[u, yy])
        elif k == 2:
            add(gbuf.at[u, c, :, x, z1], r2.at[u])
        elif k == 3:
            add(gbuf.at[u, c, :, x, z1, z2], r3.at[u])
        elif k == 4:
            total = gbuf[u, c, :, x, z1, z2].astype(F32) + r4[u].astype(F32)
            fin[u, c] = total.astype(BF16)

    def odd_land(u, k):
        if k == 0:
            for yy in range(2):
                for xx in range(2):
                    add(gbuf.at[u, c, yy, xx], r0.at[u, yy, xx])
        elif k == 1:
            for xx in range(2):
                add(gbuf.at[u, c, y, xx], r1.at[u, xx])
        elif k == 2:
            add(gbuf.at[u, c, y, x], r2.at[u])
        elif k == 3:
            add(gbuf.at[u, c, y, x, z1], r3.at[u])
        elif k == 4:
            total = gbuf[u, c, y, x, z1, z2].astype(F32) + r4[u, 0].astype(F32)
            fin[u, c, y] = total.astype(BF16)

    def write_out(u):
        @pl.when(u < 6)
        def _():
            for sub in range(4):
                block = fin[u, sub // 2, sub % 2].astype(F32)
                for t in range(6):
                    wdown_ref[pl.ds(pl.multiple_of(64 * u + 16 * sub, 16), 16), 128 * t : 128 * (t + 1)] = block[
                        16 * t : 16 * (t + 1)
                    ]

        @pl.when(jnp.logical_and(u >= 6, u < 12))
        def _():
            for sub in range(4):
                start = pl.multiple_of((u - 6) * 512 + 128 * sub, 128)
                wup_ref[:, pl.ds(start, 128)] = fin[u, sub // 2, sub % 2].astype(F32)

        @pl.when(u >= 12)
        def _():
            for half in range(2):
                tile = (u - 12) * 2 + half

                @pl.when(tile < 9)
                def _():
                    for yy in range(2):
                        start = pl.multiple_of(tile * 256 + 128 * yy, 128)
                        win_ref[:, pl.ds(start, 128)] = fin[u, half, yy].astype(F32)

                @pl.when(tile >= 9)
                def _():
                    for yy in range(2):
                        start = pl.multiple_of((tile - 9) * 256 + 128 * yy, 128)
                        wproj_ref[:, pl.ds(start, 128)] = fin[u, half, yy].astype(F32)

    def place(u, half, result):
        for s in range(8):
            for yy in range(2):
                gbuf[u, half, yy, s % 2, (s // 2) % 2, s // 4] = result[
                    96 * s : 96 * (s + 1), 128 * yy : 128 * (yy + 1)
                ].astype(BF16)

    def produce(u):
        @pl.when(u < 6)
        def _():
            lhs = gt[u]
            for nt in range(3):
                result = jnp.dot(lhs, dm_ref[:, 256 * nt : 256 * (nt + 1)], preferred_element_type=F32)
                for s in range(8):
                    for sub in range(4):
                        rows = result[64 * s + 16 * sub : 64 * s + 16 * (sub + 1)].astype(BF16)
                        for tt in range(2):
                            t = 2 * nt + tt
                            gbuf[u, sub // 2, sub % 2, s % 2, (s // 2) % 2, s // 4, 16 * t : 16 * (t + 1)] = rows[
                                :, 128 * tt : 128 * (tt + 1)
                            ]

        @pl.when(jnp.logical_and(u >= 6, u < 12))
        def _():
            for half in range(2):
                start = pl.multiple_of((u - 6) * 512 + 256 * half, 256)
                place(u, half, jnp.dot(h2t[...], du_ref[:, pl.ds(start, 256)], preferred_element_type=F32))

        @pl.when(u >= 12)
        def _():
            for half in range(2):
                tile = (u - 12) * 2 + half

                @pl.when(tile < 9)
                def _():
                    start = pl.multiple_of(tile * 256, 256)
                    place(u, half, jnp.dot(h1t[...], dqkv_ref[:, pl.ds(start, 256)], preferred_element_type=F32))

                @pl.when(tile >= 9)
                def _():
                    start = pl.multiple_of((tile - 9) * 256, 256)
                    place(u, half, jnp.dot(ot[...], da_ref[:, pl.ds(start, 256)], preferred_element_type=F32))

    vaxes = ("core", "x", "y", "z1", "z2")

    def vcopy(k):
        return pltpu.make_async_remote_copy(
            src_ref=vbuf.at[k], dst_ref=vrecv.at[k], send_sem=vssem.at[k], recv_sem=vrsem.at[k],
            device_id=partner[vaxes[k]], device_id_type=MESH,
        )

    vbuf[0] = vec_ref[...]
    vcopy(0).start()

    for s in range(8):
        for j in range(6):
            lo = 384 * s + 64 * j
            if j % 2 == 0:
                both = g_ref[:, lo : lo + 128].T
                gt[j, 64 * s : 64 * (s + 1)] = both[:64]
                gt[j + 1, 64 * s : 64 * (s + 1)] = both[64:]
    for src, dst in ((h2_ref, h2t), (h1_ref, h1t), (o_ref, ot)):
        for s in range(6):
            dst[128 * s : 128 * (s + 1)] = src[:, 128 * s : 128 * (s + 1)].T

    def step(t, _):
        @pl.when(t < PAIRS)
        def _():
            for b in range(2):
                u = 2 * t + b
                produce(u)
                even(u, 0).start()

        for k in range(7):
            p = t - 1 - k

            @pl.when(jnp.logical_and(p >= 0, p < PAIRS))
            def _(k=k, p=p):
                u = 2 * p
                if k < 6:
                    even(u, k).wait()
                    even_land(u, k)
                    if k < 5:
                        even(u, k + 1).start()
                    else:
                        write_out(u)
                odd(u + 1, k).wait()
                odd_land(u + 1, k)
                if k < 6:
                    odd(u + 1, k + 1).start()
                else:
                    write_out(u + 1)

        for k in range(5):

            @pl.when(t == k)
            def _(k=k):
                vcopy(k).wait()
                vbuf[k + 1] = vbuf[k] + vrecv[k]
                if k < 4:
                    vcopy(k + 1).start()

        return 0

    lax.fori_loop(0, PAIRS + 7, step, 0)
    vout_ref[...] = vbuf[5, w]


def wgrads(g, dm, h2, du, o, da, h1, dqkv, vec):
    vm = pl.BlockSpec(memory_space=pltpu.VMEM)
    return pl.pallas_call(
        wgrad_kernel,
        out_shape=(
            jax.ShapeDtypeStruct((96, 2304), F32),
            jax.ShapeDtypeStruct((96, 768), F32),
            jax.ShapeDtypeStruct((96, 3072), F32),
            jax.ShapeDtypeStruct((384, 768), F32),
            jax.ShapeDtypeStruct((16, 128), F32),
        ),
        in_specs=[vm] * 9,
        out_specs=(vm,) * 5,
        scratch_shapes=[
            pltpu.VMEM((UNITS, 2, 2, 2, 2, 2, 96, 128), BF16),
            pltpu.VMEM((UNITS, 2, 2, 2, 2, 96, 128), BF16),
            pltpu.VMEM((UNITS, 2, 2, 2, 96, 128), BF16),
            pltpu.VMEM((UNITS, 2, 2, 96, 128), BF16),
            pltpu.VMEM((UNITS, 2, 96, 128), BF16),
            pltpu.VMEM((UNITS, 2, 96, 128), BF16),
            pltpu.VMEM((UNITS, 2, 2, 96, 128), BF16),
            pltpu.VMEM((6, 512, ROWS), BF16),
            pltpu.VMEM((768, ROWS), BF16),
            pltpu.VMEM((768, ROWS), BF16),
            pltpu.VMEM((768, ROWS), BF16),
            pltpu.VMEM((6, 8, 16, 128), F32),
            pltpu.VMEM((5, 8, 16, 128), F32),
            pltpu.SemaphoreType.DMA((UNITS, 7)),
            pltpu.SemaphoreType.DMA((UNITS, 7)),
            pltpu.SemaphoreType.DMA((5,)),
            pltpu.SemaphoreType.DMA((5,)),
        ],
        compiler_params=pltpu.CompilerParams(collective_id=0, has_side_effects=True, vmem_limit_bytes=63 << 20),
        name="wgrads",
    )(g, dm, h2, du, o, da, h1, dqkv, vec)


SLOT = 288


def half_masks(block):
    lanes = lax.broadcasted_iota(jnp.int32, block.shape, 1)
    zero = jnp.zeros_like(block)
    return [jnp.where((lanes < 64) == (h == 0), block, zero) for h in range(2)]


def dot_nt(a, b):
    return lax.dot_general(a, b, (((1,), (1,)), ((), ())), preferred_element_type=F32)


def dot_nn(a, b):
    return jnp.dot(a, b, preferred_element_type=F32)


def dot_tn(a, b):
    return lax.dot_general(a, b, (((0,), (0,)), ((), ())), preferred_element_type=F32)


def attn_fwd_kernel(q_ref, k_ref, v_ref, rid_ref, kid_ref, o_ref):
    q = q_ref[...]
    keys = half_masks(k_ref[...])
    values = half_masks(v_ref[...])
    valid = rid_ref[...] == kid_ref[...]
    total = None
    for h in range(2):
        s = jnp.where(valid, dot_nt(q, keys[h]) * 0.125, MASKED)
        e = jnp.exp(s - jnp.max(s, axis=-1, keepdims=True))
        p = (e / jnp.sum(e, axis=-1, keepdims=True)).astype(BF16)
        part = dot_nn(p, values[h])
        total = part if total is None else total + part
    o_ref[...] = total.astype(BF16)


def attn_bwd_kernel(q_ref, k_ref, v_ref, do_ref, rid_ref, kid_ref, dq_ref, dk_ref, dv_ref):
    queries = half_masks(q_ref[...])
    keys = half_masks(k_ref[...])
    v = v_ref[...]
    grads = half_masks(do_ref[...])
    valid = rid_ref[...] == kid_ref[...]
    dq = dk = dv = None
    for h in range(2):
        s = jnp.where(valid, dot_nt(k_ref[...], queries[h]) * 0.125, MASKED)
        e = jnp.exp(s - jnp.max(s, axis=0, keepdims=True))
        p = e / jnp.sum(e, axis=0, keepdims=True)
        dp = dot_nt(v, grads[h])
        ds = (p * (dp - jnp.sum(p * dp, axis=0, keepdims=True))).astype(BF16)
        parts = dot_tn(ds, keys[h]), dot_nn(ds, queries[h]), dot_nn(p.astype(BF16), grads[h])
        dq, dk, dv = parts if dq is None else (dq + parts[0], dk + parts[1], dv + parts[2])
    dq_ref[...] = (dq * 0.125).astype(BF16)
    dk_ref[...] = (dk * 0.125).astype(BF16)
    dv_ref[...] = dv.astype(BF16)


def attn_specs():
    def col(offset):
        return pl.BlockSpec((None, SLOT, 128), lambda i, h: (i, 0, offset + h))

    column = pl.BlockSpec((None, SLOT, 1), lambda i, h: (i, 0, 0))
    row = pl.BlockSpec((None, 1, SLOT), lambda i, h: (i, 0, 0))
    return col, column, row


def attn_fwd(qkv, rid, kid):
    col, column, row = attn_specs()
    return pl.pallas_call(
        attn_fwd_kernel,
        grid=(2, 6),
        out_shape=jax.ShapeDtypeStruct((2, SLOT, 768), BF16),
        in_specs=[col(0), col(6), col(12), column, row],
        out_specs=col(0),
        name="attn_fwd",
    )(qkv, qkv, qkv, rid[:, :, None], kid[:, None, :])


def attn_bwd(qkv, do, rid, kid):
    col, column, row = attn_specs()
    return pl.pallas_call(
        attn_bwd_kernel,
        grid=(2, 6),
        out_shape=(jax.ShapeDtypeStruct((2, SLOT, 768), BF16),) * 3,
        in_specs=[col(0), col(6), col(12), col(0), row, column],
        out_specs=(col(0),) * 3,
        name="attn_bwd",
    )(qkv, qkv, qkv, do, rid[:, None, :], kid[:, :, None])


def on_device_local(
    tokens, attn_gain, attn_shift, in_weight, query_value_bias, proj_weight, proj_bias, attn_scale,
    mlp_gain, mlp_shift, up_weight, up_bias, down_weight, down_bias, mlp_scale, crop_lengths, out_grad,
):
    wide = lax.axis_index("wide")
    quarter = wide % 4
    image = wide // 4
    shift = jnp.array([0, 32, 64, 32], jnp.int32)[quarter]
    rows = jnp.where(quarter < 2, 288, 224)
    slot = jnp.arange(SLOT, dtype=jnp.int32)
    live = (slot < rows)[None, :, None]

    def gather_crops(values):
        own = values.reshape(2, 256, D)
        halo = lax.ppermute(own[:, :64], "wide", [(i, i - 1) for i in range(8) if i % 4])
        joined = jnp.concatenate([own, halo, jnp.zeros((2, 32, D), own.dtype)], axis=1)
        moved = lax.dynamic_slice_in_dim(joined, shift, SLOT, 1)
        return jnp.where(live, moved, jnp.zeros_like(moved)).reshape(ROWS, D)

    def return_crops(values):
        shaped = jnp.concatenate([jnp.zeros((2, 64, D), BF16), values.reshape(2, SLOT, D), jnp.zeros((2, 64, D), BF16)], axis=1)
        moved = lax.dynamic_slice_in_dim(shaped, 64 - shift, 320, 1)
        halo = lax.ppermute(moved[:, 256:], "wide", [(i, i + 1) for i in range(8) if i % 4 < 3])
        head = jnp.where((jnp.arange(64) < shift)[None, :, None], halo, moved[:, :64])
        return jnp.concatenate([head, moved[:, 64:256]], axis=1).reshape(512, D)

    lengths = lax.dynamic_slice(
        crop_lengths.reshape(2, 2, 10), (0, image, 0), (2, 1, 10)
    ).reshape(2, 10)
    local = slot // LSLOT
    rid = jnp.where(quarter < 2, 0, local)
    rid = jnp.broadcast_to(rid[None], (2, SLOT))
    first_local = jnp.where(quarter == 3, 6, 2)
    local_lengths = lax.dynamic_slice(jnp.pad(lengths, ((0, 0), (0, 2))), (0, first_local), (2, 6))
    local_lengths = jnp.where(jnp.arange(6)[None] < 4, local_lengths, 0)
    local_valid = (slot % LSLOT)[None] < jnp.take_along_axis(local_lengths, jnp.broadcast_to(local[None], (2, SLOT)), 1)
    global_length = jnp.where(quarter == 0, lengths[:, 0], lengths[:, 1])
    key_valid = jnp.where(quarter < 2, slot[None] < global_length[:, None], local_valid)
    kid = jnp.where(key_valid, rid, -1)

    inputs = gather_crops(tokens).astype(F32)
    cotangent = gather_crops(out_grad).astype(F32)
    first_gain = attn_gain.astype(F32)
    normed, first_back = jax.vjp(layer_norm, inputs, first_gain, attn_shift.astype(F32))
    normed_low = normed.astype(BF16)
    qv_rows = query_value_bias.astype(F32)
    full_bias = jnp.concatenate([qv_rows[0], jnp.zeros_like(qv_rows[0]), qv_rows[1]])
    qkv = (jnp.dot(normed_low, in_weight, preferred_element_type=F32) + full_bias).astype(BF16)
    qkv = qkv.reshape(2, SLOT, 3 * D)
    mixed = attn_fwd(qkv, rid, kid).reshape(ROWS, D)
    branch = jnp.dot(mixed, proj_weight, preferred_element_type=F32) + proj_bias.astype(F32)
    first_scale = attn_scale.astype(F32)
    middle = inputs + first_scale * branch
    second, second_back = jax.vjp(layer_norm, middle, mlp_gain.astype(F32), mlp_shift.astype(F32))
    second_low = second.astype(BF16)
    hidden = jnp.dot(second_low, up_weight, preferred_element_type=F32) + up_bias.astype(F32)
    activated, gelu_back = jax.vjp(gelu_exact, hidden)
    activated_low = activated.astype(BF16)
    outcome = jnp.dot(activated_low, down_weight, preferred_element_type=F32) + down_bias.astype(F32)
    second_scale = mlp_scale.astype(F32)
    output = (middle + second_scale * outcome).astype(BF16)
    grad_mlp_scale = jnp.sum(cotangent * outcome, axis=0)
    grad_outcome = (cotangent * second_scale).astype(BF16)
    grad_down_bias = jnp.sum(grad_outcome.astype(F32), axis=0)
    grad_activated = dot_nt(grad_outcome, down_weight)
    grad_hidden = gelu_back(grad_activated)[0].astype(BF16)
    grad_up_bias = jnp.sum(grad_hidden.astype(F32), axis=0)
    grad_second = dot_nt(grad_hidden, up_weight)
    grad_middle, grad_mlp_gain, grad_mlp_shift = second_back(grad_second)
    grad_middle = grad_middle + cotangent
    grad_attn_scale = jnp.sum(grad_middle * branch, axis=0)
    grad_branch = (grad_middle * first_scale).astype(BF16)
    grad_proj_bias = jnp.sum(grad_branch.astype(F32), axis=0)
    grad_mixed = dot_nt(grad_branch, proj_weight).astype(BF16)
    grad_qkv = jnp.concatenate(attn_bwd(qkv, grad_mixed.reshape(2, SLOT, D), rid, kid), axis=2).reshape(ROWS, 3 * D)
    bias_sums = jnp.sum(grad_qkv.astype(F32), axis=0).reshape(3, D)
    grad_normed = dot_nt(grad_qkv, in_weight)
    grad_inputs, grad_attn_gain, grad_attn_shift = first_back(grad_normed)
    input_grad = (grad_inputs + grad_middle).astype(BF16)
    vectors = jnp.stack(
        [grad_attn_gain, grad_attn_shift, bias_sums[0], bias_sums[2], grad_proj_bias, grad_attn_scale,
         grad_mlp_gain, grad_mlp_shift, grad_down_bias, grad_mlp_scale], axis=0,
    ).reshape(10, 8, 96)
    vectors = jnp.concatenate([vectors, grad_up_bias.reshape(8, 4, 96).transpose(1, 0, 2)], axis=0)
    vectors = jnp.pad(vectors.transpose(1, 0, 2), ((0, 0), (0, 2), (0, 32)))
    g_in, g_proj, g_up, g_down, v = wgrads(
        activated_low, grad_outcome, second_low, grad_hidden, mixed, grad_branch, normed_low, grad_qkv, vectors
    )
    v = v[:, :96]
    return (
        return_crops(output), return_crops(input_grad),
        v[0], v[1], g_in, v[2:4], g_proj, v[4], v[5], v[6], v[7], g_up, v[10:14].reshape(384), g_down, v[8], v[9],
    )


def solution(mesh):
    local = mesh.shape["wide"] == 8 and mesh.shape["narrow"] == 4
    return jax.shard_map(
        on_device_local if local else on_device,
        mesh=mesh,
        in_specs=(
            P(("narrow", "wide"), None),
            P(),
            P(),
            P(),
            P(),
            P(),
            P(),
            P(),
            P(),
            P(),
            P(),
            P(),
            P(),
            P(),
            P(),
            P("narrow", None),
            P(("narrow", "wide"), None),
        ),
        out_specs=(
            P(("narrow", "wide"), None),
            P(("narrow", "wide"), None),
            P("wide"),
            P("wide"),
            P("wide", None),
            P(None, "wide"),
            P("wide", None),
            P("wide"),
            P("wide"),
            P("wide"),
            P("wide"),
            P("wide", None),
            P("wide"),
            P("wide", None),
            P("wide"),
            P("wide"),
        ),
        check_vma=False,
    )
```

```python
import jax
import jax.numpy as jnp
from jax import lax
from jax.experimental import pallas as pl
from jax.experimental.pallas import tpu as pltpu
from jax.sharding import PartitionSpec as P

D = 768
HEAD_DIM = 64
HEAD_GROUPS = 4
GSLOT = 288
LSLOT = 56
GROUP_IMG = 2
IMG_ROWS = 1024
STREAM = 2048
TOK_DEV = 512


NORM_EPSILON = 1e-06
MASKED = -1e30


def layer_norm(values, gain_row, shift_row):
    row_mean = jnp.mean(values, axis=-1, keepdims=True)
    centered = values - row_mean
    variance = jnp.mean(centered * centered, axis=-1, keepdims=True)
    return centered * lax.rsqrt(variance + NORM_EPSILON) * gain_row + shift_row


def gelu_exact(values):
    return 0.5 * values * (1.0 + jax.scipy.special.erf(values * 0.7071067811865476))


def key_masks(lengths):
    positions = jnp.arange(GSLOT, dtype=jnp.int32)
    global_valid = positions[None, None, :] < lengths[:, :2, None]
    global_valid = global_valid.reshape(GROUP_IMG * 2, 1, 1, GSLOT)
    row_ids = jnp.arange(8 * LSLOT, dtype=jnp.int32)
    crop_ids = row_ids // LSLOT
    offsets = row_ids % LSLOT
    local_lengths = jnp.repeat(lengths[:, 2:], LSLOT, axis=1)
    same_crop = crop_ids[:, None] == crop_ids[None, :]
    local_valid = same_crop[None] & (offsets[None, None, :] < local_lengths[:, None, :])
    return (global_valid, local_valid[:, None])


def split_crops(values):
    global_part = values[:, : 2 * GSLOT].reshape(
        GROUP_IMG * 2, GSLOT, values.shape[2], values.shape[3]
    )
    return (global_part, values[:, 2 * GSLOT :])


def join_crops(global_part, local_part):
    widened = global_part.reshape(GROUP_IMG, 2 * GSLOT, local_part.shape[2], local_part.shape[3])
    return jnp.concatenate([widened, local_part], axis=1)


def unpack_heads(packed):
    per_group = packed.shape[2] // HEAD_DIM
    return [packed[which].reshape(GROUP_IMG, IMG_ROWS, per_group, HEAD_DIM) for which in range(3)]


def tile_logits(queries, key_rows, key_mask, score_scale):
    raw = (
        jnp.einsum("bqhk,bshk->bhqs", queries, key_rows, preferred_element_type=jnp.float32)
        * score_scale
    )
    return jnp.where(key_mask, raw, MASKED)


def forward_tile(queries, key_rows, values, key_mask, score_scale):
    logits = tile_logits(queries, key_rows, key_mask, score_scale)
    row_max = jnp.max(logits, axis=-1, keepdims=True)
    exponent = jnp.exp(logits - row_max)
    row_total = jnp.sum(exponent, axis=-1, keepdims=True)
    weights = (exponent / row_total).astype(jnp.bfloat16)
    result = jnp.einsum("bhqs,bshk->bqhk", weights, values, preferred_element_type=jnp.float32)
    return (result.astype(jnp.bfloat16), row_max + jnp.log(row_total))


def backward_tile(queries, key_rows, values, grad_out, key_mask, logsum, score_scale):
    logits = tile_logits(queries, key_rows, key_mask, score_scale)
    probabilities = jnp.exp(logits - logsum)
    grad_probs = jnp.einsum("bqhk,bshk->bhqs", grad_out, values, preferred_element_type=jnp.float32)
    inner = jnp.sum(probabilities * grad_probs, axis=-1, keepdims=True)
    grad_logits = (probabilities * (grad_probs - inner)).astype(jnp.bfloat16)
    grad_queries = (
        jnp.einsum("bhqs,bshk->bqhk", grad_logits, key_rows, preferred_element_type=jnp.float32)
        * score_scale
    )
    grad_keys = (
        jnp.einsum("bhqs,bqhk->bshk", grad_logits, queries, preferred_element_type=jnp.float32)
        * score_scale
    )
    grad_values = jnp.einsum(
        "bhqs,bqhk->bshk",
        probabilities.astype(jnp.bfloat16),
        grad_out,
        preferred_element_type=jnp.float32,
    )
    return (
        grad_queries.astype(jnp.bfloat16),
        grad_keys.astype(jnp.bfloat16),
        grad_values.astype(jnp.bfloat16),
    )


def attention_forward(packed, masks, score_scale):
    members = [split_crops(member) for member in unpack_heads(packed)]
    results = []
    logsums = []
    for which in range(2):
        result, logsum = forward_tile(
            members[0][which], members[1][which], members[2][which], masks[which], score_scale
        )
        results.append(result)
        logsums.append(logsum)
    return (join_crops(results[0], results[1]).reshape(STREAM, packed.shape[2]), logsums)


def attention_backward(packed, grad_attended, logsums, masks, score_scale):
    members = [split_crops(member) for member in unpack_heads(packed)]
    grad_parts = split_crops(grad_attended.reshape(GROUP_IMG, IMG_ROWS, -1, HEAD_DIM))
    tile_grads = [
        backward_tile(
            members[0][which],
            members[1][which],
            members[2][which],
            grad_parts[which],
            masks[which],
            logsums[which],
            score_scale,
        )
        for which in range(2)
    ]
    joined = [
        join_crops(tile_grads[0][member], tile_grads[1][member]).reshape(STREAM, packed.shape[2])
        for member in range(3)
    ]
    return jnp.stack(joined)


def on_device(
    tokens,
    attn_gain,
    attn_shift,
    in_weight,
    query_value_bias,
    proj_weight,
    proj_bias,
    attn_scale,
    mlp_gain,
    mlp_shift,
    up_weight,
    up_bias,
    down_weight,
    down_bias,
    mlp_scale,
    crop_lengths,
    out_grad,
):
    wide_size = lax.axis_size("wide")
    crop_groups = wide_size // HEAD_GROUPS
    block_rows = TOK_DEV // crop_groups
    head_width = D // HEAD_GROUPS
    score_scale = HEAD_DIM ** (-0.5)
    own_group = lax.axis_index("wide") // HEAD_GROUPS
    own_lengths = lax.dynamic_slice_in_dim(crop_lengths, own_group * GROUP_IMG, GROUP_IMG, 0)
    masks = key_masks(own_lengths)
    inputs = tokens.astype(jnp.float32)
    first_gain = attn_gain.astype(jnp.float32)
    first_shift = attn_shift.astype(jnp.float32)
    normed, first_back = jax.vjp(layer_norm, inputs, first_gain, first_shift)
    normed_low = normed.astype(jnp.bfloat16)
    normed_blocks = normed_low.reshape(crop_groups, block_rows, D)
    weight_in = in_weight.reshape(D, 3, HEAD_GROUPS, head_width)
    qv_rows = query_value_bias.astype(jnp.float32)
    full_bias = jnp.stack([qv_rows[0], jnp.zeros_like(qv_rows[0]), qv_rows[1]]).reshape(
        3, 1, HEAD_GROUPS, 1, head_width
    )
    projected = (
        jnp.einsum("gbd,dchk->cghbk", normed_blocks, weight_in, preferred_element_type=jnp.float32)
        + full_bias
    )
    send_heads = projected.astype(jnp.bfloat16).reshape(3, wide_size, block_rows, head_width)
    arrived = lax.all_to_all(send_heads, "wide", split_axis=1, concat_axis=1, tiled=True)
    packed = arrived.reshape(3, STREAM, head_width)
    attended, logsums = attention_forward(packed, masks, score_scale)
    returned = lax.all_to_all(
        attended.reshape(wide_size, block_rows, head_width),
        "wide",
        split_axis=0,
        concat_axis=0,
        tiled=True,
    )
    mixed_rows = returned.reshape(crop_groups, HEAD_GROUPS, block_rows, head_width)
    weight_proj = proj_weight.reshape(HEAD_GROUPS, head_width, D)
    branch = jnp.einsum(
        "ghbk,hkd->gbd", mixed_rows, weight_proj, preferred_element_type=jnp.float32
    )
    branch = branch.reshape(TOK_DEV, D) + proj_bias.astype(jnp.float32)
    first_scale = attn_scale.astype(jnp.float32)
    middle = inputs + first_scale * branch
    second, second_back = jax.vjp(
        layer_norm, middle, mlp_gain.astype(jnp.float32), mlp_shift.astype(jnp.float32)
    )
    second_low = second.astype(jnp.bfloat16)
    hidden = jnp.dot(second_low, up_weight, preferred_element_type=jnp.float32) + up_bias.astype(
        jnp.float32
    )
    activated, gelu_back = jax.vjp(gelu_exact, hidden)
    activated_low = activated.astype(jnp.bfloat16)
    outcome = jnp.dot(
        activated_low, down_weight, preferred_element_type=jnp.float32
    ) + down_bias.astype(jnp.float32)
    second_scale = mlp_scale.astype(jnp.float32)
    output = (middle + second_scale * outcome).astype(jnp.bfloat16)
    cotangent = out_grad.astype(jnp.float32)
    grad_mlp_scale = jnp.sum(cotangent * outcome, axis=0)
    grad_outcome = (cotangent * second_scale).astype(jnp.bfloat16)
    grad_down_weight = jnp.einsum(
        "tf,td->fd", activated_low, grad_outcome, preferred_element_type=jnp.float32
    )
    grad_down_bias = jnp.sum(grad_outcome.astype(jnp.float32), axis=0)
    grad_activated = jnp.einsum(
        "td,fd->tf", grad_outcome, down_weight, preferred_element_type=jnp.float32
    )
    grad_hidden = gelu_back(grad_activated)[0].astype(jnp.bfloat16)
    grad_up_weight = jnp.einsum(
        "td,tf->df", second_low, grad_hidden, preferred_element_type=jnp.float32
    )
    grad_up_bias = jnp.sum(grad_hidden.astype(jnp.float32), axis=0)
    grad_second = jnp.einsum(
        "tf,df->td", grad_hidden, up_weight, preferred_element_type=jnp.float32
    )
    grad_middle, grad_mlp_gain, grad_mlp_shift = second_back(grad_second)
    grad_middle = grad_middle + cotangent
    grad_attn_scale = jnp.sum(grad_middle * branch, axis=0)
    grad_branch = (grad_middle * first_scale).astype(jnp.bfloat16)
    branch_blocks = grad_branch.reshape(crop_groups, block_rows, D)
    grad_proj_weight = jnp.einsum(
        "ghbk,gbd->hkd", mixed_rows, branch_blocks, preferred_element_type=jnp.float32
    ).reshape(D, D)
    grad_proj_bias = jnp.sum(grad_branch.astype(jnp.float32), axis=0)
    grad_mixed = jnp.einsum(
        "gbd,hkd->ghbk", branch_blocks, weight_proj, preferred_element_type=jnp.float32
    )
    grad_mixed = grad_mixed.astype(jnp.bfloat16).reshape(wide_size, block_rows, head_width)
    again, grad_arrived = (
        lax.all_to_all(send_heads, "wide", split_axis=1, concat_axis=1, tiled=True),
        lax.all_to_all(grad_mixed[None], "wide", split_axis=1, concat_axis=1, tiled=True),
    )
    packed_back = again.reshape(3, STREAM, head_width)
    grad_attended = grad_arrived.reshape(STREAM, head_width)
    grad_packed = attention_backward(packed_back, grad_attended, logsums, masks, score_scale)
    grad_sent = lax.all_to_all(
        grad_packed.reshape(3, wide_size, block_rows, head_width),
        "wide",
        split_axis=1,
        concat_axis=1,
        tiled=True,
    )
    grad_heads = grad_sent.reshape(3, crop_groups, HEAD_GROUPS, block_rows, head_width)
    grad_in_weight = jnp.einsum(
        "gbd,cghbk->dchk", normed_blocks, grad_heads, preferred_element_type=jnp.float32
    ).reshape(D, 3 * D)
    bias_sums = jnp.sum(grad_heads.astype(jnp.float32), axis=(1, 3)).reshape(3, D)
    grad_query_value_bias = jnp.stack([bias_sums[0], bias_sums[2]])
    grad_normed = jnp.einsum(
        "cghbk,dchk->gbd", grad_heads, weight_in, preferred_element_type=jnp.float32
    ).reshape(TOK_DEV, D)
    grad_inputs, grad_attn_gain, grad_attn_shift = first_back(grad_normed)
    input_grad = (grad_inputs + grad_middle).astype(jnp.bfloat16)
    shares = (
        lax.psum_scatter(
            grad_attn_gain.astype(jnp.bfloat16), "wide", scatter_dimension=0, tiled=True
        ).astype(jnp.float32),
        lax.psum_scatter(
            grad_attn_shift.astype(jnp.bfloat16), "wide", scatter_dimension=0, tiled=True
        ).astype(jnp.float32),
        lax.psum_scatter(
            grad_in_weight.astype(jnp.bfloat16), "wide", scatter_dimension=0, tiled=True
        ).astype(jnp.float32),
        lax.psum_scatter(
            grad_query_value_bias.astype(jnp.bfloat16), "wide", scatter_dimension=1, tiled=True
        ).astype(jnp.float32),
        lax.psum_scatter(
            grad_proj_weight.astype(jnp.bfloat16), "wide", scatter_dimension=0, tiled=True
        ).astype(jnp.float32),
        lax.psum_scatter(
            grad_proj_bias.astype(jnp.bfloat16), "wide", scatter_dimension=0, tiled=True
        ).astype(jnp.float32),
        lax.psum_scatter(
            grad_attn_scale.astype(jnp.bfloat16), "wide", scatter_dimension=0, tiled=True
        ).astype(jnp.float32),
        lax.psum_scatter(
            grad_mlp_gain.astype(jnp.bfloat16), "wide", scatter_dimension=0, tiled=True
        ).astype(jnp.float32),
        lax.psum_scatter(
            grad_mlp_shift.astype(jnp.bfloat16), "wide", scatter_dimension=0, tiled=True
        ).astype(jnp.float32),
        lax.psum_scatter(
            grad_up_weight.astype(jnp.bfloat16), "wide", scatter_dimension=0, tiled=True
        ).astype(jnp.float32),
        lax.psum_scatter(
            grad_up_bias.astype(jnp.bfloat16), "wide", scatter_dimension=0, tiled=True
        ).astype(jnp.float32),
        lax.psum_scatter(
            grad_down_weight.astype(jnp.bfloat16), "wide", scatter_dimension=0, tiled=True
        ).astype(jnp.float32),
        lax.psum_scatter(
            grad_down_bias.astype(jnp.bfloat16), "wide", scatter_dimension=0, tiled=True
        ).astype(jnp.float32),
        lax.psum_scatter(
            grad_mlp_scale.astype(jnp.bfloat16), "wide", scatter_dimension=0, tiled=True
        ).astype(jnp.float32),
    )
    results = (
        lax.psum(shares[0].astype(jnp.bfloat16), "narrow").astype(jnp.float32),
        lax.psum(shares[1].astype(jnp.bfloat16), "narrow").astype(jnp.float32),
        lax.psum(shares[2].astype(jnp.bfloat16), "narrow").astype(jnp.float32),
        lax.psum(shares[3].astype(jnp.bfloat16), "narrow").astype(jnp.float32),
        lax.psum(shares[4].astype(jnp.bfloat16), "narrow").astype(jnp.float32),
        lax.psum(shares[5].astype(jnp.bfloat16), "narrow").astype(jnp.float32),
        lax.psum(shares[6].astype(jnp.bfloat16), "narrow").astype(jnp.float32),
        lax.psum(shares[7].astype(jnp.bfloat16), "narrow").astype(jnp.float32),
        lax.psum(shares[8].astype(jnp.bfloat16), "narrow").astype(jnp.float32),
        lax.psum(shares[9].astype(jnp.bfloat16), "narrow").astype(jnp.float32),
        lax.psum(shares[10].astype(jnp.bfloat16), "narrow").astype(jnp.float32),
        lax.psum(shares[11].astype(jnp.bfloat16), "narrow").astype(jnp.float32),
        lax.psum(shares[12].astype(jnp.bfloat16), "narrow").astype(jnp.float32),
        lax.psum(shares[13].astype(jnp.bfloat16), "narrow").astype(jnp.float32),
    )
    return (
        output,
        input_grad,
        results[0],
        results[1],
        results[2],
        results[3],
        results[4],
        results[5],
        results[6],
        results[7],
        results[8],
        results[9],
        results[10],
        results[11],
        results[12],
        results[13],
    )


MESH = pl.DeviceIdType.MESH
F32 = jnp.float32
BF16 = jnp.bfloat16
SLOT = 288
ROWS = 576
UNITS = 18
PAIRS = 9
BLOCK = 48
BLOCKS = ROWS // BLOCK
ATTN_GAIN, ATTN_SHIFT, Q_BIAS, V_BIAS, PROJ_BIAS, ATTN_SCALE, MLP_GAIN, MLP_SHIFT, DOWN_BIAS, MLP_SCALE = range(10)
UP_BIAS = 10


def dot_nn(a, b):
    return jnp.dot(a, b, preferred_element_type=F32)


def dot_nt(a, b):
    return lax.dot_general(a, b, (((1,), (1,)), ((), ())), preferred_element_type=F32)


def dot_tn(a, b):
    return lax.dot_general(a, b, (((0,), (0,)), ((), ())), preferred_element_type=F32)


def halves(block):
    lanes = lax.broadcasted_iota(jnp.int32, block.shape, 1)
    zero = jnp.zeros_like(block)
    return [jnp.where((lanes < 64) == (h == 0), block, zero) for h in range(2)]


def fold_rows(values):
    return jnp.sum(values.reshape(values.shape[0] // 8, 8, values.shape[1]), axis=0)


def norm_parts(values):
    mean = jnp.sum(values, axis=-1, keepdims=True) * (1.0 / D)
    centered = values - mean
    variance = jnp.sum(centered * centered, axis=-1, keepdims=True) * (1.0 / D)
    rstd = lax.rsqrt(variance + NORM_EPSILON)
    return centered * rstd, rstd


def layer_kernel(
    tok_ref, og_ref, len_ref,
    attn_gain_ref, attn_shift_ref, qv_ref, proj_bias_ref, attn_scale_ref, mlp_gain_ref, mlp_shift_ref,
    up_bias_ref, down_bias_ref, mlp_scale_ref,
    in_hbm, proj_hbm, up_hbm, down_hbm,
    out_hbm, ig_hbm, gin_ref, gproj_ref, gup_ref, gdown_ref, vout_ref,
    win, wproj, wup, wdown,
    xb, db, ob, h1, t1, t2, qkv, att, branch, mid, h2, dm, gact, dhid, macc, dacc, ub, gb, bias, bias_t,
    prm, sums, usums,
    gbuf, r0, r1, r2, r3, r4, fin, wdt, vbuf, vrecv,
    wsem, upsem, lsem, hsend, hrecv, ssem, rsem, vssem, vrsem,
):
    n = lax.axis_index("narrow")
    w = lax.axis_index("wide")
    c = n % 2
    y = n // 2
    x = w % 2
    z1 = (w // 2) % 2
    z2 = w // 4
    quarter = w % 4
    shift = 32 * (quarter % 2) + 32 * (quarter // 2) * (2 - 2 * (quarter % 2)) + 0 * quarter
    partner = {
        "core": (n + 1 - 2 * c, w),
        "y": (n + 2 - 4 * y, w),
        "x": (n, w + 1 - 2 * x),
        "z1": (n, w + 2 - 4 * z1),
        "z2": (n, w + 4 - 8 * z2),
        "diagonal": (n, w + 3 - 2 * quarter),
    }

    weights = [
        pltpu.make_async_copy(in_hbm, win, wsem.at[0]),
        pltpu.make_async_copy(proj_hbm, wproj, wsem.at[1]),
    ]
    downs = [pltpu.make_async_copy(down_hbm.at[:, j], wdown.at[j], wsem.at[2 + j]) for j in range(3)]
    ups = [
        [
            pltpu.make_async_copy(
                up_hbm.at[:, 128 * (3 * s + j) : 128 * (3 * s + j + 1)],
                wup.at[:, 128 * (8 * j + s) : 128 * (8 * j + s + 1)],
                upsem.at[j, s],
            )
            for s in range(8)
        ]
        for j in range(3)
    ]
    own = pl.ds(pl.multiple_of(64 - shift, 32), 256)
    loads = [
        pltpu.make_async_copy(tok_ref, xb.at[:, own], lsem.at[0]),
        pltpu.make_async_copy(og_ref, db.at[:, own], lsem.at[1]),
    ]
    loads[0].start()
    weights[0].start()
    loads[1].start()
    weights[1].start()
    for j in range(3):
        for s in range(8):
            ups[j][s].start()
        downs[j].start()

    barrier = pltpu.get_barrier_semaphore()
    for target in partner.values():
        pl.semaphore_signal(barrier, inc=1, device_id=target, device_id_type=MESH)
    pl.semaphore_wait(barrier, 6)

    before_shift = 32 * ((quarter + 3) % 2) + 32 * ((quarter - 1) // 2) * (2 - 2 * ((quarter + 3) % 2))
    before = (n, w - 1)
    after = (n, w + 1)

    def halo_in(src, dst, k):
        return pltpu.make_async_remote_copy(
            src_ref=src.at[:, 0:64],
            dst_ref=dst.at[:, pl.ds(pl.multiple_of(320 - before_shift, 32), 64)],
            send_sem=hsend.at[k], recv_sem=hrecv.at[k], device_id=before, device_id_type=MESH,
        )

    def halo_back(buf, k, size):
        return pltpu.make_async_remote_copy(
            src_ref=buf.at[:, pl.ds(pl.multiple_of(320 - shift, 32), size)],
            dst_ref=buf.at[:, 64 - size : 64],
            send_sem=hsend.at[k], recv_sem=hrecv.at[k], device_id=after, device_id_type=MESH,
        )

    @pl.when(quarter > 0)
    def _():
        halo_in(tok_ref, xb, 0).start()
        halo_in(og_ref, db, 1).start()

    for row, ref in (
        (ATTN_GAIN, attn_gain_ref), (ATTN_SHIFT, attn_shift_ref), (PROJ_BIAS, proj_bias_ref), (ATTN_SCALE, attn_scale_ref),
        (MLP_GAIN, mlp_gain_ref), (MLP_SHIFT, mlp_shift_ref), (DOWN_BIAS, down_bias_ref), (MLP_SCALE, mlp_scale_ref),
    ):
        prm[row : row + 1, 0:D] = ref[...].astype(F32).reshape(1, D)
    qv = qv_ref[...].astype(F32)
    prm[Q_BIAS : Q_BIAS + 1, 0:D] = qv[0:1]
    prm[V_BIAS : V_BIAS + 1, 0:D] = qv[1:2]
    up_row = up_bias_ref[...].astype(F32).reshape(1, 4 * D)
    for j in range(3):
        for s in range(8):
            prm[UP_BIAS + j : UP_BIAS + j + 1, 128 * s : 128 * (s + 1)] = up_row[:, 128 * (3 * s + j) : 128 * (3 * s + j + 1)]
    sums[...] = jnp.zeros_like(sums)
    usums[...] = jnp.zeros_like(usums)

    def param(row):
        return prm[row : row + 1, 0:D]

    is_local = quarter // 2
    for i in range(2):
        image = 2 * i + z2

        def crop_of(axis, valid_only):
            shape = (1, SLOT) if axis == 1 else (SLOT, 1)
            place = lax.broadcasted_iota(jnp.int32, shape, axis)
            ids = jnp.full(shape, -1 if valid_only else 4, jnp.int32)
            for m in range(4):
                start = 56 * m * is_local
                if valid_only:
                    local_length = len_ref[image, 2 + 4 * (quarter % 2) + m]
                    global_length = len_ref[image, quarter % 2] if m == 0 else 0
                    size = is_local * local_length + (1 - is_local) * global_length
                else:
                    size = 56 * is_local + (1 - is_local) * (SLOT if m == 0 else 0)
                inside = jnp.logical_and(place >= start, place < start + size)
                ids = jnp.where(inside, m, ids)
            return ids

        bias[i] = jnp.where(crop_of(0, False) == crop_of(1, True), 0.0, MASKED)
        bias_t[i] = jnp.where(crop_of(1, False) == crop_of(0, True), 0.0, MASKED)

    for load in loads:
        load.wait()

    @pl.when(quarter > 0)
    def _():
        halo_in(tok_ref, xb, 0).wait_send()
        halo_in(og_ref, db, 1).wait_send()

    @pl.when(quarter < 3)
    def _():
        halo_in(tok_ref, xb, 0).wait_recv()
        halo_in(og_ref, db, 1).wait_recv()

    @pl.when(quarter > 1)
    def _():
        xb[:, 288:352] = jnp.zeros((2, 64, D), BF16)
        db[:, 288:352] = jnp.zeros((2, 64, D), BF16)

    def at(b):
        i, k = b // 6, b % 6
        return i, pl.ds(pl.multiple_of(64 + BLOCK * k, 16), BLOCK), pl.ds(pl.multiple_of(BLOCK * b, 16), BLOCK)

    def first_norm(b, _):
        i, slots, rows = at(b)
        normed, _ = norm_parts(xb[i, slots].astype(F32))
        h1[rows] = (normed * param(ATTN_GAIN) + param(ATTN_SHIFT)).astype(BF16)
        grad = db[i, slots].astype(F32)
        low = (grad * param(MLP_SCALE)).astype(BF16)
        dm[rows] = low
        sums[DOWN_BIAS] += fold_rows(low.astype(F32))
        return 0

    lax.fori_loop(0, BLOCKS, first_norm, 0)

    weights[0].wait()
    for tile in range(9):
        cols = slice(256 * tile, 256 * (tile + 1))
        result = dot_nn(h1[...], win[:, cols])
        if tile < 3:
            result = (result + prm[Q_BIAS : Q_BIAS + 1, cols]).astype(BF16) * jnp.asarray(0.125, BF16)
        elif tile >= 6:
            result = result + prm[V_BIAS : V_BIAS + 1, 256 * (tile - 6) : 256 * (tile - 5)]
        qkv[:, cols] = result.astype(BF16)

    def pair_at(index):
        i, h = index // 6, index % 6
        rows = pl.ds(pl.multiple_of(SLOT * i, 16), SLOT)
        return i, rows, [pl.ds(pl.multiple_of(D * m + 128 * h, 128), 128) for m in range(3)]

    def attend(index, _):
        i, rows, cols = pair_at(index)
        q, v = qkv[rows, cols[0]], qkv[rows, cols[2]]
        keys = halves(qkv[rows, cols[1]])
        lanes = lax.broadcasted_iota(jnp.int32, (SLOT, 128), 1)
        ones = jnp.ones_like(v)
        parts = []
        for h in range(2):
            s = dot_nt(q, keys[h]) + bias[i]
            e = jnp.exp(s - jnp.max(s, axis=-1, keepdims=True)).astype(BF16)
            part = dot_nn(e, jnp.where((lanes < 64) == (h == 0), v, ones))
            parts.append(part / pltpu.roll(part, 64, 1))
        att[rows, cols[0]] = jnp.where(lanes < 64, parts[0], parts[1]).astype(BF16)
        return 0

    lax.fori_loop(0, 12, attend, 0)

    weights[1].wait()
    for tile in range(3):
        cols = slice(256 * tile, 256 * (tile + 1))
        result = dot_nn(att[...], wproj[:, cols]) + prm[PROJ_BIAS : PROJ_BIAS + 1, cols]
        branch[:, cols] = result.astype(BF16)
        scaled = prm[ATTN_SCALE : ATTN_SCALE + 1, cols] * result
        for i in range(2):
            mid[SLOT * i : SLOT * (i + 1), cols] = (
                xb[i, 64 : 64 + SLOT, cols].astype(F32) + scaled[SLOT * i : SLOT * (i + 1)]
            )

    def second_norm(b, _):
        _, _, rows = at(b)
        normed, _ = norm_parts(mid[rows])
        h2[rows] = (normed * param(MLP_GAIN) + param(MLP_SHIFT)).astype(BF16)
        return 0

    lax.fori_loop(0, BLOCKS, second_norm, 0)

    def transpose_into(dst, src):
        for k in range(6):
            dst[128 * k : 128 * (k + 1)] = src[:, 128 * k : 128 * (k + 1)].T

    def copy(src, dst, unit, stage, axis):
        return pltpu.make_async_remote_copy(
            src_ref=src, dst_ref=dst, send_sem=ssem.at[unit, stage], recv_sem=rsem.at[unit, stage],
            device_id=partner[axis], device_id_type=MESH,
        )

    def even(u, k):
        if k == 0:
            return copy(gbuf.at[u, 1 - c], r0.at[u % r0.shape[0]], u, 0, "core")
        if k == 1:
            return copy(gbuf.at[u, c, :, 1 - x], r1.at[u % r1.shape[0]], u, 1, "x")
        if k == 2:
            return copy(gbuf.at[u, c, :, x, 1 - z1], r2.at[u % r2.shape[0]], u, 2, "z1")
        if k == 3:
            return copy(gbuf.at[u, c, :, x, z1, 1 - z2], r3.at[u % r3.shape[0]], u, 3, "z2")
        if k == 4:
            return copy(gbuf.at[u, c, :, x, z1, z2], r4.at[u % r4.shape[0]], u, 4, "y")
        return copy(fin.at[u, c], fin.at[u, c], u, 5, "core")

    def odd(u, k):
        if k == 0:
            return copy(gbuf.at[u, 1 - c], r0.at[u % r0.shape[0]], u, 0, "core")
        if k == 1:
            return copy(gbuf.at[u, c, 1 - y], r1.at[u % r1.shape[0]], u, 1, "y")
        if k == 2:
            return copy(gbuf.at[u, c, y, 1 - x], r2.at[u % r2.shape[0]], u, 2, "x")
        if k == 3:
            return copy(gbuf.at[u, c, y, x, 1 - z1], r3.at[u % r3.shape[0]], u, 3, "z1")
        if k == 4:
            return copy(gbuf.at[u, c, y, x, z1, 1 - z2], r4.at[u % r4.shape[0], 0], u, 4, "z2")
        if k == 5:
            return copy(fin.at[u, c, y], fin.at[u, c, y], u, 5, "y")
        return copy(fin.at[u, c], fin.at[u, c], u, 6, "core")

    def add(dst, src):
        dst[...] = (dst[...].astype(F32) + src[...].astype(F32)).astype(BF16)

    def land_core(u):
        def body(index, _):
            yy, xx = index // 2, index % 2
            add(gbuf.at[u, c, yy, xx], r0.at[u % r0.shape[0], yy, xx])
            return 0

        lax.fori_loop(0, 4, body, 0)

    def even_land(u, k):
        if k == 0:
            land_core(u)
        elif k == 1:
            for yy in range(2):
                add(gbuf.at[u, c, yy, x], r1.at[u % r1.shape[0], yy])
        elif k == 2:
            add(gbuf.at[u, c, :, x, z1], r2.at[u % r2.shape[0]])
        elif k == 3:
            add(gbuf.at[u, c, :, x, z1, z2], r3.at[u % r3.shape[0]])
        elif k == 4:
            total = gbuf[u, c, :, x, z1, z2].astype(F32) + r4[u % r4.shape[0]].astype(F32)
            fin[u, c] = total.astype(BF16)

    def odd_land(u, k):
        if k == 0:
            land_core(u)
        elif k == 1:
            for xx in range(2):
                add(gbuf.at[u, c, y, xx], r1.at[u % r1.shape[0], xx])
        elif k == 2:
            add(gbuf.at[u, c, y, x], r2.at[u % r2.shape[0]])
        elif k == 3:
            add(gbuf.at[u, c, y, x, z1], r3.at[u % r3.shape[0]])
        elif k == 4:
            total = gbuf[u, c, y, x, z1, z2].astype(F32) + r4[u % r4.shape[0], 0].astype(F32)
            fin[u, c, y] = total.astype(BF16)

    def write_out(p, a):
        u = 2 * p + a
        is_mlp = p < 6

        @pl.when(jnp.logical_and(is_mlp, p % 2 == 0))
        def _():
            for sub in range(4):
                wdt[384 * a + 96 * sub : 384 * a + 96 * (sub + 1), pl.ds(pl.multiple_of(128 * (p // 2), 128), 128)] = fin[
                    u, sub // 2, sub % 2
                ]

        @pl.when(jnp.logical_and(is_mlp, p % 2 == 1))
        def _():
            for sub in range(4):
                tile = 3 * (4 * a + sub) + p // 2
                gup_ref[:, pl.ds(pl.multiple_of(128 * tile, 128), 128)] = fin[u, sub // 2, sub % 2]

        @pl.when(p >= 6)
        def _():
            for cc in range(2):
                tile = 4 * (p - 6) + 2 * a + cc

                @pl.when(tile < 9)
                def _():
                    for yy in range(2):
                        gin_ref[:, pl.ds(pl.multiple_of(256 * tile + 128 * yy, 128), 128)] = fin[u, cc, yy]

                @pl.when(tile >= 9)
                def _():
                    for yy in range(2):
                        start = pl.multiple_of(256 * (tile - 9) + 128 * yy, 128)
                        gproj_ref[:, pl.ds(start, 128)] = fin[u, cc, yy]

    def event(p, k):
        u = 2 * p
        if k < 6:
            even(u, k).wait()
            even_land(u, k)
            if k < 5:
                even(u, k + 1).start()
            else:
                write_out(p, 0)
        odd(u + 1, k).wait()
        odd_land(u + 1, k)
        if k < 6:
            odd(u + 1, k + 1).start()
        else:
            write_out(p, 1)

    def guarded(p, k):
        if isinstance(p, int):
            if 0 <= p < PAIRS:
                event(p, k)
            return

        @pl.when(jnp.logical_and(p >= 0, p < PAIRS))
        def _():
            event(p, k)

    def send(p):
        even(2 * p, 0).start()
        even(2 * p + 1, 0).start()

    def back(b):
        for k in range(1, 7):
            guarded(b + 1 - k, k)

    transpose_into(t1, dm)
    transpose_into(t2, h2)

    def gelu_block(j, tile, b):
        _, _, rows = at(b)
        cols = pl.ds(pl.multiple_of(256 * tile, 256), 256)
        u = ub[rows] + prm[pl.ds(UP_BIAS + j, 1), cols]
        phi = 0.5 * (1.0 + lax.erf(u * 0.7071067811865476))
        gact[rows, cols] = (u * phi).astype(BF16)
        slope = phi + u * (jnp.exp(u * u * -0.5) * 0.3989422804014327)
        low = (gb[rows] * slope).astype(BF16)
        dhid[rows, cols] = low
        usums[:, pl.ds(pl.multiple_of(1024 * j + 256 * tile, 256), 256)] += fold_rows(low.astype(F32))

    def mlp(j, _):
        def wait_weights(jj):
            for s in range(8):
                ups[jj][s].wait()
            downs[jj].wait()

        for jj in range(3):

            @pl.when(j == jj)
            def _(jj=jj):
                wait_weights(jj)

        def hidden_tile(tile, _):
            cols = pl.ds(pl.multiple_of(1024 * j + 256 * tile, 256), 256)
            ub[...] = dot_nn(h2[...], wup[:, cols])
            down = wdown[j, pl.ds(2 * tile, 2)].reshape(256, D)
            gb[...] = dot_nt(dm[...], down)

            def block(b, _):
                gelu_block(j, tile, b)
                return 0

            lax.fori_loop(0, BLOCKS, block, 0)
            return 0

        lax.fori_loop(0, 4, hidden_tile, 0)

        def down_grad(nt, _):
            result = dot_nn(t1[...], gact[:, pl.ds(pl.multiple_of(256 * nt, 256), 256)])
            for ss in range(2):
                for sub in range(8):
                    gbuf[4 * j + sub // 4, (sub // 2) % 2, sub % 2, ss, nt % 2, nt // 2] = result[
                        96 * sub : 96 * (sub + 1), 128 * ss : 128 * (ss + 1)
                    ].astype(BF16)
            return 0

        lax.fori_loop(0, 4, down_grad, 0)
        back(2 * j - 4)
        send(2 * j)

        def up_grad(nt, _):
            result = dot_nn(t2[...], dhid[:, pl.ds(pl.multiple_of(256 * nt, 256), 256)])
            for s in range(8):
                for yy in range(2):
                    gbuf[4 * j + 2 + nt // 2, nt % 2, yy, s % 2, (s // 2) % 2, s // 4] = result[
                        96 * s : 96 * (s + 1), 128 * yy : 128 * (yy + 1)
                    ].astype(BF16)
            return 0

        lax.fori_loop(0, 4, up_grad, 0)
        send(2 * j + 1)
        event(2 * j, 0)

        def combine(nt, _):
            cols = pl.ds(pl.multiple_of(256 * nt, 256), 256)
            up_rows = wup[cols, pl.ds(pl.multiple_of(1024 * j, 1024), 1024)]
            more = dot_nn(gact[...], wdown[j, :, :, cols].reshape(1024, 256))
            more_d = dot_nt(dhid[...], up_rows)

            @pl.when(j == 0)
            def _():
                macc[:, cols] = more
                dacc[:, cols] = more_d

            @pl.when(j > 0)
            def _():
                macc[:, cols] += more
                dacc[:, cols] += more_d

            return 0

        lax.fori_loop(0, 3, combine, 0)
        event(2 * j + 1, 0)
        return 0

    lax.fori_loop(0, 3, mlp, 0)

    back(1)

    def second_back(b, _):
        i, slots, rows = at(b)
        grad = db[i, slots].astype(F32)
        y_rows = mid[rows]
        outcome = macc[rows] + param(DOWN_BIAS)
        ob[i, slots] = (y_rows + param(MLP_SCALE) * outcome).astype(BF16)
        sums[MLP_SCALE] += fold_rows(grad * outcome)
        normed, rstd = norm_parts(y_rows)
        dh = dacc[rows]
        sums[MLP_GAIN] += fold_rows(dh * normed)
        sums[MLP_SHIFT] += fold_rows(dh)
        e = dh * param(MLP_GAIN)
        mean_e = jnp.sum(e, axis=-1, keepdims=True) * (1.0 / D)
        mean_en = jnp.sum(e * normed, axis=-1, keepdims=True) * (1.0 / D)
        dy = grad + rstd * (e - mean_e - normed * mean_en)
        dacc[rows] = dy
        sums[ATTN_SCALE] += fold_rows(dy * branch[rows].astype(F32))
        low = (dy * param(ATTN_SCALE)).astype(BF16)
        dm[rows] = low
        sums[PROJ_BIAS] += fold_rows(low.astype(F32))
        return 0

    lax.fori_loop(0, BLOCKS, second_back, 0)

    def give_back(buf, k):
        @pl.when(quarter % 2 == 0)
        def _():
            halo_back(buf, k, 32).start()

        @pl.when(quarter == 1)
        def _():
            halo_back(buf, k, 64).start()

    def take_back(buf, k):
        @pl.when(quarter % 2 == 0)
        def _():
            halo_back(buf, k, 32).wait_send()

        @pl.when(quarter == 1)
        def _():
            halo_back(buf, k, 64).wait_send()

        @pl.when(quarter % 2 == 1)
        def _():
            halo_back(buf, k, 32).wait_recv()

        @pl.when(quarter == 2)
        def _():
            halo_back(buf, k, 64).wait_recv()

    give_back(ob, 2)

    for tile in range(3):
        cols = slice(256 * tile, 256 * (tile + 1))
        h2[:, cols] = dot_nt(dm[...], wproj[cols]).astype(BF16)

    def attend_back(index, _):
        i, rows, cols = pair_at(index)
        k, v = qkv[rows, cols[1]], qkv[rows, cols[2]]
        queries, keys, grads = halves(qkv[rows, cols[0]]), halves(k), halves(h2[rows, cols[0]])
        dq = dk = dv = None
        for h in range(2):
            s = dot_nt(k, queries[h]) + bias_t[i]
            e = jnp.exp(s - jnp.max(s, axis=0, keepdims=True))
            p = e * (1.0 / jnp.sum(e, axis=0, keepdims=True))
            dp = dot_nt(v, grads[h])
            ds = (p * (dp - jnp.sum(p * dp, axis=0, keepdims=True))).astype(BF16)
            parts = dot_tn(ds, keys[h]), dot_nn(ds, queries[h]), dot_nn(p.astype(BF16), grads[h])
            dq, dk, dv = parts if dq is None else (dq + parts[0], dk + parts[1], dv + parts[2])
        low_q, low_v = (dq * 0.125).astype(BF16), dv.astype(BF16)
        qkv[rows, cols[0]] = low_q
        qkv[rows, cols[1]] = dk.astype(BF16)
        qkv[rows, cols[2]] = low_v
        sums[Q_BIAS, :, cols[0]] += fold_rows(low_q.astype(F32))
        sums[V_BIAS, :, cols[0]] += fold_rows(low_v.astype(F32))
        return 0

    lax.fori_loop(0, 4, attend_back, 0)
    back(2)
    lax.fori_loop(4, 9, attend_back, 0)
    back(3)
    lax.fori_loop(9, 12, attend_back, 0)

    transpose_into(t1, h1)
    transpose_into(t2, att)

    def attn_grad(index, _):
        m, nt = index // 4, index % 4

        def put(result):
            for s in range(8):
                for yy in range(2):
                    gbuf[12 + 2 * m + nt // 2, nt % 2, yy, s % 2, (s // 2) % 2, s // 4] = result[
                        96 * s : 96 * (s + 1), 128 * yy : 128 * (yy + 1)
                    ].astype(BF16)

        @pl.when(index < 9)
        def _():
            put(dot_nn(t1[...], qkv[:, pl.ds(pl.multiple_of(256 * index, 256), 256)]))

        @pl.when(index >= 9)
        def _():
            put(dot_nn(t2[...], dm[:, pl.ds(pl.multiple_of(256 * (index - 9), 256), 256)]))

        return 0

    for m in range(3):
        lax.fori_loop(4 * m, 4 * m + 4, attn_grad, 0)
        send(6 + m)
        if m > 0:
            event(5 + m, 0)
    event(8, 0)
    back(4)

    for tile in range(3):
        cols = slice(256 * tile, 256 * (tile + 1))
        macc[:, cols] = dot_nt(qkv[...], win[cols])

    def first_back(b, _):
        i, slots, rows = at(b)
        normed, rstd = norm_parts(xb[i, slots].astype(F32))
        dh = macc[rows]
        sums[ATTN_GAIN] += fold_rows(dh * normed)
        sums[ATTN_SHIFT] += fold_rows(dh)
        e = dh * param(ATTN_GAIN)
        mean_e = jnp.sum(e, axis=-1, keepdims=True) * (1.0 / D)
        mean_en = jnp.sum(e * normed, axis=-1, keepdims=True) * (1.0 / D)
        db[i, slots] = (dacc[rows] + rstd * (e - mean_e - normed * mean_en)).astype(BF16)
        return 0

    lax.fori_loop(0, BLOCKS, first_back, 0)
    give_back(db, 3)

    vaxes = ("core", "x", "y", "z1", "z2")

    def vcopy(k):
        return pltpu.make_async_remote_copy(
            src_ref=vbuf.at[k], dst_ref=vrecv.at[k], send_sem=vssem.at[k], recv_sem=vrsem.at[k],
            device_id=partner[vaxes[k]], device_id_type=MESH,
        )

    def vland(k):
        vcopy(k).wait()
        vbuf[k + 1] = vbuf[k] + vrecv[k]
        if k < 4:
            vcopy(k + 1).start()

    vbuf[0] = jnp.zeros_like(vbuf[0])
    for row in range(10):
        vbuf[0, row : row + 1, 0:D] = jnp.sum(sums[row], axis=0, keepdims=True)
    for j in range(3):
        vbuf[0, UP_BIAS + j : UP_BIAS + j + 1] = jnp.sum(usums[:, 1024 * j : 1024 * (j + 1)], axis=0, keepdims=True)
    vcopy(0).start()

    def drain(b, _):
        back(b)
        for k in range(5):

            @pl.when(b == 5 + k)
            def _(k=k):
                vland(k)

        return 0

    lax.fori_loop(5, PAIRS + 5, drain, 0)

    rolled = pltpu.roll(vbuf[5, :, 0:D], (D - 96 * w) % D, 1)
    vout_ref[...] = rolled[:, 0:128]
    vout_ref[UP_BIAS : UP_BIAS + 3] = vbuf[5, UP_BIAS : UP_BIAS + 3, pl.ds(pl.multiple_of(128 * w, 128), 128)]

    for a in range(3):
        for b in range(6):
            gdown_ref[128 * a : 128 * (a + 1), 128 * b : 128 * (b + 1)] = wdt[
                128 * b : 128 * (b + 1), 128 * a : 128 * (a + 1)
            ].T

    take_back(ob, 2)
    take_back(db, 3)
    stores = [
        pltpu.make_async_copy(ob.at[:, own], out_hbm, lsem.at[0]),
        pltpu.make_async_copy(db.at[:, own], ig_hbm, lsem.at[1]),
    ]
    for store in stores:
        store.start()
    for store in stores:
        store.wait()


def layer(tokens, out_grad, lengths, vectors, weights):
    vm = pl.BlockSpec(memory_space=pltpu.VMEM)
    hbm = pl.BlockSpec(memory_space=pl.ANY)
    dma = pltpu.SemaphoreType.DMA
    slots = pltpu.VMEM((2, 384, D), BF16)
    square = pltpu.VMEM((ROWS, D), BF16)
    wide_square = pltpu.VMEM((ROWS, D), F32)
    block = (96, 128)
    return pl.pallas_call(
        layer_kernel,
        out_shape=(
            jax.ShapeDtypeStruct((2, 256, D), BF16),
            jax.ShapeDtypeStruct((2, 256, D), BF16),
            jax.ShapeDtypeStruct((96, 3 * D), BF16),
            jax.ShapeDtypeStruct((96, D), BF16),
            jax.ShapeDtypeStruct((96, 4 * D), BF16),
            jax.ShapeDtypeStruct((384, D), BF16),
            jax.ShapeDtypeStruct((16, 128), F32),
        ),
        in_specs=[hbm, hbm, pl.BlockSpec(memory_space=pltpu.SMEM)] + [vm] * 10 + [hbm] * 4,
        out_specs=(hbm, hbm, vm, vm, vm, vm, vm),
        scratch_shapes=[
            pltpu.VMEM((D, 3 * D), BF16),
            pltpu.VMEM((D, D), BF16),
            pltpu.VMEM((D, 4 * D), BF16),
            pltpu.VMEM((3, 8, 128, D), BF16),
            slots, slots, slots,
            square,
            pltpu.VMEM((D, ROWS), BF16),
            pltpu.VMEM((D, ROWS), BF16),
            pltpu.VMEM((ROWS, 3 * D), BF16),
            square, square,
            wide_square,
            square, square,
            pltpu.VMEM((ROWS, 1024), BF16),
            pltpu.VMEM((ROWS, 1024), BF16),
            wide_square, wide_square,
            pltpu.VMEM((ROWS, 256), F32),
            pltpu.VMEM((ROWS, 256), F32),
            pltpu.VMEM((2, SLOT, SLOT), F32),
            pltpu.VMEM((2, SLOT, SLOT), F32),
            pltpu.VMEM((16, 1024), F32),
            pltpu.VMEM((10, 8, D), F32),
            pltpu.VMEM((8, 4 * D), F32),
            pltpu.VMEM((UNITS, 2, 2, 2, 2, 2) + block, BF16),
            pltpu.VMEM((8, 2, 2, 2, 2) + block, BF16),
            pltpu.VMEM((12, 2, 2, 2) + block, BF16),
            pltpu.VMEM((8, 2, 2) + block, BF16),
            pltpu.VMEM((8, 2) + block, BF16),
            pltpu.VMEM((8, 2) + block, BF16),
            pltpu.VMEM((UNITS, 2, 2) + block, BF16),
            pltpu.VMEM((D, 384), BF16),
            pltpu.VMEM((6, 16, 1024), F32),
            pltpu.VMEM((5, 16, 1024), F32),
            dma((5,)), dma((3, 8)), dma((2,)), dma((4,)), dma((4,)),
            dma((UNITS, 7)), dma((UNITS, 7)), dma((5,)), dma((5,)),
        ],
        compiler_params=pltpu.CompilerParams(collective_id=0, has_side_effects=True, vmem_limit_bytes=64 << 20),
        name="layer",
    )(tokens, out_grad, lengths, *vectors, *weights)


def on_device_local(
    tokens, attn_gain, attn_shift, in_weight, query_value_bias, proj_weight, proj_bias, attn_scale,
    mlp_gain, mlp_shift, up_weight, up_bias, down_weight, down_bias, mlp_scale, crop_lengths, out_grad,
):
    output, input_grad, g_in, g_proj, g_up, g_down, v = layer(
        tokens.reshape(2, 256, D), out_grad.reshape(2, 256, D), crop_lengths,
        (attn_gain, attn_shift, query_value_bias, proj_bias, attn_scale, mlp_gain, mlp_shift, up_bias, down_bias, mlp_scale),
        (in_weight, proj_weight, up_weight, down_weight.reshape(8, 3, 128, D)),
    )
    rows = v[:10, :96]
    return (
        output.reshape(TOK_DEV, D), input_grad.reshape(TOK_DEV, D),
        rows[ATTN_GAIN], rows[ATTN_SHIFT], g_in.astype(F32), rows[Q_BIAS : V_BIAS + 1], g_proj.astype(F32), rows[PROJ_BIAS],
        rows[ATTN_SCALE], rows[MLP_GAIN], rows[MLP_SHIFT], g_up.astype(F32), v[UP_BIAS : UP_BIAS + 3].reshape(384),
        g_down.astype(F32), rows[DOWN_BIAS], rows[MLP_SCALE],
    )


def solution(mesh):
    local = mesh.shape["wide"] == 8 and mesh.shape["narrow"] == 4
    return jax.shard_map(
        on_device_local if local else on_device,
        mesh=mesh,
        in_specs=(
            P(("narrow", "wide"), None),
            P(),
            P(),
            P(),
            P(),
            P(),
            P(),
            P(),
            P(),
            P(),
            P(),
            P(),
            P(),
            P(),
            P(),
            P("narrow", None),
            P(("narrow", "wide"), None),
        ),
        out_specs=(
            P(("narrow", "wide"), None),
            P(("narrow", "wide"), None),
            P("wide"),
            P("wide"),
            P("wide", None),
            P(None, "wide"),
            P("wide", None),
            P("wide"),
            P("wide"),
            P("wide"),
            P("wide"),
            P("wide", None),
            P("wide"),
            P("wide", None),
            P("wide"),
            P("wide"),
        ),
        check_vma=False,
    )
```

```python
import jax
import jax.numpy as jnp
from jax import lax
from jax.experimental import pallas as pl
from jax.experimental.pallas import tpu as pltpu
from jax.sharding import PartitionSpec as P

D = 768
HEAD_DIM = 64
HEAD_GROUPS = 4
GSLOT = 288
LSLOT = 56
GROUP_IMG = 2
IMG_ROWS = 1024
STREAM = 2048
TOK_DEV = 512


NORM_EPSILON = 1e-06
MASKED = -1e30


def layer_norm(values, gain_row, shift_row):
    row_mean = jnp.mean(values, axis=-1, keepdims=True)
    centered = values - row_mean
    variance = jnp.mean(centered * centered, axis=-1, keepdims=True)
    return centered * lax.rsqrt(variance + NORM_EPSILON) * gain_row + shift_row


def gelu_exact(values):
    return 0.5 * values * (1.0 + jax.scipy.special.erf(values * 0.7071067811865476))


def key_masks(lengths):
    positions = jnp.arange(GSLOT, dtype=jnp.int32)
    global_valid = positions[None, None, :] < lengths[:, :2, None]
    global_valid = global_valid.reshape(GROUP_IMG * 2, 1, 1, GSLOT)
    row_ids = jnp.arange(8 * LSLOT, dtype=jnp.int32)
    crop_ids = row_ids // LSLOT
    offsets = row_ids % LSLOT
    local_lengths = jnp.repeat(lengths[:, 2:], LSLOT, axis=1)
    same_crop = crop_ids[:, None] == crop_ids[None, :]
    local_valid = same_crop[None] & (offsets[None, None, :] < local_lengths[:, None, :])
    return (global_valid, local_valid[:, None])


def split_crops(values):
    global_part = values[:, : 2 * GSLOT].reshape(
        GROUP_IMG * 2, GSLOT, values.shape[2], values.shape[3]
    )
    return (global_part, values[:, 2 * GSLOT :])


def join_crops(global_part, local_part):
    widened = global_part.reshape(GROUP_IMG, 2 * GSLOT, local_part.shape[2], local_part.shape[3])
    return jnp.concatenate([widened, local_part], axis=1)


def unpack_heads(packed):
    per_group = packed.shape[2] // HEAD_DIM
    return [packed[which].reshape(GROUP_IMG, IMG_ROWS, per_group, HEAD_DIM) for which in range(3)]


def tile_logits(queries, key_rows, key_mask, score_scale):
    raw = (
        jnp.einsum("bqhk,bshk->bhqs", queries, key_rows, preferred_element_type=jnp.float32)
        * score_scale
    )
    return jnp.where(key_mask, raw, MASKED)


def forward_tile(queries, key_rows, values, key_mask, score_scale):
    logits = tile_logits(queries, key_rows, key_mask, score_scale)
    row_max = jnp.max(logits, axis=-1, keepdims=True)
    exponent = jnp.exp(logits - row_max)
    row_total = jnp.sum(exponent, axis=-1, keepdims=True)
    weights = (exponent / row_total).astype(jnp.bfloat16)
    result = jnp.einsum("bhqs,bshk->bqhk", weights, values, preferred_element_type=jnp.float32)
    return (result.astype(jnp.bfloat16), row_max + jnp.log(row_total))


def backward_tile(queries, key_rows, values, grad_out, key_mask, logsum, score_scale):
    logits = tile_logits(queries, key_rows, key_mask, score_scale)
    probabilities = jnp.exp(logits - logsum)
    grad_probs = jnp.einsum("bqhk,bshk->bhqs", grad_out, values, preferred_element_type=jnp.float32)
    inner = jnp.sum(probabilities * grad_probs, axis=-1, keepdims=True)
    grad_logits = (probabilities * (grad_probs - inner)).astype(jnp.bfloat16)
    grad_queries = (
        jnp.einsum("bhqs,bshk->bqhk", grad_logits, key_rows, preferred_element_type=jnp.float32)
        * score_scale
    )
    grad_keys = (
        jnp.einsum("bhqs,bqhk->bshk", grad_logits, queries, preferred_element_type=jnp.float32)
        * score_scale
    )
    grad_values = jnp.einsum(
        "bhqs,bqhk->bshk",
        probabilities.astype(jnp.bfloat16),
        grad_out,
        preferred_element_type=jnp.float32,
    )
    return (
        grad_queries.astype(jnp.bfloat16),
        grad_keys.astype(jnp.bfloat16),
        grad_values.astype(jnp.bfloat16),
    )


def attention_forward(packed, masks, score_scale):
    members = [split_crops(member) for member in unpack_heads(packed)]
    results = []
    logsums = []
    for which in range(2):
        result, logsum = forward_tile(
            members[0][which], members[1][which], members[2][which], masks[which], score_scale
        )
        results.append(result)
        logsums.append(logsum)
    return (join_crops(results[0], results[1]).reshape(STREAM, packed.shape[2]), logsums)


def attention_backward(packed, grad_attended, logsums, masks, score_scale):
    members = [split_crops(member) for member in unpack_heads(packed)]
    grad_parts = split_crops(grad_attended.reshape(GROUP_IMG, IMG_ROWS, -1, HEAD_DIM))
    tile_grads = [
        backward_tile(
            members[0][which],
            members[1][which],
            members[2][which],
            grad_parts[which],
            masks[which],
            logsums[which],
            score_scale,
        )
        for which in range(2)
    ]
    joined = [
        join_crops(tile_grads[0][member], tile_grads[1][member]).reshape(STREAM, packed.shape[2])
        for member in range(3)
    ]
    return jnp.stack(joined)


def on_device(
    tokens,
    attn_gain,
    attn_shift,
    in_weight,
    query_value_bias,
    proj_weight,
    proj_bias,
    attn_scale,
    mlp_gain,
    mlp_shift,
    up_weight,
    up_bias,
    down_weight,
    down_bias,
    mlp_scale,
    crop_lengths,
    out_grad,
):
    wide_size = lax.axis_size("wide")
    crop_groups = wide_size // HEAD_GROUPS
    block_rows = TOK_DEV // crop_groups
    head_width = D // HEAD_GROUPS
    score_scale = HEAD_DIM ** (-0.5)
    own_group = lax.axis_index("wide") // HEAD_GROUPS
    own_lengths = lax.dynamic_slice_in_dim(crop_lengths, own_group * GROUP_IMG, GROUP_IMG, 0)
    masks = key_masks(own_lengths)
    inputs = tokens.astype(jnp.float32)
    first_gain = attn_gain.astype(jnp.float32)
    first_shift = attn_shift.astype(jnp.float32)
    normed, first_back = jax.vjp(layer_norm, inputs, first_gain, first_shift)
    normed_low = normed.astype(jnp.bfloat16)
    normed_blocks = normed_low.reshape(crop_groups, block_rows, D)
    weight_in = in_weight.reshape(D, 3, HEAD_GROUPS, head_width)
    qv_rows = query_value_bias.astype(jnp.float32)
    full_bias = jnp.stack([qv_rows[0], jnp.zeros_like(qv_rows[0]), qv_rows[1]]).reshape(
        3, 1, HEAD_GROUPS, 1, head_width
    )
    projected = (
        jnp.einsum("gbd,dchk->cghbk", normed_blocks, weight_in, preferred_element_type=jnp.float32)
        + full_bias
    )
    send_heads = projected.astype(jnp.bfloat16).reshape(3, wide_size, block_rows, head_width)
    arrived = lax.all_to_all(send_heads, "wide", split_axis=1, concat_axis=1, tiled=True)
    packed = arrived.reshape(3, STREAM, head_width)
    attended, logsums = attention_forward(packed, masks, score_scale)
    returned = lax.all_to_all(
        attended.reshape(wide_size, block_rows, head_width),
        "wide",
        split_axis=0,
        concat_axis=0,
        tiled=True,
    )
    mixed_rows = returned.reshape(crop_groups, HEAD_GROUPS, block_rows, head_width)
    weight_proj = proj_weight.reshape(HEAD_GROUPS, head_width, D)
    branch = jnp.einsum(
        "ghbk,hkd->gbd", mixed_rows, weight_proj, preferred_element_type=jnp.float32
    )
    branch = branch.reshape(TOK_DEV, D) + proj_bias.astype(jnp.float32)
    first_scale = attn_scale.astype(jnp.float32)
    middle = inputs + first_scale * branch
    second, second_back = jax.vjp(
        layer_norm, middle, mlp_gain.astype(jnp.float32), mlp_shift.astype(jnp.float32)
    )
    second_low = second.astype(jnp.bfloat16)
    hidden = jnp.dot(second_low, up_weight, preferred_element_type=jnp.float32) + up_bias.astype(
        jnp.float32
    )
    activated, gelu_back = jax.vjp(gelu_exact, hidden)
    activated_low = activated.astype(jnp.bfloat16)
    outcome = jnp.dot(
        activated_low, down_weight, preferred_element_type=jnp.float32
    ) + down_bias.astype(jnp.float32)
    second_scale = mlp_scale.astype(jnp.float32)
    output = (middle + second_scale * outcome).astype(jnp.bfloat16)
    cotangent = out_grad.astype(jnp.float32)
    grad_mlp_scale = jnp.sum(cotangent * outcome, axis=0)
    grad_outcome = (cotangent * second_scale).astype(jnp.bfloat16)
    grad_down_weight = jnp.einsum(
        "tf,td->fd", activated_low, grad_outcome, preferred_element_type=jnp.float32
    )
    grad_down_bias = jnp.sum(grad_outcome.astype(jnp.float32), axis=0)
    grad_activated = jnp.einsum(
        "td,fd->tf", grad_outcome, down_weight, preferred_element_type=jnp.float32
    )
    grad_hidden = gelu_back(grad_activated)[0].astype(jnp.bfloat16)
    grad_up_weight = jnp.einsum(
        "td,tf->df", second_low, grad_hidden, preferred_element_type=jnp.float32
    )
    grad_up_bias = jnp.sum(grad_hidden.astype(jnp.float32), axis=0)
    grad_second = jnp.einsum(
        "tf,df->td", grad_hidden, up_weight, preferred_element_type=jnp.float32
    )
    grad_middle, grad_mlp_gain, grad_mlp_shift = second_back(grad_second)
    grad_middle = grad_middle + cotangent
    grad_attn_scale = jnp.sum(grad_middle * branch, axis=0)
    grad_branch = (grad_middle * first_scale).astype(jnp.bfloat16)
    branch_blocks = grad_branch.reshape(crop_groups, block_rows, D)
    grad_proj_weight = jnp.einsum(
        "ghbk,gbd->hkd", mixed_rows, branch_blocks, preferred_element_type=jnp.float32
    ).reshape(D, D)
    grad_proj_bias = jnp.sum(grad_branch.astype(jnp.float32), axis=0)
    grad_mixed = jnp.einsum(
        "gbd,hkd->ghbk", branch_blocks, weight_proj, preferred_element_type=jnp.float32
    )
    grad_mixed = grad_mixed.astype(jnp.bfloat16).reshape(wide_size, block_rows, head_width)
    again, grad_arrived = (
        lax.all_to_all(send_heads, "wide", split_axis=1, concat_axis=1, tiled=True),
        lax.all_to_all(grad_mixed[None], "wide", split_axis=1, concat_axis=1, tiled=True),
    )
    packed_back = again.reshape(3, STREAM, head_width)
    grad_attended = grad_arrived.reshape(STREAM, head_width)
    grad_packed = attention_backward(packed_back, grad_attended, logsums, masks, score_scale)
    grad_sent = lax.all_to_all(
        grad_packed.reshape(3, wide_size, block_rows, head_width),
        "wide",
        split_axis=1,
        concat_axis=1,
        tiled=True,
    )
    grad_heads = grad_sent.reshape(3, crop_groups, HEAD_GROUPS, block_rows, head_width)
    grad_in_weight = jnp.einsum(
        "gbd,cghbk->dchk", normed_blocks, grad_heads, preferred_element_type=jnp.float32
    ).reshape(D, 3 * D)
    bias_sums = jnp.sum(grad_heads.astype(jnp.float32), axis=(1, 3)).reshape(3, D)
    grad_query_value_bias = jnp.stack([bias_sums[0], bias_sums[2]])
    grad_normed = jnp.einsum(
        "cghbk,dchk->gbd", grad_heads, weight_in, preferred_element_type=jnp.float32
    ).reshape(TOK_DEV, D)
    grad_inputs, grad_attn_gain, grad_attn_shift = first_back(grad_normed)
    input_grad = (grad_inputs + grad_middle).astype(jnp.bfloat16)
    shares = (
        lax.psum_scatter(
            grad_attn_gain.astype(jnp.bfloat16), "wide", scatter_dimension=0, tiled=True
        ).astype(jnp.float32),
        lax.psum_scatter(
            grad_attn_shift.astype(jnp.bfloat16), "wide", scatter_dimension=0, tiled=True
        ).astype(jnp.float32),
        lax.psum_scatter(
            grad_in_weight.astype(jnp.bfloat16), "wide", scatter_dimension=0, tiled=True
        ).astype(jnp.float32),
        lax.psum_scatter(
            grad_query_value_bias.astype(jnp.bfloat16), "wide", scatter_dimension=1, tiled=True
        ).astype(jnp.float32),
        lax.psum_scatter(
            grad_proj_weight.astype(jnp.bfloat16), "wide", scatter_dimension=0, tiled=True
        ).astype(jnp.float32),
        lax.psum_scatter(
            grad_proj_bias.astype(jnp.bfloat16), "wide", scatter_dimension=0, tiled=True
        ).astype(jnp.float32),
        lax.psum_scatter(
            grad_attn_scale.astype(jnp.bfloat16), "wide", scatter_dimension=0, tiled=True
        ).astype(jnp.float32),
        lax.psum_scatter(
            grad_mlp_gain.astype(jnp.bfloat16), "wide", scatter_dimension=0, tiled=True
        ).astype(jnp.float32),
        lax.psum_scatter(
            grad_mlp_shift.astype(jnp.bfloat16), "wide", scatter_dimension=0, tiled=True
        ).astype(jnp.float32),
        lax.psum_scatter(
            grad_up_weight.astype(jnp.bfloat16), "wide", scatter_dimension=0, tiled=True
        ).astype(jnp.float32),
        lax.psum_scatter(
            grad_up_bias.astype(jnp.bfloat16), "wide", scatter_dimension=0, tiled=True
        ).astype(jnp.float32),
        lax.psum_scatter(
            grad_down_weight.astype(jnp.bfloat16), "wide", scatter_dimension=0, tiled=True
        ).astype(jnp.float32),
        lax.psum_scatter(
            grad_down_bias.astype(jnp.bfloat16), "wide", scatter_dimension=0, tiled=True
        ).astype(jnp.float32),
        lax.psum_scatter(
            grad_mlp_scale.astype(jnp.bfloat16), "wide", scatter_dimension=0, tiled=True
        ).astype(jnp.float32),
    )
    results = (
        lax.psum(shares[0].astype(jnp.bfloat16), "narrow").astype(jnp.float32),
        lax.psum(shares[1].astype(jnp.bfloat16), "narrow").astype(jnp.float32),
        lax.psum(shares[2].astype(jnp.bfloat16), "narrow").astype(jnp.float32),
        lax.psum(shares[3].astype(jnp.bfloat16), "narrow").astype(jnp.float32),
        lax.psum(shares[4].astype(jnp.bfloat16), "narrow").astype(jnp.float32),
        lax.psum(shares[5].astype(jnp.bfloat16), "narrow").astype(jnp.float32),
        lax.psum(shares[6].astype(jnp.bfloat16), "narrow").astype(jnp.float32),
        lax.psum(shares[7].astype(jnp.bfloat16), "narrow").astype(jnp.float32),
        lax.psum(shares[8].astype(jnp.bfloat16), "narrow").astype(jnp.float32),
        lax.psum(shares[9].astype(jnp.bfloat16), "narrow").astype(jnp.float32),
        lax.psum(shares[10].astype(jnp.bfloat16), "narrow").astype(jnp.float32),
        lax.psum(shares[11].astype(jnp.bfloat16), "narrow").astype(jnp.float32),
        lax.psum(shares[12].astype(jnp.bfloat16), "narrow").astype(jnp.float32),
        lax.psum(shares[13].astype(jnp.bfloat16), "narrow").astype(jnp.float32),
    )
    return (
        output,
        input_grad,
        results[0],
        results[1],
        results[2],
        results[3],
        results[4],
        results[5],
        results[6],
        results[7],
        results[8],
        results[9],
        results[10],
        results[11],
        results[12],
        results[13],
    )


MESH = pl.DeviceIdType.MESH
F32 = jnp.float32
BF16 = jnp.bfloat16
SLOT = 288
ROWS = 576
UNITS = 18
PAIRS = 9
BLOCK = 48
BLOCKS = ROWS // BLOCK
ATTN_GAIN, ATTN_SHIFT, Q_BIAS, V_BIAS, PROJ_BIAS, ATTN_SCALE, MLP_GAIN, MLP_SHIFT, DOWN_BIAS, MLP_SCALE = range(10)
UP_BIAS = 10


def dot_nn(a, b):
    return jnp.dot(a, b, preferred_element_type=F32)


def dot_nt(a, b):
    return lax.dot_general(a, b, (((1,), (1,)), ((), ())), preferred_element_type=F32)


def dot_tn(a, b):
    return lax.dot_general(a, b, (((0,), (0,)), ((), ())), preferred_element_type=F32)


def halves(block):
    lanes = lax.broadcasted_iota(jnp.int32, block.shape, 1)
    zero = jnp.zeros_like(block)
    return [jnp.where((lanes < 64) == (h == 0), block, zero) for h in range(2)]


def fold_rows(values):
    return jnp.sum(values.reshape(values.shape[0] // 8, 8, values.shape[1]), axis=0)


def norm_parts(values):
    mean = jnp.sum(values, axis=-1, keepdims=True) * (1.0 / D)
    centered = values - mean
    variance = jnp.sum(centered * centered, axis=-1, keepdims=True) * (1.0 / D)
    rstd = lax.rsqrt(variance + NORM_EPSILON)
    return centered * rstd, rstd


def layer_kernel(
    tok_ref, og_ref, len_ref,
    attn_gain_ref, attn_shift_ref, qv_ref, proj_bias_ref, attn_scale_ref, mlp_gain_ref, mlp_shift_ref,
    up_bias_ref, down_bias_ref, mlp_scale_ref,
    in_hbm, proj_hbm, up_hbm, down_hbm,
    out_hbm, ig_hbm, gin_ref, gproj_ref, gup_ref, gdown_ref, vout_ref,
    win, wproj, wup, wdown,
    xb, db, ob, h1, t1, t2, qkv, att, branch, mid, h2, dm, gact, dhid, macc, dacc, ub, gb, bias, bias_t,
    prm, sums, usums,
    gbuf, r0, r1, r2, r3, r4, fin, wdt, vbuf, vrecv,
    wsem, upsem, lsem, hsend, hrecv, ssem, rsem, vssem, vrsem,
):
    n = lax.axis_index("narrow")
    w = lax.axis_index("wide")
    c = n % 2
    y = n // 2
    x = w % 2
    z1 = (w // 2) % 2
    z2 = w // 4
    quarter = w % 4
    shift = 32 * (quarter % 2) + 32 * (quarter // 2) * (2 - 2 * (quarter % 2)) + 0 * quarter
    partner = {
        "core": (n + 1 - 2 * c, w),
        "y": (n + 2 - 4 * y, w),
        "x": (n, w + 1 - 2 * x),
        "z1": (n, w + 2 - 4 * z1),
        "z2": (n, w + 4 - 8 * z2),
        "diagonal": (n, w + 3 - 2 * quarter),
    }

    weights = [
        pltpu.make_async_copy(in_hbm, win, wsem.at[0]),
        pltpu.make_async_copy(proj_hbm, wproj, wsem.at[1]),
    ]
    downs = [pltpu.make_async_copy(down_hbm.at[:, j], wdown.at[j], wsem.at[2 + j]) for j in range(3)]
    ups = [
        [
            pltpu.make_async_copy(
                up_hbm.at[:, 128 * (3 * s + j) : 128 * (3 * s + j + 1)],
                wup.at[:, 128 * (8 * j + s) : 128 * (8 * j + s + 1)],
                upsem.at[j, s],
            )
            for s in range(8)
        ]
        for j in range(3)
    ]
    own = pl.ds(pl.multiple_of(64 - shift, 32), 256)
    loads = [
        pltpu.make_async_copy(tok_ref, xb.at[:, own], lsem.at[0]),
        pltpu.make_async_copy(og_ref, db.at[:, own], lsem.at[1]),
    ]
    loads[0].start()
    weights[0].start()
    loads[1].start()
    weights[1].start()
    for j in range(3):
        for s in range(8):
            ups[j][s].start()
        downs[j].start()

    barrier = pltpu.get_barrier_semaphore()
    for target in partner.values():
        pl.semaphore_signal(barrier, inc=1, device_id=target, device_id_type=MESH)
    pl.semaphore_wait(barrier, 6)

    before_shift = 32 * ((quarter + 3) % 2) + 32 * ((quarter - 1) // 2) * (2 - 2 * ((quarter + 3) % 2))
    before = (n, w - 1)
    after = (n, w + 1)

    def halo_in(src, dst, k):
        return pltpu.make_async_remote_copy(
            src_ref=src.at[:, 0:64],
            dst_ref=dst.at[:, pl.ds(pl.multiple_of(320 - before_shift, 32), 64)],
            send_sem=hsend.at[k], recv_sem=hrecv.at[k], device_id=before, device_id_type=MESH,
        )

    def halo_back(buf, k, size):
        return pltpu.make_async_remote_copy(
            src_ref=buf.at[:, pl.ds(pl.multiple_of(320 - shift, 32), size)],
            dst_ref=buf.at[:, 64 - size : 64],
            send_sem=hsend.at[k], recv_sem=hrecv.at[k], device_id=after, device_id_type=MESH,
        )

    @pl.when(quarter > 0)
    def _():
        halo_in(tok_ref, xb, 0).start()
        halo_in(og_ref, db, 1).start()

    for row, ref in (
        (ATTN_GAIN, attn_gain_ref), (ATTN_SHIFT, attn_shift_ref), (PROJ_BIAS, proj_bias_ref), (ATTN_SCALE, attn_scale_ref),
        (MLP_GAIN, mlp_gain_ref), (MLP_SHIFT, mlp_shift_ref), (DOWN_BIAS, down_bias_ref), (MLP_SCALE, mlp_scale_ref),
    ):
        prm[row : row + 1, 0:D] = ref[...].astype(F32).reshape(1, D)
    qv = qv_ref[...].astype(F32)
    prm[Q_BIAS : Q_BIAS + 1, 0:D] = qv[0:1]
    prm[V_BIAS : V_BIAS + 1, 0:D] = qv[1:2]
    up_row = up_bias_ref[...].astype(F32).reshape(1, 4 * D)
    for j in range(3):
        for s in range(8):
            prm[UP_BIAS + j : UP_BIAS + j + 1, 128 * s : 128 * (s + 1)] = up_row[:, 128 * (3 * s + j) : 128 * (3 * s + j + 1)]
    sums[...] = jnp.zeros_like(sums)
    usums[...] = jnp.zeros_like(usums)

    def param(row):
        return prm[row : row + 1, 0:D]

    is_local = quarter // 2
    for i in range(2):
        image = 2 * i + z2

        def crop_of(axis, valid_only):
            shape = (1, SLOT) if axis == 1 else (SLOT, 1)
            place = lax.broadcasted_iota(jnp.int32, shape, axis)
            ids = jnp.full(shape, -1 if valid_only else 4, jnp.int32)
            for m in range(4):
                start = 56 * m * is_local
                if valid_only:
                    local_length = len_ref[image, 2 + 4 * (quarter % 2) + m]
                    global_length = len_ref[image, quarter % 2] if m == 0 else 0
                    size = is_local * local_length + (1 - is_local) * global_length
                else:
                    size = 56 * is_local + (1 - is_local) * (SLOT if m == 0 else 0)
                inside = jnp.logical_and(place >= start, place < start + size)
                ids = jnp.where(inside, m, ids)
            return ids

        bias[i] = jnp.where(crop_of(0, False) == crop_of(1, True), 0.0, MASKED)
        bias_t[i] = jnp.where(crop_of(1, False) == crop_of(0, True), 0.0, MASKED)

    def take_halo(src, dst, k):
        @pl.when(quarter > 0)
        def _():
            halo_in(src, dst, k).wait_send()

        @pl.when(quarter < 3)
        def _():
            halo_in(src, dst, k).wait_recv()

        @pl.when(quarter > 1)
        def _():
            dst[:, 288:352] = jnp.zeros((2, 64, D), BF16)

    def at(b):
        i, k = b // 6, b % 6
        return i, pl.ds(pl.multiple_of(64 + BLOCK * k, 16), BLOCK), pl.ds(pl.multiple_of(BLOCK * b, 16), BLOCK)

    def first_norm(b):
        i, slots, rows = at(b)
        normed, _ = norm_parts(xb[i, slots].astype(F32))
        h1[rows] = (normed * param(ATTN_GAIN) + param(ATTN_SHIFT)).astype(BF16)

    def project(low, high):
        rows = jnp.concatenate([h1[SLOT * i + low : SLOT * i + high] for i in range(2)], axis=0)
        for tile in range(9):
            cols = slice(256 * tile, 256 * (tile + 1))
            result = dot_nn(rows, win[:, cols])
            if tile < 3:
                result = (result + prm[Q_BIAS : Q_BIAS + 1, cols]).astype(BF16) * jnp.asarray(0.125, BF16)
            elif tile >= 6:
                result = result + prm[V_BIAS : V_BIAS + 1, 256 * (tile - 6) : 256 * (tile - 5)]
            result = result.astype(BF16)
            for i in range(2):
                qkv[SLOT * i + low : SLOT * i + high, cols] = result[(high - low) * i : (high - low) * (i + 1)]

    loads[0].wait()
    for b in (0, 1, 2, 3, 6, 7, 8, 9):
        first_norm(b)
    weights[0].wait()
    project(0, 192)
    take_halo(tok_ref, xb, 0)
    for b in (4, 5, 10, 11):
        first_norm(b)
    project(192, SLOT)

    def pair_at(index):
        i, h = index % 2, index // 2
        rows = pl.ds(pl.multiple_of(SLOT * i, 16), SLOT)
        return i, rows, [pl.ds(pl.multiple_of(D * m + 128 * h, 128), 128) for m in range(3)]

    def attend(index, _):
        i, rows, cols = pair_at(index)
        q, v = qkv[rows, cols[0]], qkv[rows, cols[2]]
        keys = halves(qkv[rows, cols[1]])
        lanes = lax.broadcasted_iota(jnp.int32, (SLOT, 128), 1)
        ones = jnp.ones_like(v)
        parts = []
        for h in range(2):
            s = dot_nt(q, keys[h]) + bias[i]
            e = jnp.exp(s - jnp.max(s, axis=-1, keepdims=True)).astype(BF16)
            part = dot_nn(e, jnp.where((lanes < 64) == (h == 0), v, ones))
            parts.append(part / pltpu.roll(part, 64, 1))
        att[rows, cols[0]] = jnp.where(lanes < 64, parts[0], parts[1]).astype(BF16)
        return 0

    lax.fori_loop(0, 12, attend, 0)

    weights[1].wait()
    for tile in range(3):
        cols = slice(256 * tile, 256 * (tile + 1))
        result = dot_nn(att[...], wproj[:, cols]) + prm[PROJ_BIAS : PROJ_BIAS + 1, cols]
        branch[:, cols] = result.astype(BF16)
        scaled = prm[ATTN_SCALE : ATTN_SCALE + 1, cols] * result
        for i in range(2):
            mid[SLOT * i : SLOT * (i + 1), cols] = (
                xb[i, 64 : 64 + SLOT, cols].astype(F32) + scaled[SLOT * i : SLOT * (i + 1)]
            )

    loads[1].wait()
    take_halo(og_ref, db, 1)

    def second_norm(b, _):
        i, slots, rows = at(b)
        low = (db[i, slots].astype(F32) * param(MLP_SCALE)).astype(BF16)
        dm[rows] = low
        sums[DOWN_BIAS] += fold_rows(low.astype(F32))
        normed, _ = norm_parts(mid[rows])
        h2[rows] = (normed * param(MLP_GAIN) + param(MLP_SHIFT)).astype(BF16)
        return 0

    lax.fori_loop(0, BLOCKS, second_norm, 0)

    def transpose_into(dst, src):
        for k in range(6):
            dst[128 * k : 128 * (k + 1)] = src[:, 128 * k : 128 * (k + 1)].T

    def copy(src, dst, unit, stage, axis):
        return pltpu.make_async_remote_copy(
            src_ref=src, dst_ref=dst, send_sem=ssem.at[unit, stage], recv_sem=rsem.at[unit, stage],
            device_id=partner[axis], device_id_type=MESH,
        )

    def even(u, k):
        if k == 0:
            return copy(gbuf.at[u, 1 - c], r0.at[u % r0.shape[0]], u, 0, "core")
        if k == 1:
            return copy(gbuf.at[u, c, :, 1 - x], r1.at[u % r1.shape[0]], u, 1, "x")
        if k == 2:
            return copy(gbuf.at[u, c, :, x, 1 - z1], r2.at[u % r2.shape[0]], u, 2, "z1")
        if k == 3:
            return copy(gbuf.at[u, c, :, x, z1, 1 - z2], r3.at[u % r3.shape[0]], u, 3, "z2")
        if k == 4:
            return copy(gbuf.at[u, c, :, x, z1, z2], r4.at[u % r4.shape[0]], u, 4, "y")
        return copy(fin.at[u % 12, c], fin.at[u % 12, c], u, 5, "core")

    def odd(u, k):
        if k == 0:
            return copy(gbuf.at[u, 1 - c], r0.at[u % r0.shape[0]], u, 0, "core")
        if k == 1:
            return copy(gbuf.at[u, c, 1 - y], r1.at[u % r1.shape[0]], u, 1, "y")
        if k == 2:
            return copy(gbuf.at[u, c, y, 1 - x], r2.at[u % r2.shape[0]], u, 2, "x")
        if k == 3:
            return copy(gbuf.at[u, c, y, x, 1 - z1], r3.at[u % r3.shape[0]], u, 3, "z1")
        if k == 4:
            return copy(gbuf.at[u, c, y, x, z1, 1 - z2], r4.at[u % r4.shape[0], 0], u, 4, "z2")
        if k == 5:
            return copy(fin.at[u % 12, c, y], fin.at[u % 12, c, y], u, 5, "y")
        return copy(fin.at[u % 12, c], fin.at[u % 12, c], u, 6, "core")

    def add(dst, src):
        dst[...] = (dst[...].astype(F32) + src[...].astype(F32)).astype(BF16)

    def land_core(u):
        def body(index, _):
            yy, xx = index // 2, index % 2
            add(gbuf.at[u, c, yy, xx], r0.at[u % r0.shape[0], yy, xx])
            return 0

        lax.fori_loop(0, 4, body, 0)

    def even_land(u, k):
        if k == 0:
            land_core(u)
        elif k == 1:
            for yy in range(2):
                add(gbuf.at[u, c, yy, x], r1.at[u % r1.shape[0], yy])
        elif k == 2:
            add(gbuf.at[u, c, :, x, z1], r2.at[u % r2.shape[0]])
        elif k == 3:
            add(gbuf.at[u, c, :, x, z1, z2], r3.at[u % r3.shape[0]])
        elif k == 4:
            total = gbuf[u, c, :, x, z1, z2].astype(F32) + r4[u % r4.shape[0]].astype(F32)
            fin[u % 12, c] = total.astype(BF16)

    def odd_land(u, k):
        if k == 0:
            land_core(u)
        elif k == 1:
            for xx in range(2):
                add(gbuf.at[u, c, y, xx], r1.at[u % r1.shape[0], xx])
        elif k == 2:
            add(gbuf.at[u, c, y, x], r2.at[u % r2.shape[0]])
        elif k == 3:
            add(gbuf.at[u, c, y, x, z1], r3.at[u % r3.shape[0]])
        elif k == 4:
            total = gbuf[u, c, y, x, z1, z2].astype(F32) + r4[u % r4.shape[0], 0].astype(F32)
            fin[u % 12, c, y] = total.astype(BF16)

    def in_tile(index):
        return 3 * ((index - 3) % 3) + (index - 3) // 3

    def write_out(p, a):
        u = 2 * p + a
        is_mlp = p < 6

        @pl.when(jnp.logical_and(is_mlp, p % 2 == 0))
        def _():
            for sub in range(4):
                wdt[384 * a + 96 * sub : 384 * a + 96 * (sub + 1), pl.ds(pl.multiple_of(128 * (p // 2), 128), 128)] = fin[
                    u % 12, sub // 2, sub % 2
                ]

        @pl.when(jnp.logical_and(is_mlp, p % 2 == 1))
        def _():
            for sub in range(4):
                tile = 3 * (4 * a + sub) + p // 2
                gup_ref[:, pl.ds(pl.multiple_of(128 * tile, 128), 128)] = fin[u % 12, sub // 2, sub % 2]

        @pl.when(p >= 6)
        def _():
            for cc in range(2):
                index = 4 * (p - 6) + 2 * a + cc

                def put_tile(dst, tile):
                    for yy in range(2):
                        dst[:, pl.ds(pl.multiple_of(256 * tile + 128 * yy, 128), 128)] = fin[u % 12, cc, yy]

                @pl.when(index < 3)
                def _():
                    put_tile(gproj_ref, index)

                @pl.when(index >= 3)
                def _():
                    put_tile(gin_ref, in_tile(index))

    def event(p, k):
        u = 2 * p
        if k < 6:
            even(u, k).wait()
            even_land(u, k)
            if k < 5:
                even(u, k + 1).start()
            else:
                write_out(p, 0)
        odd(u + 1, k).wait()
        odd_land(u + 1, k)
        if k < 6:
            odd(u + 1, k + 1).start()
        else:
            write_out(p, 1)

    def guarded(p, k):
        if isinstance(p, int):
            if 0 <= p < PAIRS:
                event(p, k)
            return

        @pl.when(jnp.logical_and(p >= 0, p < PAIRS))
        def _():
            event(p, k)

    def send(p):
        even(2 * p, 0).start()
        even(2 * p + 1, 0).start()

    def back(b):
        for k in range(1, 7):
            guarded(b + 1 - k, k)

    transpose_into(t1, dm)
    transpose_into(t2, h2)

    def gelu_block(j, tile, b):
        _, _, rows = at(b)
        cols = pl.ds(pl.multiple_of(256 * tile, 256), 256)
        u = ub[rows] + prm[pl.ds(UP_BIAS + j, 1), cols]
        phi = 0.5 * (1.0 + lax.erf(u * 0.7071067811865476))
        gact[rows, cols] = (u * phi).astype(BF16)
        slope = phi + u * (jnp.exp(u * u * -0.5) * 0.3989422804014327)
        low = (gb[rows] * slope).astype(BF16)
        dhid[rows, cols] = low
        usums[:, pl.ds(pl.multiple_of(1024 * j + 256 * tile, 256), 256)] += fold_rows(low.astype(F32))

    def mlp(j, _):
        def wait_weights(jj):
            for s in range(8):
                ups[jj][s].wait()
            downs[jj].wait()

        for jj in range(3):

            @pl.when(j == jj)
            def _(jj=jj):
                wait_weights(jj)

        def hidden_tile(tile, _):
            cols = pl.ds(pl.multiple_of(1024 * j + 256 * tile, 256), 256)
            ub[...] = dot_nn(h2[...], wup[:, cols])
            down = wdown[j, pl.ds(2 * tile, 2)].reshape(256, D)
            gb[...] = dot_nt(dm[...], down)

            def block(b, _):
                gelu_block(j, tile, b)
                return 0

            lax.fori_loop(0, BLOCKS, block, 0)
            return 0

        lax.fori_loop(0, 4, hidden_tile, 0)
        back(2 * j - 2)

        def down_grad(nt, _):
            result = dot_nn(t1[...], gact[:, pl.ds(pl.multiple_of(256 * nt, 256), 256)])
            for ss in range(2):
                for sub in range(8):
                    gbuf[4 * j + sub // 4, (sub // 2) % 2, sub % 2, ss, nt % 2, nt // 2] = result[
                        96 * sub : 96 * (sub + 1), 128 * ss : 128 * (ss + 1)
                    ].astype(BF16)
            return 0

        lax.fori_loop(0, 4, down_grad, 0)
        send(2 * j)

        def up_grad(nt, _):
            result = dot_nn(t2[...], dhid[:, pl.ds(pl.multiple_of(256 * nt, 256), 256)])
            for s in range(8):
                for yy in range(2):
                    gbuf[4 * j + 2 + nt // 2, nt % 2, yy, s % 2, (s // 2) % 2, s // 4] = result[
                        96 * s : 96 * (s + 1), 128 * yy : 128 * (yy + 1)
                    ].astype(BF16)
            return 0

        lax.fori_loop(0, 4, up_grad, 0)
        send(2 * j + 1)
        event(2 * j, 0)

        def combine(nt, _):
            cols = pl.ds(pl.multiple_of(256 * nt, 256), 256)
            up_rows = wup[cols, pl.ds(pl.multiple_of(1024 * j, 1024), 1024)]
            more = dot_nn(gact[...], wdown[j, :, :, cols].reshape(1024, 256))
            more_d = dot_nt(dhid[...], up_rows)

            @pl.when(j == 0)
            def _():
                macc[:, cols] = more
                dacc[:, cols] = more_d

            @pl.when(j > 0)
            def _():
                macc[:, cols] += more
                dacc[:, cols] += more_d

            return 0

        lax.fori_loop(0, 3, combine, 0)
        event(2 * j + 1, 0)
        back(2 * j - 1)
        return 0

    lax.fori_loop(0, 3, mlp, 0)

    transpose_into(t1, h1)
    transpose_into(t2, att)

    def second_back(b, _):
        i, slots, rows = at(b)
        grad = db[i, slots].astype(F32)
        y_rows = mid[rows]
        outcome = macc[rows] + param(DOWN_BIAS)
        ob[i, slots] = (y_rows + param(MLP_SCALE) * outcome).astype(BF16)
        sums[MLP_SCALE] += fold_rows(grad * outcome)
        normed, rstd = norm_parts(y_rows)
        dh = dacc[rows]
        sums[MLP_GAIN] += fold_rows(dh * normed)
        sums[MLP_SHIFT] += fold_rows(dh)
        e = dh * param(MLP_GAIN)
        mean_e = jnp.sum(e, axis=-1, keepdims=True) * (1.0 / D)
        mean_en = jnp.sum(e * normed, axis=-1, keepdims=True) * (1.0 / D)
        dy = grad + rstd * (e - mean_e - normed * mean_en)
        dacc[rows] = dy
        sums[ATTN_SCALE] += fold_rows(dy * branch[rows].astype(F32))
        low = (dy * param(ATTN_SCALE)).astype(BF16)
        dm[rows] = low
        sums[PROJ_BIAS] += fold_rows(low.astype(F32))
        return 0

    lax.fori_loop(0, BLOCKS, second_back, 0)

    def give_back(buf, k):
        @pl.when(quarter % 2 == 0)
        def _():
            halo_back(buf, k, 32).start()

        @pl.when(quarter == 1)
        def _():
            halo_back(buf, k, 64).start()

    def take_back(buf, k):
        @pl.when(quarter % 2 == 0)
        def _():
            halo_back(buf, k, 32).wait_send()

        @pl.when(quarter == 1)
        def _():
            halo_back(buf, k, 64).wait_send()

        @pl.when(quarter % 2 == 1)
        def _():
            halo_back(buf, k, 32).wait_recv()

        @pl.when(quarter == 2)
        def _():
            halo_back(buf, k, 64).wait_recv()

    give_back(ob, 2)
    back(4)

    for tile in range(3):
        cols = slice(256 * tile, 256 * (tile + 1))
        h2[:, cols] = dot_nt(dm[...], wproj[cols]).astype(BF16)

    def attend_back(index, _):
        i, rows, cols = pair_at(index)
        k, v = qkv[rows, cols[1]], qkv[rows, cols[2]]
        queries, keys, grads = halves(qkv[rows, cols[0]]), halves(k), halves(h2[rows, cols[0]])
        dq = dk = dv = None
        for h in range(2):
            s = dot_nt(k, queries[h]) + bias_t[i]
            e = jnp.exp(s - jnp.max(s, axis=0, keepdims=True))
            p = e * (1.0 / jnp.sum(e, axis=0, keepdims=True))
            dp = dot_nt(v, grads[h])
            ds = (p * (dp - jnp.sum(p * dp, axis=0, keepdims=True))).astype(BF16)
            parts = dot_tn(ds, keys[h]), dot_nn(ds, queries[h]), dot_nn(p.astype(BF16), grads[h])
            dq, dk, dv = parts if dq is None else (dq + parts[0], dk + parts[1], dv + parts[2])
        low_q, low_v = (dq * 0.125).astype(BF16), dv.astype(BF16)
        qkv[rows, cols[0]] = low_q
        qkv[rows, cols[1]] = dk.astype(BF16)
        qkv[rows, cols[2]] = low_v
        sums[Q_BIAS, :, cols[0]] += fold_rows(low_q.astype(F32))
        sums[V_BIAS, :, cols[0]] += fold_rows(low_v.astype(F32))
        return 0

    def attn_grad(index, _):
        m, nt = index // 4, index % 4

        def put(result):
            for s in range(8):
                for yy in range(2):
                    gbuf[12 + 2 * m + nt // 2, nt % 2, yy, s % 2, (s // 2) % 2, s // 4] = result[
                        96 * s : 96 * (s + 1), 128 * yy : 128 * (yy + 1)
                    ].astype(BF16)

        @pl.when(index < 3)
        def _():
            put(dot_nn(t2[...], dm[:, pl.ds(pl.multiple_of(256 * index, 256), 256)]))

        @pl.when(index >= 3)
        def _():
            put(dot_nn(t1[...], qkv[:, pl.ds(pl.multiple_of(256 * in_tile(index), 256), 256)]))

        return 0

    lax.fori_loop(0, 4, attend_back, 0)
    lax.fori_loop(0, 4, attn_grad, 0)
    send(6)
    back(5)
    lax.fori_loop(4, 8, attend_back, 0)
    event(6, 0)
    lax.fori_loop(4, 8, attn_grad, 0)
    send(7)
    lax.fori_loop(8, 12, attend_back, 0)
    event(7, 0)
    back(6)
    lax.fori_loop(8, 12, attn_grad, 0)
    send(8)

    for tile in range(3):
        cols = slice(256 * tile, 256 * (tile + 1))
        macc[:, cols] = dot_nt(qkv[...], win[cols])

    def first_back(b, _):
        i, slots, rows = at(b)
        normed, rstd = norm_parts(xb[i, slots].astype(F32))
        dh = macc[rows]
        sums[ATTN_GAIN] += fold_rows(dh * normed)
        sums[ATTN_SHIFT] += fold_rows(dh)
        e = dh * param(ATTN_GAIN)
        mean_e = jnp.sum(e, axis=-1, keepdims=True) * (1.0 / D)
        mean_en = jnp.sum(e * normed, axis=-1, keepdims=True) * (1.0 / D)
        db[i, slots] = (dacc[rows] + rstd * (e - mean_e - normed * mean_en)).astype(BF16)
        return 0

    lax.fori_loop(0, BLOCKS, first_back, 0)
    give_back(db, 3)
    event(8, 0)
    back(7)

    vaxes = ("core", "x", "y", "z1", "z2")

    def vcopy(k):
        return pltpu.make_async_remote_copy(
            src_ref=vbuf.at[k], dst_ref=vrecv.at[k], send_sem=vssem.at[k], recv_sem=vrsem.at[k],
            device_id=partner[vaxes[k]], device_id_type=MESH,
        )

    def vland(k):
        vcopy(k).wait()
        vbuf[k + 1] = vbuf[k] + vrecv[k]
        if k < 4:
            vcopy(k + 1).start()

    vbuf[0] = jnp.zeros_like(vbuf[0])
    for row in range(10):
        vbuf[0, row : row + 1, 0:D] = jnp.sum(sums[row], axis=0, keepdims=True)
    for j in range(3):
        vbuf[0, UP_BIAS + j : UP_BIAS + j + 1] = jnp.sum(usums[:, 1024 * j : 1024 * (j + 1)], axis=0, keepdims=True)
    vcopy(0).start()

    def drain(b, _):
        back(b)
        for k in range(5):

            @pl.when(b == 8 + k)
            def _(k=k):
                vland(k)

        return 0

    lax.fori_loop(8, PAIRS + 5, drain, 0)

    rolled = pltpu.roll(vbuf[5, :, 0:D], (D - 96 * w) % D, 1)
    vout_ref[...] = rolled[:, 0:128]
    vout_ref[UP_BIAS : UP_BIAS + 3] = vbuf[5, UP_BIAS : UP_BIAS + 3, pl.ds(pl.multiple_of(128 * w, 128), 128)]

    for a in range(3):
        for b in range(6):
            gdown_ref[128 * a : 128 * (a + 1), 128 * b : 128 * (b + 1)] = wdt[
                128 * b : 128 * (b + 1), 128 * a : 128 * (a + 1)
            ].T

    take_back(ob, 2)
    take_back(db, 3)
    stores = [
        pltpu.make_async_copy(ob.at[:, own], out_hbm, lsem.at[0]),
        pltpu.make_async_copy(db.at[:, own], ig_hbm, lsem.at[1]),
    ]
    for store in stores:
        store.start()
    for store in stores:
        store.wait()


def layer(tokens, out_grad, lengths, vectors, weights):
    vm = pl.BlockSpec(memory_space=pltpu.VMEM)
    hbm = pl.BlockSpec(memory_space=pl.ANY)
    dma = pltpu.SemaphoreType.DMA
    slots = pltpu.VMEM((2, 384, D), BF16)
    square = pltpu.VMEM((ROWS, D), BF16)
    wide_square = pltpu.VMEM((ROWS, D), F32)
    block = (96, 128)
    return pl.pallas_call(
        layer_kernel,
        out_shape=(
            jax.ShapeDtypeStruct((2, 256, D), BF16),
            jax.ShapeDtypeStruct((2, 256, D), BF16),
            jax.ShapeDtypeStruct((96, 3 * D), BF16),
            jax.ShapeDtypeStruct((96, D), BF16),
            jax.ShapeDtypeStruct((96, 4 * D), BF16),
            jax.ShapeDtypeStruct((384, D), BF16),
            jax.ShapeDtypeStruct((16, 128), F32),
        ),
        in_specs=[hbm, hbm, pl.BlockSpec(memory_space=pltpu.SMEM)] + [vm] * 10 + [hbm] * 4,
        out_specs=(hbm, hbm, vm, vm, vm, vm, vm),
        scratch_shapes=[
            pltpu.VMEM((D, 3 * D), BF16),
            pltpu.VMEM((D, D), BF16),
            pltpu.VMEM((D, 4 * D), BF16),
            pltpu.VMEM((3, 8, 128, D), BF16),
            slots, slots, slots,
            square,
            pltpu.VMEM((D, ROWS), BF16),
            pltpu.VMEM((D, ROWS), BF16),
            pltpu.VMEM((ROWS, 3 * D), BF16),
            square, square,
            wide_square,
            square, square,
            pltpu.VMEM((ROWS, 1024), BF16),
            pltpu.VMEM((ROWS, 1024), BF16),
            wide_square, wide_square,
            pltpu.VMEM((ROWS, 256), F32),
            pltpu.VMEM((ROWS, 256), F32),
            pltpu.VMEM((2, SLOT, SLOT), F32),
            pltpu.VMEM((2, SLOT, SLOT), F32),
            pltpu.VMEM((16, 1024), F32),
            pltpu.VMEM((10, 8, D), F32),
            pltpu.VMEM((8, 4 * D), F32),
            pltpu.VMEM((UNITS, 2, 2, 2, 2, 2) + block, BF16),
            pltpu.VMEM((8, 2, 2, 2, 2) + block, BF16),
            pltpu.VMEM((12, 2, 2, 2) + block, BF16),
            pltpu.VMEM((8, 2, 2) + block, BF16),
            pltpu.VMEM((8, 2) + block, BF16),
            pltpu.VMEM((8, 2) + block, BF16),
            pltpu.VMEM((12, 2, 2) + block, BF16),
            pltpu.VMEM((D, 384), BF16),
            pltpu.VMEM((6, 16, 1024), F32),
            pltpu.VMEM((5, 16, 1024), F32),
            dma((5,)), dma((3, 8)), dma((2,)), dma((4,)), dma((4,)),
            dma((UNITS, 7)), dma((UNITS, 7)), dma((5,)), dma((5,)),
        ],
        compiler_params=pltpu.CompilerParams(collective_id=0, has_side_effects=True, vmem_limit_bytes=64 << 20),
        name="layer",
    )(tokens, out_grad, lengths, *vectors, *weights)


def finish_kernel(
    out_in, ig_in, in_ref, proj_ref, up_ref, down_ref, v_ref,
    out_ref, ig_ref, ag_ref, as_ref, gin_ref, qv_ref, gproj_ref, pb_ref, sc_ref, mg_ref, ms_ref, gup_ref, ub_ref,
    gdown_ref, bd_ref, sm_ref,
):
    out_ref[...] = out_in[...]
    ig_ref[...] = ig_in[...]
    for src, dst in ((in_ref, gin_ref), (proj_ref, gproj_ref), (up_ref, gup_ref), (down_ref, gdown_ref)):
        dst[...] = src[...].astype(F32)
    for row, dst in (
        (ATTN_GAIN, ag_ref), (ATTN_SHIFT, as_ref), (PROJ_BIAS, pb_ref), (ATTN_SCALE, sc_ref), (MLP_GAIN, mg_ref),
        (MLP_SHIFT, ms_ref), (DOWN_BIAS, bd_ref), (MLP_SCALE, sm_ref),
    ):
        dst[...] = v_ref[row, 0:96]
    qv_ref[...] = v_ref[Q_BIAS : V_BIAS + 1, 0:96]
    for j in range(3):
        ub_ref[128 * j : 128 * (j + 1)] = v_ref[UP_BIAS + j]


def finish(output, input_grad, g_in, g_proj, g_up, g_down, v):
    vm = pl.BlockSpec(memory_space=pltpu.VMEM)
    row = jax.ShapeDtypeStruct((96,), F32)

    def wide(shape):
        return jax.ShapeDtypeStruct(shape, F32)

    rows = jax.ShapeDtypeStruct((TOK_DEV, D), BF16)
    return pl.pallas_call(
        finish_kernel,
        out_shape=(
            rows, rows, row, row, wide((96, 3 * D)), wide((2, 96)), wide((96, D)), row, row, row, row, wide((96, 4 * D)),
            wide((384,)), wide((384, D)), row, row,
        ),
        in_specs=[vm] * 7,
        out_specs=(vm,) * 16,
        name="finish",
    )(output.reshape(TOK_DEV, D), input_grad.reshape(TOK_DEV, D), g_in, g_proj, g_up, g_down, v)


def on_device_local(
    tokens, attn_gain, attn_shift, in_weight, query_value_bias, proj_weight, proj_bias, attn_scale,
    mlp_gain, mlp_shift, up_weight, up_bias, down_weight, down_bias, mlp_scale, crop_lengths, out_grad,
):
    output, input_grad, g_in, g_proj, g_up, g_down, v = layer(
        tokens.reshape(2, 256, D), out_grad.reshape(2, 256, D), crop_lengths,
        (attn_gain, attn_shift, query_value_bias, proj_bias, attn_scale, mlp_gain, mlp_shift, up_bias, down_bias, mlp_scale),
        (in_weight, proj_weight, up_weight, down_weight.reshape(8, 3, 128, D)),
    )
    return finish(output, input_grad, g_in, g_proj, g_up, g_down, v)


def solution(mesh):
    local = mesh.shape["wide"] == 8 and mesh.shape["narrow"] == 4
    return jax.shard_map(
        on_device_local if local else on_device,
        mesh=mesh,
        in_specs=(
            P(("narrow", "wide"), None),
            P(),
            P(),
            P(),
            P(),
            P(),
            P(),
            P(),
            P(),
            P(),
            P(),
            P(),
            P(),
            P(),
            P(),
            P("narrow", None),
            P(("narrow", "wide"), None),
        ),
        out_specs=(
            P(("narrow", "wide"), None),
            P(("narrow", "wide"), None),
            P("wide"),
            P("wide"),
            P("wide", None),
            P(None, "wide"),
            P("wide", None),
            P("wide"),
            P("wide"),
            P("wide"),
            P("wide"),
            P("wide", None),
            P("wide"),
            P("wide", None),
            P("wide"),
            P("wide"),
        ),
        check_vma=False,
    )
```

```python
import jax
import jax.numpy as jnp
from jax import lax
from jax.experimental import pallas as pl
from jax.experimental.pallas import tpu as pltpu
from jax.sharding import PartitionSpec as P

D = 768
HEAD_DIM = 64
HEAD_GROUPS = 4
GSLOT = 288
LSLOT = 56
GROUP_IMG = 2
IMG_ROWS = 1024
STREAM = 2048
TOK_DEV = 512


NORM_EPSILON = 1e-06
MASKED = -1e30


def layer_norm(values, gain_row, shift_row):
    row_mean = jnp.mean(values, axis=-1, keepdims=True)
    centered = values - row_mean
    variance = jnp.mean(centered * centered, axis=-1, keepdims=True)
    return centered * lax.rsqrt(variance + NORM_EPSILON) * gain_row + shift_row


def gelu_exact(values):
    return 0.5 * values * (1.0 + jax.scipy.special.erf(values * 0.7071067811865476))


def key_masks(lengths):
    positions = jnp.arange(GSLOT, dtype=jnp.int32)
    global_valid = positions[None, None, :] < lengths[:, :2, None]
    global_valid = global_valid.reshape(GROUP_IMG * 2, 1, 1, GSLOT)
    row_ids = jnp.arange(8 * LSLOT, dtype=jnp.int32)
    crop_ids = row_ids // LSLOT
    offsets = row_ids % LSLOT
    local_lengths = jnp.repeat(lengths[:, 2:], LSLOT, axis=1)
    same_crop = crop_ids[:, None] == crop_ids[None, :]
    local_valid = same_crop[None] & (offsets[None, None, :] < local_lengths[:, None, :])
    return (global_valid, local_valid[:, None])


def split_crops(values):
    global_part = values[:, : 2 * GSLOT].reshape(
        GROUP_IMG * 2, GSLOT, values.shape[2], values.shape[3]
    )
    return (global_part, values[:, 2 * GSLOT :])


def join_crops(global_part, local_part):
    widened = global_part.reshape(GROUP_IMG, 2 * GSLOT, local_part.shape[2], local_part.shape[3])
    return jnp.concatenate([widened, local_part], axis=1)


def unpack_heads(packed):
    per_group = packed.shape[2] // HEAD_DIM
    return [packed[which].reshape(GROUP_IMG, IMG_ROWS, per_group, HEAD_DIM) for which in range(3)]


def tile_logits(queries, key_rows, key_mask, score_scale):
    raw = (
        jnp.einsum("bqhk,bshk->bhqs", queries, key_rows, preferred_element_type=jnp.float32)
        * score_scale
    )
    return jnp.where(key_mask, raw, MASKED)


def forward_tile(queries, key_rows, values, key_mask, score_scale):
    logits = tile_logits(queries, key_rows, key_mask, score_scale)
    row_max = jnp.max(logits, axis=-1, keepdims=True)
    exponent = jnp.exp(logits - row_max)
    row_total = jnp.sum(exponent, axis=-1, keepdims=True)
    weights = (exponent / row_total).astype(jnp.bfloat16)
    result = jnp.einsum("bhqs,bshk->bqhk", weights, values, preferred_element_type=jnp.float32)
    return (result.astype(jnp.bfloat16), row_max + jnp.log(row_total))


def backward_tile(queries, key_rows, values, grad_out, key_mask, logsum, score_scale):
    logits = tile_logits(queries, key_rows, key_mask, score_scale)
    probabilities = jnp.exp(logits - logsum)
    grad_probs = jnp.einsum("bqhk,bshk->bhqs", grad_out, values, preferred_element_type=jnp.float32)
    inner = jnp.sum(probabilities * grad_probs, axis=-1, keepdims=True)
    grad_logits = (probabilities * (grad_probs - inner)).astype(jnp.bfloat16)
    grad_queries = (
        jnp.einsum("bhqs,bshk->bqhk", grad_logits, key_rows, preferred_element_type=jnp.float32)
        * score_scale
    )
    grad_keys = (
        jnp.einsum("bhqs,bqhk->bshk", grad_logits, queries, preferred_element_type=jnp.float32)
        * score_scale
    )
    grad_values = jnp.einsum(
        "bhqs,bqhk->bshk",
        probabilities.astype(jnp.bfloat16),
        grad_out,
        preferred_element_type=jnp.float32,
    )
    return (
        grad_queries.astype(jnp.bfloat16),
        grad_keys.astype(jnp.bfloat16),
        grad_values.astype(jnp.bfloat16),
    )


def attention_forward(packed, masks, score_scale):
    members = [split_crops(member) for member in unpack_heads(packed)]
    results = []
    logsums = []
    for which in range(2):
        result, logsum = forward_tile(
            members[0][which], members[1][which], members[2][which], masks[which], score_scale
        )
        results.append(result)
        logsums.append(logsum)
    return (join_crops(results[0], results[1]).reshape(STREAM, packed.shape[2]), logsums)


def attention_backward(packed, grad_attended, logsums, masks, score_scale):
    members = [split_crops(member) for member in unpack_heads(packed)]
    grad_parts = split_crops(grad_attended.reshape(GROUP_IMG, IMG_ROWS, -1, HEAD_DIM))
    tile_grads = [
        backward_tile(
            members[0][which],
            members[1][which],
            members[2][which],
            grad_parts[which],
            masks[which],
            logsums[which],
            score_scale,
        )
        for which in range(2)
    ]
    joined = [
        join_crops(tile_grads[0][member], tile_grads[1][member]).reshape(STREAM, packed.shape[2])
        for member in range(3)
    ]
    return jnp.stack(joined)


def on_device(
    tokens,
    attn_gain,
    attn_shift,
    in_weight,
    query_value_bias,
    proj_weight,
    proj_bias,
    attn_scale,
    mlp_gain,
    mlp_shift,
    up_weight,
    up_bias,
    down_weight,
    down_bias,
    mlp_scale,
    crop_lengths,
    out_grad,
):
    wide_size = lax.axis_size("wide")
    crop_groups = wide_size // HEAD_GROUPS
    block_rows = TOK_DEV // crop_groups
    head_width = D // HEAD_GROUPS
    score_scale = HEAD_DIM ** (-0.5)
    own_group = lax.axis_index("wide") // HEAD_GROUPS
    own_lengths = lax.dynamic_slice_in_dim(crop_lengths, own_group * GROUP_IMG, GROUP_IMG, 0)
    masks = key_masks(own_lengths)
    inputs = tokens.astype(jnp.float32)
    first_gain = attn_gain.astype(jnp.float32)
    first_shift = attn_shift.astype(jnp.float32)
    normed, first_back = jax.vjp(layer_norm, inputs, first_gain, first_shift)
    normed_low = normed.astype(jnp.bfloat16)
    normed_blocks = normed_low.reshape(crop_groups, block_rows, D)
    weight_in = in_weight.reshape(D, 3, HEAD_GROUPS, head_width)
    qv_rows = query_value_bias.astype(jnp.float32)
    full_bias = jnp.stack([qv_rows[0], jnp.zeros_like(qv_rows[0]), qv_rows[1]]).reshape(
        3, 1, HEAD_GROUPS, 1, head_width
    )
    projected = (
        jnp.einsum("gbd,dchk->cghbk", normed_blocks, weight_in, preferred_element_type=jnp.float32)
        + full_bias
    )
    send_heads = projected.astype(jnp.bfloat16).reshape(3, wide_size, block_rows, head_width)
    arrived = lax.all_to_all(send_heads, "wide", split_axis=1, concat_axis=1, tiled=True)
    packed = arrived.reshape(3, STREAM, head_width)
    attended, logsums = attention_forward(packed, masks, score_scale)
    returned = lax.all_to_all(
        attended.reshape(wide_size, block_rows, head_width),
        "wide",
        split_axis=0,
        concat_axis=0,
        tiled=True,
    )
    mixed_rows = returned.reshape(crop_groups, HEAD_GROUPS, block_rows, head_width)
    weight_proj = proj_weight.reshape(HEAD_GROUPS, head_width, D)
    branch = jnp.einsum(
        "ghbk,hkd->gbd", mixed_rows, weight_proj, preferred_element_type=jnp.float32
    )
    branch = branch.reshape(TOK_DEV, D) + proj_bias.astype(jnp.float32)
    first_scale = attn_scale.astype(jnp.float32)
    middle = inputs + first_scale * branch
    second, second_back = jax.vjp(
        layer_norm, middle, mlp_gain.astype(jnp.float32), mlp_shift.astype(jnp.float32)
    )
    second_low = second.astype(jnp.bfloat16)
    hidden = jnp.dot(second_low, up_weight, preferred_element_type=jnp.float32) + up_bias.astype(
        jnp.float32
    )
    activated, gelu_back = jax.vjp(gelu_exact, hidden)
    activated_low = activated.astype(jnp.bfloat16)
    outcome = jnp.dot(
        activated_low, down_weight, preferred_element_type=jnp.float32
    ) + down_bias.astype(jnp.float32)
    second_scale = mlp_scale.astype(jnp.float32)
    output = (middle + second_scale * outcome).astype(jnp.bfloat16)
    cotangent = out_grad.astype(jnp.float32)
    grad_mlp_scale = jnp.sum(cotangent * outcome, axis=0)
    grad_outcome = (cotangent * second_scale).astype(jnp.bfloat16)
    grad_down_weight = jnp.einsum(
        "tf,td->fd", activated_low, grad_outcome, preferred_element_type=jnp.float32
    )
    grad_down_bias = jnp.sum(grad_outcome.astype(jnp.float32), axis=0)
    grad_activated = jnp.einsum(
        "td,fd->tf", grad_outcome, down_weight, preferred_element_type=jnp.float32
    )
    grad_hidden = gelu_back(grad_activated)[0].astype(jnp.bfloat16)
    grad_up_weight = jnp.einsum(
        "td,tf->df", second_low, grad_hidden, preferred_element_type=jnp.float32
    )
    grad_up_bias = jnp.sum(grad_hidden.astype(jnp.float32), axis=0)
    grad_second = jnp.einsum(
        "tf,df->td", grad_hidden, up_weight, preferred_element_type=jnp.float32
    )
    grad_middle, grad_mlp_gain, grad_mlp_shift = second_back(grad_second)
    grad_middle = grad_middle + cotangent
    grad_attn_scale = jnp.sum(grad_middle * branch, axis=0)
    grad_branch = (grad_middle * first_scale).astype(jnp.bfloat16)
    branch_blocks = grad_branch.reshape(crop_groups, block_rows, D)
    grad_proj_weight = jnp.einsum(
        "ghbk,gbd->hkd", mixed_rows, branch_blocks, preferred_element_type=jnp.float32
    ).reshape(D, D)
    grad_proj_bias = jnp.sum(grad_branch.astype(jnp.float32), axis=0)
    grad_mixed = jnp.einsum(
        "gbd,hkd->ghbk", branch_blocks, weight_proj, preferred_element_type=jnp.float32
    )
    grad_mixed = grad_mixed.astype(jnp.bfloat16).reshape(wide_size, block_rows, head_width)
    again, grad_arrived = (
        lax.all_to_all(send_heads, "wide", split_axis=1, concat_axis=1, tiled=True),
        lax.all_to_all(grad_mixed[None], "wide", split_axis=1, concat_axis=1, tiled=True),
    )
    packed_back = again.reshape(3, STREAM, head_width)
    grad_attended = grad_arrived.reshape(STREAM, head_width)
    grad_packed = attention_backward(packed_back, grad_attended, logsums, masks, score_scale)
    grad_sent = lax.all_to_all(
        grad_packed.reshape(3, wide_size, block_rows, head_width),
        "wide",
        split_axis=1,
        concat_axis=1,
        tiled=True,
    )
    grad_heads = grad_sent.reshape(3, crop_groups, HEAD_GROUPS, block_rows, head_width)
    grad_in_weight = jnp.einsum(
        "gbd,cghbk->dchk", normed_blocks, grad_heads, preferred_element_type=jnp.float32
    ).reshape(D, 3 * D)
    bias_sums = jnp.sum(grad_heads.astype(jnp.float32), axis=(1, 3)).reshape(3, D)
    grad_query_value_bias = jnp.stack([bias_sums[0], bias_sums[2]])
    grad_normed = jnp.einsum(
        "cghbk,dchk->gbd", grad_heads, weight_in, preferred_element_type=jnp.float32
    ).reshape(TOK_DEV, D)
    grad_inputs, grad_attn_gain, grad_attn_shift = first_back(grad_normed)
    input_grad = (grad_inputs + grad_middle).astype(jnp.bfloat16)
    shares = (
        lax.psum_scatter(
            grad_attn_gain.astype(jnp.bfloat16), "wide", scatter_dimension=0, tiled=True
        ).astype(jnp.float32),
        lax.psum_scatter(
            grad_attn_shift.astype(jnp.bfloat16), "wide", scatter_dimension=0, tiled=True
        ).astype(jnp.float32),
        lax.psum_scatter(
            grad_in_weight.astype(jnp.bfloat16), "wide", scatter_dimension=0, tiled=True
        ).astype(jnp.float32),
        lax.psum_scatter(
            grad_query_value_bias.astype(jnp.bfloat16), "wide", scatter_dimension=1, tiled=True
        ).astype(jnp.float32),
        lax.psum_scatter(
            grad_proj_weight.astype(jnp.bfloat16), "wide", scatter_dimension=0, tiled=True
        ).astype(jnp.float32),
        lax.psum_scatter(
            grad_proj_bias.astype(jnp.bfloat16), "wide", scatter_dimension=0, tiled=True
        ).astype(jnp.float32),
        lax.psum_scatter(
            grad_attn_scale.astype(jnp.bfloat16), "wide", scatter_dimension=0, tiled=True
        ).astype(jnp.float32),
        lax.psum_scatter(
            grad_mlp_gain.astype(jnp.bfloat16), "wide", scatter_dimension=0, tiled=True
        ).astype(jnp.float32),
        lax.psum_scatter(
            grad_mlp_shift.astype(jnp.bfloat16), "wide", scatter_dimension=0, tiled=True
        ).astype(jnp.float32),
        lax.psum_scatter(
            grad_up_weight.astype(jnp.bfloat16), "wide", scatter_dimension=0, tiled=True
        ).astype(jnp.float32),
        lax.psum_scatter(
            grad_up_bias.astype(jnp.bfloat16), "wide", scatter_dimension=0, tiled=True
        ).astype(jnp.float32),
        lax.psum_scatter(
            grad_down_weight.astype(jnp.bfloat16), "wide", scatter_dimension=0, tiled=True
        ).astype(jnp.float32),
        lax.psum_scatter(
            grad_down_bias.astype(jnp.bfloat16), "wide", scatter_dimension=0, tiled=True
        ).astype(jnp.float32),
        lax.psum_scatter(
            grad_mlp_scale.astype(jnp.bfloat16), "wide", scatter_dimension=0, tiled=True
        ).astype(jnp.float32),
    )
    results = (
        lax.psum(shares[0].astype(jnp.bfloat16), "narrow").astype(jnp.float32),
        lax.psum(shares[1].astype(jnp.bfloat16), "narrow").astype(jnp.float32),
        lax.psum(shares[2].astype(jnp.bfloat16), "narrow").astype(jnp.float32),
        lax.psum(shares[3].astype(jnp.bfloat16), "narrow").astype(jnp.float32),
        lax.psum(shares[4].astype(jnp.bfloat16), "narrow").astype(jnp.float32),
        lax.psum(shares[5].astype(jnp.bfloat16), "narrow").astype(jnp.float32),
        lax.psum(shares[6].astype(jnp.bfloat16), "narrow").astype(jnp.float32),
        lax.psum(shares[7].astype(jnp.bfloat16), "narrow").astype(jnp.float32),
        lax.psum(shares[8].astype(jnp.bfloat16), "narrow").astype(jnp.float32),
        lax.psum(shares[9].astype(jnp.bfloat16), "narrow").astype(jnp.float32),
        lax.psum(shares[10].astype(jnp.bfloat16), "narrow").astype(jnp.float32),
        lax.psum(shares[11].astype(jnp.bfloat16), "narrow").astype(jnp.float32),
        lax.psum(shares[12].astype(jnp.bfloat16), "narrow").astype(jnp.float32),
        lax.psum(shares[13].astype(jnp.bfloat16), "narrow").astype(jnp.float32),
    )
    return (
        output,
        input_grad,
        results[0],
        results[1],
        results[2],
        results[3],
        results[4],
        results[5],
        results[6],
        results[7],
        results[8],
        results[9],
        results[10],
        results[11],
        results[12],
        results[13],
    )


MESH = pl.DeviceIdType.MESH
F32 = jnp.float32
BF16 = jnp.bfloat16
SLOT = 288
ROWS = 576
UNITS = 18
PAIRS = 9
BLOCK = 48
BLOCKS = ROWS // BLOCK
STAGES = {
    "A": ("core", "x", "z1", "z2", "y whole", "core back"),
    "B": ("core", "y", "x", "z1", "z2", "y back", "core back"),
    "C": ("core", "z1", "z2", "x", "y whole", "core back"),
    "D": ("core", "y", "z1", "z2", "x", "y back", "core back"),
    "E": ("core", "x", "y", "z1", "z2", "y back", "core back"),
}
AXES = ("core", "x", "y", "z1", "z2")
KINDS = "CEEBADBABBABBEBEEE"
PLAN = {
    "down 0": ((0, -1), (1, -1)),
    "up 0": ((2, -1), (3, -1)),
    "combine 0 0": ((0, 0),),
    "combine 0 1": ((1, 0), (2, 0)),
    "combine 0 2": ((3, 0),),
    "hidden 1 b": ((0, 1), (1, 1)),
    "down 1": ((4, -1), (5, -1), (3, 1)),
    "up 1": ((6, -1), (7, -1)),
    "combine 1 0": ((4, 0), (2, 1), (5, 0), (1, 2)),
    "combine 1 1": ((6, 0), (7, 0), (0, 2), (3, 2), (1, 3)),
    "combine 1 2": ((2, 2),),
    "hidden 2 a": ((3, 3),),
    "hidden 2 b": ((4, 1), (5, 1), (2, 3), (1, 4), (3, 4)),
    "down 2": ((8, -1), (9, -1)),
    "up 2": ((10, -1), (11, -1), (7, 1)),
    "combine 2 0": ((8, 0), (6, 1), (9, 0), (4, 2), (0, 3), (1, 5), (3, 5)),
    "combine 2 1": ((10, 0), (11, 0), (5, 2), (2, 4), (1, 6), (3, 6)),
    "combine 2 2": ((6, 2),),
    "norm a": ((8, 1), (7, 2)),
    "norm b": ((18, -1), (10, 1), (4, 3)),
    "grad 12": ((12, -1), (18, 0), (9, 1), (8, 2), (5, 3), (6, 3)),
    "attend 0 a": ((12, 0), (7, 3), (0, 4)),
    "attend 0 b": ((0, 5),),
    "grad 13": ((13, -1), (11, 1), (18, 1), (2, 5)),
    "grad 14": ((14, -1), (4, 4)),
    "attend 1 a": ((13, 0), (14, 0), (9, 2), (10, 2), (8, 3), (5, 4), (4, 5), (2, 6)),
    "attend 1 b": ((12, 1), (11, 2), (9, 3), (6, 4), (7, 4)),
    "grad 15": ((15, -1), (18, 2)),
    "attend 2 a": ((15, 0), (13, 1), (10, 3), (11, 3), (8, 4), (7, 5)),
    "attend 2 b": ((14, 1), (12, 2), (18, 3), (9, 4), (5, 5), (6, 5)),
    "grad 16": ((16, -1), (11, 4), (5, 6), (6, 6)),
    "grad 17": ((17, -1), (15, 1), (13, 2), (12, 3), (16, 0), (10, 4)),
    "dh1 0": ((17, 0), (14, 2), (8, 5), (9, 5), (10, 5), (18, 4), (11, 5)),
    "dh1 1": ((13, 3), (8, 6), (9, 6), (11, 6), (15, 2)),
    "dh1 2": ((14, 3), (12, 4)),
    "input a": ((16, 1), (13, 4), (15, 3), (12, 5)),
    "input b": ((19, -1), (14, 4), (12, 6)),
    "drain": ((15, 4), (16, 2), (17, 1), (19, 0), (13, 5), (14, 5), (15, 5), (13, 6), (14, 6), (15, 6), (17, 2), (19, 1), (16, 3), (17, 3), (19, 2), (16, 4), (17, 4), (19, 3), (16, 5), (17, 5), (16, 6), (19, 4), (17, 6)),
}
ATTN_GAIN, ATTN_SHIFT, Q_BIAS, V_BIAS, PROJ_BIAS, ATTN_SCALE, MLP_GAIN, MLP_SHIFT, DOWN_BIAS, MLP_SCALE = range(10)
UP_BIAS = 10
EARLY_ROWS = (PROJ_BIAS, ATTN_SCALE, MLP_GAIN, MLP_SHIFT, DOWN_BIAS, MLP_SCALE)
LATE_ROWS = (ATTN_GAIN, ATTN_SHIFT, Q_BIAS, V_BIAS)


def dot_nn(a, b):
    return jnp.dot(a, b, preferred_element_type=F32)


def dot_nt(a, b):
    return lax.dot_general(a, b, (((1,), (1,)), ((), ())), preferred_element_type=F32)


def dot_tn(a, b):
    return lax.dot_general(a, b, (((0,), (0,)), ((), ())), preferred_element_type=F32)


def halves(block):
    lanes = lax.broadcasted_iota(jnp.int32, block.shape, 1)
    zero = jnp.zeros_like(block)
    return [jnp.where((lanes < 64) == (h == 0), block, zero) for h in range(2)]


def fold_rows(values):
    return jnp.sum(values.reshape(values.shape[0] // 8, 8, values.shape[1]), axis=0)


def norm_parts(values):
    mean = jnp.sum(values, axis=-1, keepdims=True) * (1.0 / D)
    centered = values - mean
    variance = jnp.sum(centered * centered, axis=-1, keepdims=True) * (1.0 / D)
    rstd = lax.rsqrt(variance + NORM_EPSILON)
    return centered * rstd, rstd


def layer_kernel(
    tok_ref, og_ref, len_ref,
    attn_gain_ref, attn_shift_ref, qv_ref, proj_bias_ref, attn_scale_ref, mlp_gain_ref, mlp_shift_ref,
    up_bias_ref, down_bias_ref, mlp_scale_ref,
    in_hbm, proj_hbm, up_hbm, down_hbm,
    out_hbm, ig_hbm, gin_ref, gproj_ref, gup_ref, gdown_ref, vout_ref,
    win, wproj, wup, wdown,
    xb, db, ob, h1, t1, t2, qkv, att, branch, mid, h2, dm, gact, dhid, macc, dacc, ub, gb, bias, bias_t,
    prm, sums, usums,
    gbuf, r0, r1, r2, r3, r4, fin, wdt, early, early_in, late, late_in,
    wsem, upsem, lsem, hsend, hrecv, ssem, rsem, vssem, vrsem,
):
    n = lax.axis_index("narrow")
    w = lax.axis_index("wide")
    c = n % 2
    y = n // 2
    x = w % 2
    z1 = (w // 2) % 2
    z2 = w // 4
    quarter = w % 4
    shift = 32 * (quarter % 2) + 32 * (quarter // 2) * (2 - 2 * (quarter % 2)) + 0 * quarter
    partner = {
        "core": (n + 1 - 2 * c, w),
        "y": (n + 2 - 4 * y, w),
        "x": (n, w + 1 - 2 * x),
        "z1": (n, w + 2 - 4 * z1),
        "z2": (n, w + 4 - 8 * z2),
        "diagonal": (n, w + 3 - 2 * quarter),
    }

    weights = [
        pltpu.make_async_copy(in_hbm, win, wsem.at[0]),
        pltpu.make_async_copy(proj_hbm, wproj, wsem.at[1]),
    ]
    downs = [pltpu.make_async_copy(down_hbm.at[:, j], wdown.at[j], wsem.at[2 + j]) for j in range(3)]
    ups = [
        [
            pltpu.make_async_copy(
                up_hbm.at[:, 128 * (3 * s + j) : 128 * (3 * s + j + 1)],
                wup.at[:, 128 * (8 * j + s) : 128 * (8 * j + s + 1)],
                upsem.at[j],
            )
            for s in range(8)
        ]
        for j in range(3)
    ]
    own = pl.ds(pl.multiple_of(64 - shift, 32), 256)
    loads = [
        pltpu.make_async_copy(tok_ref, xb.at[:, own], lsem.at[0]),
        pltpu.make_async_copy(og_ref, db.at[:, own], lsem.at[1]),
    ]
    loads[0].start()
    weights[0].start()
    loads[1].start()
    weights[1].start()
    for j in range(3):
        for s in range(8):
            ups[j][s].start()
        downs[j].start()

    barrier = pltpu.get_barrier_semaphore()
    for target in partner.values():
        pl.semaphore_signal(barrier, inc=1, device_id=target, device_id_type=MESH)

    before_shift = 32 * ((quarter + 3) % 2) + 32 * ((quarter - 1) // 2) * (2 - 2 * ((quarter + 3) % 2))
    before = (n, w - 1)
    after = (n, w + 1)

    def halo_in(src, dst, k):
        return pltpu.make_async_remote_copy(
            src_ref=src.at[:, 0:64],
            dst_ref=dst.at[:, pl.ds(pl.multiple_of(320 - before_shift, 32), 64)],
            send_sem=hsend.at[k], recv_sem=hrecv.at[k], device_id=before, device_id_type=MESH,
        )

    def halo_back(buf, k, size):
        return pltpu.make_async_remote_copy(
            src_ref=buf.at[:, pl.ds(pl.multiple_of(320 - shift, 32), size)],
            dst_ref=buf.at[:, 64 - size : 64],
            send_sem=hsend.at[k], recv_sem=hrecv.at[k], device_id=after, device_id_type=MESH,
        )

    for row, ref in (
        (ATTN_GAIN, attn_gain_ref), (ATTN_SHIFT, attn_shift_ref), (PROJ_BIAS, proj_bias_ref), (ATTN_SCALE, attn_scale_ref),
        (MLP_GAIN, mlp_gain_ref), (MLP_SHIFT, mlp_shift_ref), (DOWN_BIAS, down_bias_ref), (MLP_SCALE, mlp_scale_ref),
    ):
        prm[row : row + 1, 0:D] = ref[...].astype(F32).reshape(1, D)
    qv = qv_ref[...].astype(F32)
    prm[Q_BIAS : Q_BIAS + 1, 0:D] = qv[0:1]
    prm[V_BIAS : V_BIAS + 1, 0:D] = qv[1:2]
    up_row = up_bias_ref[...].astype(F32).reshape(1, 4 * D)
    for j in range(3):
        for s in range(8):
            prm[UP_BIAS + j : UP_BIAS + j + 1, 128 * s : 128 * (s + 1)] = up_row[:, 128 * (3 * s + j) : 128 * (3 * s + j + 1)]
    sums[...] = jnp.zeros_like(sums)
    usums[...] = jnp.zeros_like(usums)

    def param(row):
        return prm[row : row + 1, 0:D]

    is_local = quarter // 2
    for i in range(2):
        image = 2 * i + z2

        def crop_of(axis, valid_only):
            shape = (1, SLOT) if axis == 1 else (SLOT, 1)
            place = lax.broadcasted_iota(jnp.int32, shape, axis)
            ids = jnp.full(shape, -1 if valid_only else 4, jnp.int32)
            for m in range(4):
                start = 56 * m * is_local
                if valid_only:
                    local_length = len_ref[image, 2 + 4 * (quarter % 2) + m]
                    global_length = len_ref[image, quarter % 2] if m == 0 else 0
                    size = is_local * local_length + (1 - is_local) * global_length
                else:
                    size = 56 * is_local + (1 - is_local) * (SLOT if m == 0 else 0)
                inside = jnp.logical_and(place >= start, place < start + size)
                ids = jnp.where(inside, m, ids)
            return ids

        bias[i] = jnp.where(crop_of(0, False) == crop_of(1, True), 0.0, MASKED)
        bias_t[i] = jnp.where(crop_of(1, False) == crop_of(0, True), 0.0, MASKED)

    pl.semaphore_wait(barrier, 6)

    @pl.when(quarter > 0)
    def _():
        halo_in(tok_ref, xb, 0).start()
        halo_in(og_ref, db, 1).start()

    def take_halo(src, dst, k):
        @pl.when(quarter > 0)
        def _():
            halo_in(src, dst, k).wait_send()

        @pl.when(quarter < 3)
        def _():
            halo_in(src, dst, k).wait_recv()

        @pl.when(quarter > 1)
        def _():
            dst[:, 288:352] = jnp.zeros((2, 64, D), BF16)

    def at(b):
        i, k = b // 6, b % 6
        return i, pl.ds(pl.multiple_of(64 + BLOCK * k, 16), BLOCK), pl.ds(pl.multiple_of(BLOCK * b, 16), BLOCK)

    def first_norm(b):
        i, slots, rows = at(b)
        normed, _ = norm_parts(xb[i, slots].astype(F32))
        h1[rows] = (normed * param(ATTN_GAIN) + param(ATTN_SHIFT)).astype(BF16)

    def project(low, high):
        rows = jnp.concatenate([h1[SLOT * i + low : SLOT * i + high] for i in range(2)], axis=0)
        for tile in range(9):
            cols = slice(256 * tile, 256 * (tile + 1))
            result = dot_nn(rows, win[:, cols])
            if tile < 3:
                result = (result + prm[Q_BIAS : Q_BIAS + 1, cols]).astype(BF16) * jnp.asarray(0.125, BF16)
            elif tile >= 6:
                result = result + prm[V_BIAS : V_BIAS + 1, 256 * (tile - 6) : 256 * (tile - 5)]
            result = result.astype(BF16)
            for i in range(2):
                qkv[SLOT * i + low : SLOT * i + high, cols] = result[(high - low) * i : (high - low) * (i + 1)]

    loads[0].wait()
    for b in (0, 1, 2, 3, 6, 7, 8, 9):
        first_norm(b)
    weights[0].wait()
    project(0, 192)
    take_halo(tok_ref, xb, 0)
    for b in (4, 5, 10, 11):
        first_norm(b)
    project(192, SLOT)

    def pair_at(index):
        i, h = index % 2, index // 2
        rows = pl.ds(pl.multiple_of(SLOT * i, 16), SLOT)
        return i, rows, [pl.ds(pl.multiple_of(D * m + 128 * h, 128), 128) for m in range(3)]

    def attend(index, _):
        i, rows, cols = pair_at(index)
        q, v = qkv[rows, cols[0]], qkv[rows, cols[2]]
        keys = halves(qkv[rows, cols[1]])
        lanes = lax.broadcasted_iota(jnp.int32, (SLOT, 128), 1)
        ones = jnp.ones_like(v)
        parts = []
        for h in range(2):
            s = dot_nt(q, keys[h]) + bias[i]
            e = jnp.exp(s - jnp.max(s, axis=-1, keepdims=True)).astype(BF16)
            part = dot_nn(e, jnp.where((lanes < 64) == (h == 0), v, ones))
            parts.append(part / pltpu.roll(part, 64, 1))
        att[rows, cols[0]] = jnp.where(lanes < 64, parts[0], parts[1]).astype(BF16)
        return 0

    lax.fori_loop(0, 12, attend, 0, unroll=2)

    weights[1].wait()
    for tile in range(3):
        cols = slice(256 * tile, 256 * (tile + 1))
        result = dot_nn(att[...], wproj[:, cols]) + prm[PROJ_BIAS : PROJ_BIAS + 1, cols]
        branch[:, cols] = result.astype(BF16)
        scaled = prm[ATTN_SCALE : ATTN_SCALE + 1, cols] * result
        for i in range(2):
            mid[SLOT * i : SLOT * (i + 1), cols] = (
                xb[i, 64 : 64 + SLOT, cols].astype(F32) + scaled[SLOT * i : SLOT * (i + 1)]
            )

    loads[1].wait()
    take_halo(og_ref, db, 1)

    def second_norm(b, _):
        i, slots, rows = at(b)
        low = (db[i, slots].astype(F32) * param(MLP_SCALE)).astype(BF16)
        dm[rows] = low
        sums[DOWN_BIAS] += fold_rows(low.astype(F32))
        normed, _ = norm_parts(mid[rows])
        h2[rows] = (normed * param(MLP_GAIN) + param(MLP_SHIFT)).astype(BF16)
        return 0

    lax.fori_loop(0, BLOCKS, second_norm, 0, unroll=3)

    def transpose_into(dst, src):
        for k in range(6):
            dst[128 * k : 128 * (k + 1)] = src[:, 128 * k : 128 * (k + 1)].T

    def copy(src, dst, unit, stage, axis):
        return pltpu.make_async_remote_copy(
            src_ref=src, dst_ref=dst,
            send_sem=ssem.at[unit % ssem.shape[0], stage], recv_sem=rsem.at[unit % rsem.shape[0], stage],
            device_id=partner[axis], device_id_type=MESH,
        )

    bits = {"core": c, "y": y, "x": x, "z1": z1, "z2": z2}
    landing = (r0, r1, r2, r3, r4)

    def share(u, letter, k, mine):
        stages = STAGES[letter]
        index = [u]
        for axis in bits:
            if axis in stages[:k]:
                index.append(bits[axis])
            elif axis == stages[k]:
                index.append(bits[axis] if mine else 1 - bits[axis])
            else:
                index.append(slice(None))
        return gbuf.at[tuple(index)]

    def transfer(u, letter, k):
        stage = STAGES[letter][k]
        slot = u % fin.shape[0]
        if stage == "core back":
            return copy(fin.at[slot, c], fin.at[slot, c], u, k, "core")
        if stage == "y back":
            return copy(fin.at[slot, c, y], fin.at[slot, c, y], u, k, "y")
        dst = landing[k].at[u % landing[k].shape[0]]
        if k == 4 and stage != "y whole":
            dst = dst.at[0]
        return copy(share(u, letter, k, False), dst, u, k, stage.split()[0])

    def add(dst, src):
        dst[...] = (dst[...].astype(F32) + src[...].astype(F32)).astype(BF16)

    def land(u, letter, k):
        stage = STAGES[letter][k]
        if "back" in stage:
            return
        slot = u % fin.shape[0]
        src = landing[k].at[u % landing[k].shape[0]]
        own = share(u, letter, k, True)
        if k == 0:

            def body(index, _):
                add(own.at[index // 2, index % 2], src.at[index // 2, index % 2])
                return 0

            lax.fori_loop(0, 4, body, 0)
        elif k < 4:
            add(own, src)
        elif stage == "y whole":
            fin[slot, c] = (own[...].astype(F32) + src[...].astype(F32)).astype(BF16)
        else:
            fin[slot, c, y] = (own[...].astype(F32) + src[0].astype(F32)).astype(BF16)

    def in_tile(index):
        return 3 * ((index - 3) % 3) + (index - 3) // 3

    def write_out(u):
        p, a = u // 2, u % 2
        slot = u % fin.shape[0]
        for sub in range(4):
            block = fin[slot, sub // 2, sub % 2]
            if p >= 6:
                index = 2 * (u - 12) + sub // 2
                dst, tile = (gproj_ref, index) if index < 3 else (gin_ref, in_tile(index))
                start = 256 * tile + 128 * (sub % 2)
                dst[:, start : start + 128] = block
            elif p % 2 == 1:
                start = 128 * (3 * (4 * a + sub) + p // 2)
                gup_ref[:, start : start + 128] = block
            else:
                wdt[384 * a + 96 * sub : 384 * a + 96 * (sub + 1), 64 * p : 64 * p + 128] = block

    def vector_event(buf, arrived, which, k):
        def exchange(stage):
            return pltpu.make_async_remote_copy(
                src_ref=buf.at[stage], dst_ref=arrived.at[stage], send_sem=vssem.at[which, stage],
                recv_sem=vrsem.at[which, stage], device_id=partner[AXES[stage]], device_id_type=MESH,
            )

        if k >= 0:
            exchange(k).wait()
            buf[k + 1] = (buf[k].astype(F32) + arrived[k].astype(F32)).astype(buf.dtype)
        if k < 4:
            exchange(k + 1).start()

    def event(u, k):
        if u >= UNITS:
            vector_event((early, late)[u - UNITS], (early_in, late_in)[u - UNITS], u - UNITS, k)
            return
        letter = KINDS[u]
        if k >= 0:
            transfer(u, letter, k).wait()
            land(u, letter, k)
        if k + 1 < len(STAGES[letter]):
            transfer(u, letter, k + 1).start()
        else:
            write_out(u)

    def poll(place):
        for u, k in PLAN.get(place, ()):
            event(u, k)

    transpose_into(t1, dm)

    def gelu_block(j, tile, b):
        _, _, rows = at(b)
        cols = pl.ds(pl.multiple_of(256 * tile, 256), 256)
        u = ub[rows] + prm[pl.ds(UP_BIAS + j, 1), cols]
        phi = 0.5 * (1.0 + lax.erf(u * 0.7071067811865476))
        gact[rows, cols] = (u * phi).astype(BF16)
        slope = phi + u * (jnp.exp(u * u * -0.5) * 0.3989422804014327)
        low = (gb[rows] * slope).astype(BF16)
        dhid[rows, cols] = low
        usums[:, pl.ds(pl.multiple_of(1024 * j + 256 * tile, 256), 256)] += fold_rows(low.astype(F32))

    def mlp(j):
        part = wup.at[:, 1024 * j : 1024 * (j + 1)]
        pltpu.make_async_copy(up_hbm.at[:, 0:1024], part, upsem.at[j]).wait()
        downs[j].wait()

        def hidden_tile(tile, _):
            cols = pl.ds(pl.multiple_of(1024 * j + 256 * tile, 256), 256)
            ub[...] = dot_nn(h2[...], wup[:, cols])
            down = wdown[j, pl.ds(2 * tile, 2)].reshape(256, D)
            gb[...] = dot_nt(dm[...], down)

            def block(b, _):
                gelu_block(j, tile, b)
                return 0

            lax.fori_loop(0, BLOCKS, block, 0, unroll=3)
            return 0

        def down_grad(nt, _):
            result = dot_nn(t1[...], gact[:, pl.ds(pl.multiple_of(256 * nt, 256), 256)])
            for ss in range(2):
                for sub in range(8):
                    gbuf[4 * j + sub // 4, (sub // 2) % 2, sub % 2, ss, nt % 2, nt // 2] = result[
                        96 * sub : 96 * (sub + 1), 128 * ss : 128 * (ss + 1)
                    ].astype(BF16)
            return 0

        def up_grad(nt, _):
            result = dot_nn(t2[...], dhid[:, pl.ds(pl.multiple_of(256 * nt, 256), 256)])
            for s in range(8):
                for yy in range(2):
                    gbuf[4 * j + 2 + nt // 2, nt % 2, yy, s % 2, (s // 2) % 2, s // 4] = result[
                        96 * s : 96 * (s + 1), 128 * yy : 128 * (yy + 1)
                    ].astype(BF16)
            return 0

        def combine(nt):
            cols = slice(256 * nt, 256 * (nt + 1))
            more = dot_nn(gact[...], wdown[j, :, :, cols].reshape(1024, 256))
            more_d = dot_nt(dhid[...], wup[cols, 1024 * j : 1024 * (j + 1)])
            macc[:, cols] = more if j == 0 else macc[:, cols] + more
            dacc[:, cols] = more_d if j == 0 else dacc[:, cols] + more_d

        lax.fori_loop(0, 2, hidden_tile, 0)
        poll(f"hidden {j} a")
        lax.fori_loop(2, 4, hidden_tile, 0)
        poll(f"hidden {j} b")
        lax.fori_loop(0, 4, down_grad, 0, unroll=2)
        poll(f"down {j}")
        if j == 0:
            transpose_into(t2, h2)
        lax.fori_loop(0, 4, up_grad, 0, unroll=2)
        poll(f"up {j}")
        for nt in range(3):
            combine(nt)
            poll(f"combine {j} {nt}")

    for j in range(3):
        mlp(j)

    transpose_into(t1, h1)
    transpose_into(t2, att)

    def second_back(b, _):
        i, slots, rows = at(b)
        grad = db[i, slots].astype(F32)
        y_rows = mid[rows]
        outcome = macc[rows] + param(DOWN_BIAS)
        ob[i, slots] = (y_rows + param(MLP_SCALE) * outcome).astype(BF16)
        sums[MLP_SCALE] += fold_rows(grad * outcome)
        normed, rstd = norm_parts(y_rows)
        dh = dacc[rows]
        sums[MLP_GAIN] += fold_rows(dh * normed)
        sums[MLP_SHIFT] += fold_rows(dh)
        e = dh * param(MLP_GAIN)
        mean_e = jnp.sum(e, axis=-1, keepdims=True) * (1.0 / D)
        mean_en = jnp.sum(e * normed, axis=-1, keepdims=True) * (1.0 / D)
        dy = grad + rstd * (e - mean_e - normed * mean_en)
        dacc[rows] = dy
        sums[ATTN_SCALE] += fold_rows(dy * branch[rows].astype(F32))
        low = (dy * param(ATTN_SCALE)).astype(BF16)
        dm[rows] = low
        sums[PROJ_BIAS] += fold_rows(low.astype(F32))
        return 0

    lax.fori_loop(0, 6, second_back, 0, unroll=2)
    poll("norm a")
    lax.fori_loop(6, BLOCKS, second_back, 0, unroll=2)

    def give_back(buf, k):
        @pl.when(quarter % 2 == 0)
        def _():
            halo_back(buf, k, 32).start()

        @pl.when(quarter == 1)
        def _():
            halo_back(buf, k, 64).start()

    def take_back(buf, k):
        @pl.when(quarter % 2 == 0)
        def _():
            halo_back(buf, k, 32).wait_send()

        @pl.when(quarter == 1)
        def _():
            halo_back(buf, k, 64).wait_send()

        @pl.when(quarter % 2 == 1)
        def _():
            halo_back(buf, k, 32).wait_recv()

        @pl.when(quarter == 2)
        def _():
            halo_back(buf, k, 64).wait_recv()

    give_back(ob, 2)
    rows = [jnp.sum(sums[row], axis=0, keepdims=True) for row in EARLY_ROWS]
    for index, row in enumerate(rows):
        early[0, index : index + 1, 0:D] = row.astype(BF16)
    for j in range(3):
        early[0, 6 + j : 7 + j] = jnp.sum(usums[:, 1024 * j : 1024 * (j + 1)], axis=0, keepdims=True).astype(BF16)
    poll("norm b")

    for tile in range(3):
        cols = slice(256 * tile, 256 * (tile + 1))
        h2[:, cols] = dot_nt(dm[...], wproj[cols]).astype(BF16)

    def attend_back(index, _):
        i, rows, cols = pair_at(index)
        k, v = qkv[rows, cols[1]], qkv[rows, cols[2]]
        queries, keys, grads = halves(qkv[rows, cols[0]]), halves(k), halves(h2[rows, cols[0]])
        dq = dk = dv = None
        for h in range(2):
            s = dot_nt(k, queries[h]) + bias_t[i]
            e = jnp.exp(s - jnp.max(s, axis=0, keepdims=True))
            p = e * (1.0 / jnp.sum(e, axis=0, keepdims=True))
            dp = dot_nt(v, grads[h])
            ds = (p * (dp - jnp.sum(p * dp, axis=0, keepdims=True))).astype(BF16)
            parts = dot_tn(ds, keys[h]), dot_nn(ds, queries[h]), dot_nn(p.astype(BF16), grads[h])
            dq, dk, dv = parts if dq is None else (dq + parts[0], dk + parts[1], dv + parts[2])
        low_q, low_v = (dq * 0.125).astype(BF16), dv.astype(BF16)
        qkv[rows, cols[0]] = low_q
        qkv[rows, cols[1]] = dk.astype(BF16)
        qkv[rows, cols[2]] = low_v
        sums[Q_BIAS, :, cols[0]] += fold_rows(low_q.astype(F32))
        sums[V_BIAS, :, cols[0]] += fold_rows(low_v.astype(F32))
        return 0

    def attn_grad(u):
        for half in range(2):
            index = 2 * (u - 12) + half
            if index < 3:
                result = dot_nn(t2[...], dm[:, 256 * index : 256 * (index + 1)])
            else:
                result = dot_nn(t1[...], qkv[:, 256 * in_tile(index) : 256 * (in_tile(index) + 1)])
            for s in range(8):
                for yy in range(2):
                    gbuf[u, half, yy, s % 2, (s // 2) % 2, s // 4] = result[
                        96 * s : 96 * (s + 1), 128 * yy : 128 * (yy + 1)
                    ].astype(BF16)
        poll(f"grad {u}")

    poll("branch")
    attn_grad(12)
    for m in range(3):
        lax.fori_loop(4 * m, 4 * m + 2, attend_back, 0, unroll=2)
        poll(f"attend {m} a")
        lax.fori_loop(4 * m + 2, 4 * m + 4, attend_back, 0, unroll=2)
        poll(f"attend {m} b")
        for u in ((13, 14), (15,), (16, 17))[m]:
            attn_grad(u)

    for tile in range(3):
        cols = slice(256 * tile, 256 * (tile + 1))
        macc[:, cols] = dot_nt(qkv[...], win[cols])
        poll(f"dh1 {tile}")

    def first_back(b, _):
        i, slots, rows = at(b)
        normed, rstd = norm_parts(xb[i, slots].astype(F32))
        dh = macc[rows]
        sums[ATTN_GAIN] += fold_rows(dh * normed)
        sums[ATTN_SHIFT] += fold_rows(dh)
        e = dh * param(ATTN_GAIN)
        mean_e = jnp.sum(e, axis=-1, keepdims=True) * (1.0 / D)
        mean_en = jnp.sum(e * normed, axis=-1, keepdims=True) * (1.0 / D)
        db[i, slots] = (dacc[rows] + rstd * (e - mean_e - normed * mean_en)).astype(BF16)
        return 0

    lax.fori_loop(0, 6, first_back, 0, unroll=2)
    poll("input a")
    lax.fori_loop(6, BLOCKS, first_back, 0, unroll=2)
    give_back(db, 3)

    late[0] = jnp.zeros_like(late[0])
    for index, row in enumerate(LATE_ROWS):
        late[0, index : index + 1] = jnp.sum(sums[row], axis=0, keepdims=True)
    poll("input b")
    poll("drain")

    turn = (D - 96 * w) % D
    vout_ref[0:6] = pltpu.roll(early[5, :, 0:D].astype(F32), turn, 1)[0:6, 0:128]
    vout_ref[6:9] = early[5, 6:9, pl.ds(pl.multiple_of(128 * w, 128), 128)].astype(F32)
    vout_ref[16:24] = pltpu.roll(late[5], turn, 1)[:, 0:128]

    for a in range(3):
        for b in range(6):
            gdown_ref[128 * a : 128 * (a + 1), 128 * b : 128 * (b + 1)] = wdt[
                128 * b : 128 * (b + 1), 128 * a : 128 * (a + 1)
            ].T

    take_back(ob, 2)
    take_back(db, 3)
    stores = [
        pltpu.make_async_copy(ob.at[:, own], out_hbm, lsem.at[0]),
        pltpu.make_async_copy(db.at[:, own], ig_hbm, lsem.at[1]),
    ]
    for store in stores:
        store.start()
    for store in stores:
        store.wait()


def layer(tokens, out_grad, lengths, vectors, weights):
    vm = pl.BlockSpec(memory_space=pltpu.VMEM)
    hbm = pl.BlockSpec(memory_space=pl.ANY)
    dma = pltpu.SemaphoreType.DMA
    slots = pltpu.VMEM((2, 384, D), BF16)
    square = pltpu.VMEM((ROWS, D), BF16)
    wide_square = pltpu.VMEM((ROWS, D), F32)
    block = (96, 128)
    return pl.pallas_call(
        layer_kernel,
        out_shape=(
            jax.ShapeDtypeStruct((2, 256, D), BF16),
            jax.ShapeDtypeStruct((2, 256, D), BF16),
            jax.ShapeDtypeStruct((96, 3 * D), BF16),
            jax.ShapeDtypeStruct((96, D), BF16),
            jax.ShapeDtypeStruct((96, 4 * D), BF16),
            jax.ShapeDtypeStruct((384, D), BF16),
            jax.ShapeDtypeStruct((24, 128), F32),
        ),
        in_specs=[hbm, hbm, pl.BlockSpec(memory_space=pltpu.SMEM)] + [vm] * 10 + [hbm] * 4,
        out_specs=(hbm, hbm, vm, vm, vm, vm, vm),
        scratch_shapes=[
            pltpu.VMEM((D, 3 * D), BF16),
            pltpu.VMEM((D, D), BF16),
            pltpu.VMEM((D, 4 * D), BF16),
            pltpu.VMEM((3, 8, 128, D), BF16),
            slots, slots, slots,
            square,
            pltpu.VMEM((D, ROWS), BF16),
            pltpu.VMEM((D, ROWS), BF16),
            pltpu.VMEM((ROWS, 3 * D), BF16),
            square, square,
            wide_square,
            square, square,
            pltpu.VMEM((ROWS, 1024), BF16),
            pltpu.VMEM((ROWS, 1024), BF16),
            wide_square, wide_square,
            pltpu.VMEM((ROWS, 256), F32),
            pltpu.VMEM((ROWS, 256), F32),
            pltpu.VMEM((2, SLOT, SLOT), F32),
            pltpu.VMEM((2, SLOT, SLOT), F32),
            pltpu.VMEM((16, 1024), F32),
            pltpu.VMEM((10, 8, D), F32),
            pltpu.VMEM((8, 4 * D), F32),
            pltpu.VMEM((UNITS, 2, 2, 2, 2, 2) + block, BF16),
            pltpu.VMEM((8, 2, 2, 2, 2) + block, BF16),
            pltpu.VMEM((12, 2, 2, 2) + block, BF16),
            pltpu.VMEM((8, 2, 2) + block, BF16),
            pltpu.VMEM((12, 2) + block, BF16),
            pltpu.VMEM((12, 2) + block, BF16),
            pltpu.VMEM((12, 2, 2) + block, BF16),
            pltpu.VMEM((D, 384), BF16),
            pltpu.VMEM((6, 16, 1024), BF16),
            pltpu.VMEM((5, 16, 1024), BF16),
            pltpu.VMEM((6, 8, D), F32),
            pltpu.VMEM((5, 8, D), F32),
            dma((5,)), dma((3,)), dma((2,)), dma((4,)), dma((4,)),
            dma((12, 7)), dma((12, 7)), dma((2, 5)), dma((2, 5)),
        ],
        compiler_params=pltpu.CompilerParams(collective_id=0, has_side_effects=True, vmem_limit_bytes=64 << 20),
        name="layer",
    )(tokens, out_grad, lengths, *vectors, *weights)


def finish_kernel(
    out_in, ig_in, in_ref, proj_ref, up_ref, down_ref, v_ref,
    out_ref, ig_ref, ag_ref, as_ref, gin_ref, qv_ref, gproj_ref, pb_ref, sc_ref, mg_ref, ms_ref, gup_ref, ub_ref,
    gdown_ref, bd_ref, sm_ref,
):
    out_ref[...] = out_in[...]
    ig_ref[...] = ig_in[...]
    for src, dst in ((in_ref, gin_ref), (proj_ref, gproj_ref), (up_ref, gup_ref), (down_ref, gdown_ref)):
        dst[...] = src[...].astype(F32)
    for row, dst in zip((0, 1, 2, 3, 4, 5, 16, 17), (pb_ref, sc_ref, mg_ref, ms_ref, bd_ref, sm_ref, ag_ref, as_ref)):
        dst[...] = v_ref[row, 0:96]
    qv_ref[...] = v_ref[18:20, 0:96]
    for j in range(3):
        ub_ref[128 * j : 128 * (j + 1)] = v_ref[6 + j]


def finish(output, input_grad, g_in, g_proj, g_up, g_down, v):
    vm = pl.BlockSpec(memory_space=pltpu.VMEM)
    row = jax.ShapeDtypeStruct((96,), F32)

    def wide(shape):
        return jax.ShapeDtypeStruct(shape, F32)

    rows = jax.ShapeDtypeStruct((TOK_DEV, D), BF16)
    return pl.pallas_call(
        finish_kernel,
        out_shape=(
            rows, rows, row, row, wide((96, 3 * D)), wide((2, 96)), wide((96, D)), row, row, row, row, wide((96, 4 * D)),
            wide((384,)), wide((384, D)), row, row,
        ),
        in_specs=[vm] * 7,
        out_specs=(vm,) * 16,
        name="finish",
    )(output.reshape(TOK_DEV, D), input_grad.reshape(TOK_DEV, D), g_in, g_proj, g_up, g_down, v)


def on_device_local(
    tokens, attn_gain, attn_shift, in_weight, query_value_bias, proj_weight, proj_bias, attn_scale,
    mlp_gain, mlp_shift, up_weight, up_bias, down_weight, down_bias, mlp_scale, crop_lengths, out_grad,
):
    output, input_grad, g_in, g_proj, g_up, g_down, v = layer(
        tokens.reshape(2, 256, D), out_grad.reshape(2, 256, D), crop_lengths,
        (attn_gain, attn_shift, query_value_bias, proj_bias, attn_scale, mlp_gain, mlp_shift, up_bias, down_bias, mlp_scale),
        (in_weight, proj_weight, up_weight, down_weight.reshape(8, 3, 128, D)),
    )
    return finish(output, input_grad, g_in, g_proj, g_up, g_down, v)


def solution(mesh):
    local = mesh.shape["wide"] == 8 and mesh.shape["narrow"] == 4
    return jax.shard_map(
        on_device_local if local else on_device,
        mesh=mesh,
        in_specs=(
            P(("narrow", "wide"), None),
            P(),
            P(),
            P(),
            P(),
            P(),
            P(),
            P(),
            P(),
            P(),
            P(),
            P(),
            P(),
            P(),
            P(),
            P("narrow", None),
            P(("narrow", "wide"), None),
        ),
        out_specs=(
            P(("narrow", "wide"), None),
            P(("narrow", "wide"), None),
            P("wide"),
            P("wide"),
            P("wide", None),
            P(None, "wide"),
            P("wide", None),
            P("wide"),
            P("wide"),
            P("wide"),
            P("wide"),
            P("wide", None),
            P("wide"),
            P("wide", None),
            P("wide"),
            P("wide"),
        ),
        check_vma=False,
    )
```

```python
import jax
import jax.numpy as jnp
from jax import lax
from jax.experimental import pallas as pl
from jax.experimental.pallas import tpu as pltpu
from jax.sharding import PartitionSpec as P

D = 768
HEAD_DIM = 64
HEAD_GROUPS = 4
GSLOT = 288
LSLOT = 56
GROUP_IMG = 2
IMG_ROWS = 1024
STREAM = 2048
TOK_DEV = 512


NORM_EPSILON = 1e-06
MASKED = -1e30


def layer_norm(values, gain_row, shift_row):
    row_mean = jnp.mean(values, axis=-1, keepdims=True)
    centered = values - row_mean
    variance = jnp.mean(centered * centered, axis=-1, keepdims=True)
    return centered * lax.rsqrt(variance + NORM_EPSILON) * gain_row + shift_row


def gelu_exact(values):
    return 0.5 * values * (1.0 + jax.scipy.special.erf(values * 0.7071067811865476))


def key_masks(lengths):
    positions = jnp.arange(GSLOT, dtype=jnp.int32)
    global_valid = positions[None, None, :] < lengths[:, :2, None]
    global_valid = global_valid.reshape(GROUP_IMG * 2, 1, 1, GSLOT)
    row_ids = jnp.arange(8 * LSLOT, dtype=jnp.int32)
    crop_ids = row_ids // LSLOT
    offsets = row_ids % LSLOT
    local_lengths = jnp.repeat(lengths[:, 2:], LSLOT, axis=1)
    same_crop = crop_ids[:, None] == crop_ids[None, :]
    local_valid = same_crop[None] & (offsets[None, None, :] < local_lengths[:, None, :])
    return (global_valid, local_valid[:, None])


def split_crops(values):
    global_part = values[:, : 2 * GSLOT].reshape(
        GROUP_IMG * 2, GSLOT, values.shape[2], values.shape[3]
    )
    return (global_part, values[:, 2 * GSLOT :])


def join_crops(global_part, local_part):
    widened = global_part.reshape(GROUP_IMG, 2 * GSLOT, local_part.shape[2], local_part.shape[3])
    return jnp.concatenate([widened, local_part], axis=1)


def unpack_heads(packed):
    per_group = packed.shape[2] // HEAD_DIM
    return [packed[which].reshape(GROUP_IMG, IMG_ROWS, per_group, HEAD_DIM) for which in range(3)]


def tile_logits(queries, key_rows, key_mask, score_scale):
    raw = (
        jnp.einsum("bqhk,bshk->bhqs", queries, key_rows, preferred_element_type=jnp.float32)
        * score_scale
    )
    return jnp.where(key_mask, raw, MASKED)


def forward_tile(queries, key_rows, values, key_mask, score_scale):
    logits = tile_logits(queries, key_rows, key_mask, score_scale)
    row_max = jnp.max(logits, axis=-1, keepdims=True)
    exponent = jnp.exp(logits - row_max)
    row_total = jnp.sum(exponent, axis=-1, keepdims=True)
    weights = (exponent / row_total).astype(jnp.bfloat16)
    result = jnp.einsum("bhqs,bshk->bqhk", weights, values, preferred_element_type=jnp.float32)
    return (result.astype(jnp.bfloat16), row_max + jnp.log(row_total))


def backward_tile(queries, key_rows, values, grad_out, key_mask, logsum, score_scale):
    logits = tile_logits(queries, key_rows, key_mask, score_scale)
    probabilities = jnp.exp(logits - logsum)
    grad_probs = jnp.einsum("bqhk,bshk->bhqs", grad_out, values, preferred_element_type=jnp.float32)
    inner = jnp.sum(probabilities * grad_probs, axis=-1, keepdims=True)
    grad_logits = (probabilities * (grad_probs - inner)).astype(jnp.bfloat16)
    grad_queries = (
        jnp.einsum("bhqs,bshk->bqhk", grad_logits, key_rows, preferred_element_type=jnp.float32)
        * score_scale
    )
    grad_keys = (
        jnp.einsum("bhqs,bqhk->bshk", grad_logits, queries, preferred_element_type=jnp.float32)
        * score_scale
    )
    grad_values = jnp.einsum(
        "bhqs,bqhk->bshk",
        probabilities.astype(jnp.bfloat16),
        grad_out,
        preferred_element_type=jnp.float32,
    )
    return (
        grad_queries.astype(jnp.bfloat16),
        grad_keys.astype(jnp.bfloat16),
        grad_values.astype(jnp.bfloat16),
    )


def attention_forward(packed, masks, score_scale):
    members = [split_crops(member) for member in unpack_heads(packed)]
    results = []
    logsums = []
    for which in range(2):
        result, logsum = forward_tile(
            members[0][which], members[1][which], members[2][which], masks[which], score_scale
        )
        results.append(result)
        logsums.append(logsum)
    return (join_crops(results[0], results[1]).reshape(STREAM, packed.shape[2]), logsums)


def attention_backward(packed, grad_attended, logsums, masks, score_scale):
    members = [split_crops(member) for member in unpack_heads(packed)]
    grad_parts = split_crops(grad_attended.reshape(GROUP_IMG, IMG_ROWS, -1, HEAD_DIM))
    tile_grads = [
        backward_tile(
            members[0][which],
            members[1][which],
            members[2][which],
            grad_parts[which],
            masks[which],
            logsums[which],
            score_scale,
        )
        for which in range(2)
    ]
    joined = [
        join_crops(tile_grads[0][member], tile_grads[1][member]).reshape(STREAM, packed.shape[2])
        for member in range(3)
    ]
    return jnp.stack(joined)


def on_device(
    tokens,
    attn_gain,
    attn_shift,
    in_weight,
    query_value_bias,
    proj_weight,
    proj_bias,
    attn_scale,
    mlp_gain,
    mlp_shift,
    up_weight,
    up_bias,
    down_weight,
    down_bias,
    mlp_scale,
    crop_lengths,
    out_grad,
):
    wide_size = lax.axis_size("wide")
    crop_groups = wide_size // HEAD_GROUPS
    block_rows = TOK_DEV // crop_groups
    head_width = D // HEAD_GROUPS
    score_scale = HEAD_DIM ** (-0.5)
    own_group = lax.axis_index("wide") // HEAD_GROUPS
    own_lengths = lax.dynamic_slice_in_dim(crop_lengths, own_group * GROUP_IMG, GROUP_IMG, 0)
    masks = key_masks(own_lengths)
    inputs = tokens.astype(jnp.float32)
    first_gain = attn_gain.astype(jnp.float32)
    first_shift = attn_shift.astype(jnp.float32)
    normed, first_back = jax.vjp(layer_norm, inputs, first_gain, first_shift)
    normed_low = normed.astype(jnp.bfloat16)
    normed_blocks = normed_low.reshape(crop_groups, block_rows, D)
    weight_in = in_weight.reshape(D, 3, HEAD_GROUPS, head_width)
    qv_rows = query_value_bias.astype(jnp.float32)
    full_bias = jnp.stack([qv_rows[0], jnp.zeros_like(qv_rows[0]), qv_rows[1]]).reshape(
        3, 1, HEAD_GROUPS, 1, head_width
    )
    projected = (
        jnp.einsum("gbd,dchk->cghbk", normed_blocks, weight_in, preferred_element_type=jnp.float32)
        + full_bias
    )
    send_heads = projected.astype(jnp.bfloat16).reshape(3, wide_size, block_rows, head_width)
    arrived = lax.all_to_all(send_heads, "wide", split_axis=1, concat_axis=1, tiled=True)
    packed = arrived.reshape(3, STREAM, head_width)
    attended, logsums = attention_forward(packed, masks, score_scale)
    returned = lax.all_to_all(
        attended.reshape(wide_size, block_rows, head_width),
        "wide",
        split_axis=0,
        concat_axis=0,
        tiled=True,
    )
    mixed_rows = returned.reshape(crop_groups, HEAD_GROUPS, block_rows, head_width)
    weight_proj = proj_weight.reshape(HEAD_GROUPS, head_width, D)
    branch = jnp.einsum(
        "ghbk,hkd->gbd", mixed_rows, weight_proj, preferred_element_type=jnp.float32
    )
    branch = branch.reshape(TOK_DEV, D) + proj_bias.astype(jnp.float32)
    first_scale = attn_scale.astype(jnp.float32)
    middle = inputs + first_scale * branch
    second, second_back = jax.vjp(
        layer_norm, middle, mlp_gain.astype(jnp.float32), mlp_shift.astype(jnp.float32)
    )
    second_low = second.astype(jnp.bfloat16)
    hidden = jnp.dot(second_low, up_weight, preferred_element_type=jnp.float32) + up_bias.astype(
        jnp.float32
    )
    activated, gelu_back = jax.vjp(gelu_exact, hidden)
    activated_low = activated.astype(jnp.bfloat16)
    outcome = jnp.dot(
        activated_low, down_weight, preferred_element_type=jnp.float32
    ) + down_bias.astype(jnp.float32)
    second_scale = mlp_scale.astype(jnp.float32)
    output = (middle + second_scale * outcome).astype(jnp.bfloat16)
    cotangent = out_grad.astype(jnp.float32)
    grad_mlp_scale = jnp.sum(cotangent * outcome, axis=0)
    grad_outcome = (cotangent * second_scale).astype(jnp.bfloat16)
    grad_down_weight = jnp.einsum(
        "tf,td->fd", activated_low, grad_outcome, preferred_element_type=jnp.float32
    )
    grad_down_bias = jnp.sum(grad_outcome.astype(jnp.float32), axis=0)
    grad_activated = jnp.einsum(
        "td,fd->tf", grad_outcome, down_weight, preferred_element_type=jnp.float32
    )
    grad_hidden = gelu_back(grad_activated)[0].astype(jnp.bfloat16)
    grad_up_weight = jnp.einsum(
        "td,tf->df", second_low, grad_hidden, preferred_element_type=jnp.float32
    )
    grad_up_bias = jnp.sum(grad_hidden.astype(jnp.float32), axis=0)
    grad_second = jnp.einsum(
        "tf,df->td", grad_hidden, up_weight, preferred_element_type=jnp.float32
    )
    grad_middle, grad_mlp_gain, grad_mlp_shift = second_back(grad_second)
    grad_middle = grad_middle + cotangent
    grad_attn_scale = jnp.sum(grad_middle * branch, axis=0)
    grad_branch = (grad_middle * first_scale).astype(jnp.bfloat16)
    branch_blocks = grad_branch.reshape(crop_groups, block_rows, D)
    grad_proj_weight = jnp.einsum(
        "ghbk,gbd->hkd", mixed_rows, branch_blocks, preferred_element_type=jnp.float32
    ).reshape(D, D)
    grad_proj_bias = jnp.sum(grad_branch.astype(jnp.float32), axis=0)
    grad_mixed = jnp.einsum(
        "gbd,hkd->ghbk", branch_blocks, weight_proj, preferred_element_type=jnp.float32
    )
    grad_mixed = grad_mixed.astype(jnp.bfloat16).reshape(wide_size, block_rows, head_width)
    again, grad_arrived = (
        lax.all_to_all(send_heads, "wide", split_axis=1, concat_axis=1, tiled=True),
        lax.all_to_all(grad_mixed[None], "wide", split_axis=1, concat_axis=1, tiled=True),
    )
    packed_back = again.reshape(3, STREAM, head_width)
    grad_attended = grad_arrived.reshape(STREAM, head_width)
    grad_packed = attention_backward(packed_back, grad_attended, logsums, masks, score_scale)
    grad_sent = lax.all_to_all(
        grad_packed.reshape(3, wide_size, block_rows, head_width),
        "wide",
        split_axis=1,
        concat_axis=1,
        tiled=True,
    )
    grad_heads = grad_sent.reshape(3, crop_groups, HEAD_GROUPS, block_rows, head_width)
    grad_in_weight = jnp.einsum(
        "gbd,cghbk->dchk", normed_blocks, grad_heads, preferred_element_type=jnp.float32
    ).reshape(D, 3 * D)
    bias_sums = jnp.sum(grad_heads.astype(jnp.float32), axis=(1, 3)).reshape(3, D)
    grad_query_value_bias = jnp.stack([bias_sums[0], bias_sums[2]])
    grad_normed = jnp.einsum(
        "cghbk,dchk->gbd", grad_heads, weight_in, preferred_element_type=jnp.float32
    ).reshape(TOK_DEV, D)
    grad_inputs, grad_attn_gain, grad_attn_shift = first_back(grad_normed)
    input_grad = (grad_inputs + grad_middle).astype(jnp.bfloat16)
    shares = (
        lax.psum_scatter(
            grad_attn_gain.astype(jnp.bfloat16), "wide", scatter_dimension=0, tiled=True
        ).astype(jnp.float32),
        lax.psum_scatter(
            grad_attn_shift.astype(jnp.bfloat16), "wide", scatter_dimension=0, tiled=True
        ).astype(jnp.float32),
        lax.psum_scatter(
            grad_in_weight.astype(jnp.bfloat16), "wide", scatter_dimension=0, tiled=True
        ).astype(jnp.float32),
        lax.psum_scatter(
            grad_query_value_bias.astype(jnp.bfloat16), "wide", scatter_dimension=1, tiled=True
        ).astype(jnp.float32),
        lax.psum_scatter(
            grad_proj_weight.astype(jnp.bfloat16), "wide", scatter_dimension=0, tiled=True
        ).astype(jnp.float32),
        lax.psum_scatter(
            grad_proj_bias.astype(jnp.bfloat16), "wide", scatter_dimension=0, tiled=True
        ).astype(jnp.float32),
        lax.psum_scatter(
            grad_attn_scale.astype(jnp.bfloat16), "wide", scatter_dimension=0, tiled=True
        ).astype(jnp.float32),
        lax.psum_scatter(
            grad_mlp_gain.astype(jnp.bfloat16), "wide", scatter_dimension=0, tiled=True
        ).astype(jnp.float32),
        lax.psum_scatter(
            grad_mlp_shift.astype(jnp.bfloat16), "wide", scatter_dimension=0, tiled=True
        ).astype(jnp.float32),
        lax.psum_scatter(
            grad_up_weight.astype(jnp.bfloat16), "wide", scatter_dimension=0, tiled=True
        ).astype(jnp.float32),
        lax.psum_scatter(
            grad_up_bias.astype(jnp.bfloat16), "wide", scatter_dimension=0, tiled=True
        ).astype(jnp.float32),
        lax.psum_scatter(
            grad_down_weight.astype(jnp.bfloat16), "wide", scatter_dimension=0, tiled=True
        ).astype(jnp.float32),
        lax.psum_scatter(
            grad_down_bias.astype(jnp.bfloat16), "wide", scatter_dimension=0, tiled=True
        ).astype(jnp.float32),
        lax.psum_scatter(
            grad_mlp_scale.astype(jnp.bfloat16), "wide", scatter_dimension=0, tiled=True
        ).astype(jnp.float32),
    )
    results = (
        lax.psum(shares[0].astype(jnp.bfloat16), "narrow").astype(jnp.float32),
        lax.psum(shares[1].astype(jnp.bfloat16), "narrow").astype(jnp.float32),
        lax.psum(shares[2].astype(jnp.bfloat16), "narrow").astype(jnp.float32),
        lax.psum(shares[3].astype(jnp.bfloat16), "narrow").astype(jnp.float32),
        lax.psum(shares[4].astype(jnp.bfloat16), "narrow").astype(jnp.float32),
        lax.psum(shares[5].astype(jnp.bfloat16), "narrow").astype(jnp.float32),
        lax.psum(shares[6].astype(jnp.bfloat16), "narrow").astype(jnp.float32),
        lax.psum(shares[7].astype(jnp.bfloat16), "narrow").astype(jnp.float32),
        lax.psum(shares[8].astype(jnp.bfloat16), "narrow").astype(jnp.float32),
        lax.psum(shares[9].astype(jnp.bfloat16), "narrow").astype(jnp.float32),
        lax.psum(shares[10].astype(jnp.bfloat16), "narrow").astype(jnp.float32),
        lax.psum(shares[11].astype(jnp.bfloat16), "narrow").astype(jnp.float32),
        lax.psum(shares[12].astype(jnp.bfloat16), "narrow").astype(jnp.float32),
        lax.psum(shares[13].astype(jnp.bfloat16), "narrow").astype(jnp.float32),
    )
    return (
        output,
        input_grad,
        results[0],
        results[1],
        results[2],
        results[3],
        results[4],
        results[5],
        results[6],
        results[7],
        results[8],
        results[9],
        results[10],
        results[11],
        results[12],
        results[13],
    )


MESH = pl.DeviceIdType.MESH
F32 = jnp.float32
BF16 = jnp.bfloat16
SLOT = 288
ROWS = 576
UNITS = 18
PAIRS = 9
BLOCK = 48
BLOCKS = ROWS // BLOCK
CORE, Y, X, Z1, Z2, Y_WHOLE, Y_BACK, CORE_BACK, DIAGONAL = range(9)
STAGES = {
    "A": (CORE, X, Z1, Z2, Y_WHOLE, CORE_BACK),
    "B": (CORE, Y, X, Z1, Z2, Y_BACK, CORE_BACK),
    "C": (CORE, Z1, Z2, X, Y_WHOLE, CORE_BACK),
    "D": (CORE, Y, Z1, Z2, X, Y_BACK, CORE_BACK),
    "E": (CORE, X, Y, Z1, Z2, Y_BACK, CORE_BACK),
}
AXES = (CORE, X, Y, Z1, Z2)
KINDS = "BBCADBEADBEBEEBEEE"
PLAN = (
    (),
    (),
    ((0, -1), (1, -1),),
    ((2, -1), (3, -1),),
    (),
    ((0, 0),),
    ((1, 0), (2, 0),),
    ((3, 0),),
    ((0, 1),),
    ((4, -1), (5, -1),),
    ((6, -1), (7, -1), (2, 1),),
    (),
    ((4, 0), (5, 0), (1, 1), (3, 1),),
    ((6, 0), (7, 0), (0, 2),),
    ((1, 2), (2, 2),),
    ((4, 1), (3, 2), (0, 3),),
    ((8, -1), (9, -1), (1, 3),),
    ((10, -1), (11, -1), (6, 1),),
    ((5, 1), (8, 0), (4, 2),),
    ((9, 0),),
    ((10, 0), (11, 0), (7, 1), (6, 2), (2, 3), (3, 3), (0, 4),),
    ((5, 2), (1, 4),),
    ((18, -1), (8, 1), (4, 3),),
    (),
    ((12, -1), (7, 2),),
    ((18, 0), (9, 1), (10, 1), (12, 0), (5, 3), (6, 3),),
    (),
    ((13, -1), (4, 4),),
    ((14, -1), (11, 1), (18, 1),),
    ((13, 0), (14, 0), (8, 2), (9, 2), (2, 4), (3, 4), (0, 5), (1, 5),),
    ((10, 2), (7, 3), (5, 4), (6, 4), (2, 5), (3, 5), (4, 5), (0, 6), (1, 6), (12, 1),),
    ((15, -1), (18, 2),),
    ((11, 2), (8, 3), (9, 3), (10, 3), (4, 6), (15, 0),),
    ((14, 1), (11, 3), (18, 3), (7, 4),),
    ((16, -1), (13, 1), (8, 4), (9, 4), (5, 5), (6, 5),),
    ((17, -1), (7, 5), (10, 4),),
    ((12, 2), (16, 0), (11, 4), (5, 6), (6, 6),),
    ((17, 0), (15, 1), (13, 2), (8, 5),),
    ((12, 3), (18, 4), (9, 5), (14, 2), (10, 5), (11, 5),),
    ((13, 3), (8, 6), (9, 6), (10, 6), (11, 6), (15, 2),),
    ((19, -1), (16, 1), (14, 3), (12, 4),),
    ((13, 4), (15, 3), (19, 0), (16, 2), (17, 1), (12, 5), (13, 5), (12, 6), (13, 6), (14, 4), (17, 2), (15, 4), (14, 5), (16, 3), (19, 1), (15, 5), (14, 6), (17, 3), (19, 2), (15, 6), (16, 4), (17, 4), (19, 3), (16, 5), (17, 5), (16, 6), (19, 4), (17, 6),),
)
ATTN_GAIN, ATTN_SHIFT, Q_BIAS, V_BIAS, PROJ_BIAS, ATTN_SCALE, MLP_GAIN, MLP_SHIFT, DOWN_BIAS, MLP_SCALE = range(10)
UP_BIAS = 10
EARLY_ROWS = (PROJ_BIAS, ATTN_SCALE, MLP_GAIN, MLP_SHIFT, DOWN_BIAS, MLP_SCALE)
LATE_ROWS = (ATTN_GAIN, ATTN_SHIFT, Q_BIAS, V_BIAS)


def dot_nn(a, b):
    return jnp.dot(a, b, preferred_element_type=F32)


def dot_nt(a, b):
    return lax.dot_general(a, b, (((1,), (1,)), ((), ())), preferred_element_type=F32)


def dot_tn(a, b):
    return lax.dot_general(a, b, (((0,), (0,)), ((), ())), preferred_element_type=F32)


def halves(block):
    lanes = lax.broadcasted_iota(jnp.int32, block.shape, 1)
    zero = jnp.zeros_like(block)
    return [jnp.where((lanes < 64) == (h == 0), block, zero) for h in range(2)]


def fold_rows(values):
    return jnp.sum(values.reshape(values.shape[0] // 8, 8, values.shape[1]), axis=0)


def norm_parts(values):
    mean = jnp.sum(values, axis=-1, keepdims=True) * (1.0 / D)
    centered = values - mean
    variance = jnp.sum(centered * centered, axis=-1, keepdims=True) * (1.0 / D)
    rstd = lax.rsqrt(variance + NORM_EPSILON)
    return centered * rstd, rstd


def layer_kernel(
    tok_ref, og_ref, len_ref,
    attn_gain_ref, attn_shift_ref, qv_ref, proj_bias_ref, attn_scale_ref, mlp_gain_ref, mlp_shift_ref,
    up_bias_ref, down_bias_ref, mlp_scale_ref,
    in_hbm, proj_hbm, up_hbm, down_hbm,
    out_hbm, ig_hbm, gin_ref, gproj_ref, gup_ref, gdown_ref, vout_ref,
    win, wproj, wup, wdown,
    xb, db, ob, h1, t1, t2, qkv, att, branch, mid, h2, dm, gact, dhid, macc, dacc, ub, gb, bias, bias_t,
    prm, qkv_row, sums, usums,
    gbuf, r0, r1, r2, r3, r4, fin, wdt, early, early_in, late, late_in,
    wsem, upsem, lsem, hsend, hrecv, ssem, rsem, vssem, vrsem,
):
    n = lax.axis_index("narrow")
    w = lax.axis_index("wide")
    c = n % 2
    y = n // 2
    x = w % 2
    z1 = (w // 2) % 2
    z2 = w // 4
    quarter = w % 4
    shift = 32 * (quarter % 2) + 32 * (quarter // 2) * (2 - 2 * (quarter % 2)) + 0 * quarter
    partner = {
        CORE: (n + 1 - 2 * c, w),
        Y: (n + 2 - 4 * y, w),
        X: (n, w + 1 - 2 * x),
        Z1: (n, w + 2 - 4 * z1),
        Z2: (n, w + 4 - 8 * z2),
        DIAGONAL: (n, w + 3 - 2 * quarter),
    }

    weights = [
        pltpu.make_async_copy(in_hbm, win, wsem.at[0]),
        pltpu.make_async_copy(proj_hbm, wproj, wsem.at[1]),
    ]
    downs = [pltpu.make_async_copy(down_hbm.at[:, j], wdown.at[j], wsem.at[2 + j]) for j in range(3)]
    ups = [
        [
            pltpu.make_async_copy(
                up_hbm.at[:, 128 * (3 * s + j) : 128 * (3 * s + j + 1)],
                wup.at[:, 128 * (8 * j + s) : 128 * (8 * j + s + 1)],
                upsem.at[j],
            )
            for s in range(8)
        ]
        for j in range(3)
    ]
    own = pl.ds(pl.multiple_of(64 - shift, 32), 256)
    loads = [
        pltpu.make_async_copy(tok_ref, xb.at[:, own], lsem.at[0]),
        pltpu.make_async_copy(og_ref, db.at[:, own], lsem.at[1]),
    ]
    loads[0].start()
    weights[0].start()
    loads[1].start()
    weights[1].start()
    for j in range(3):
        for s in range(8):
            ups[j][s].start()
        downs[j].start()

    barrier = pltpu.get_barrier_semaphore()
    for target in partner.values():
        pl.semaphore_signal(barrier, inc=1, device_id=target, device_id_type=MESH)

    before_shift = 32 * ((quarter + 3) % 2) + 32 * ((quarter - 1) // 2) * (2 - 2 * ((quarter + 3) % 2))
    before = (n, w - 1)
    after = (n, w + 1)

    def halo_in(src, dst, k):
        return pltpu.make_async_remote_copy(
            src_ref=src.at[:, 0:64],
            dst_ref=dst.at[:, pl.ds(pl.multiple_of(320 - before_shift, 32), 64)],
            send_sem=hsend.at[k], recv_sem=hrecv.at[k], device_id=before, device_id_type=MESH,
        )

    def halo_back(buf, k, size):
        return pltpu.make_async_remote_copy(
            src_ref=buf.at[:, pl.ds(pl.multiple_of(320 - shift, 32), size)],
            dst_ref=buf.at[:, 64 - size : 64],
            send_sem=hsend.at[k], recv_sem=hrecv.at[k], device_id=after, device_id_type=MESH,
        )

    for row, ref in (
        (ATTN_GAIN, attn_gain_ref), (ATTN_SHIFT, attn_shift_ref), (PROJ_BIAS, proj_bias_ref), (ATTN_SCALE, attn_scale_ref),
        (MLP_GAIN, mlp_gain_ref), (MLP_SHIFT, mlp_shift_ref), (DOWN_BIAS, down_bias_ref), (MLP_SCALE, mlp_scale_ref),
    ):
        prm[row : row + 1, 0:D] = ref[...].astype(F32).reshape(1, D)
    qv = qv_ref[...].astype(F32)
    qkv_row[:, 0:D] = qv[0:1]
    qkv_row[:, D : 2 * D] = jnp.zeros((1, D), F32)
    qkv_row[:, 2 * D : 3 * D] = qv[1:2]
    up_row = up_bias_ref[...].astype(F32).reshape(1, 4 * D)
    for j in range(3):
        for s in range(8):
            prm[UP_BIAS + j : UP_BIAS + j + 1, 128 * s : 128 * (s + 1)] = up_row[:, 128 * (3 * s + j) : 128 * (3 * s + j + 1)]
    sums[...] = jnp.zeros_like(sums)
    usums[...] = jnp.zeros_like(usums)

    def param(row):
        return prm[row : row + 1, 0:D]

    is_local = quarter // 2
    for i in range(2):
        image = 2 * i + z2

        def crop_of(axis, valid_only):
            shape = (1, SLOT) if axis == 1 else (SLOT, 1)
            place = lax.broadcasted_iota(jnp.int32, shape, axis)
            ids = jnp.full(shape, -1 if valid_only else 4, jnp.int32)
            for m in range(4):
                start = 56 * m * is_local
                if valid_only:
                    local_length = len_ref[image, 2 + 4 * (quarter % 2) + m]
                    global_length = len_ref[image, quarter % 2] if m == 0 else 0
                    size = is_local * local_length + (1 - is_local) * global_length
                else:
                    size = 56 * is_local + (1 - is_local) * (SLOT if m == 0 else 0)
                inside = jnp.logical_and(place >= start, place < start + size)
                ids = jnp.where(inside, m, ids)
            return ids

        bias[i] = jnp.where(crop_of(0, False) == crop_of(1, True), 0.0, MASKED)
        bias_t[i] = jnp.where(crop_of(1, False) == crop_of(0, True), 0.0, MASKED)

    pl.semaphore_wait(barrier, 6)

    @pl.when(quarter > 0)
    def _():
        halo_in(tok_ref, xb, 0).start()
        halo_in(og_ref, db, 1).start()

    def take_halo(src, dst, k):
        @pl.when(quarter > 0)
        def _():
            halo_in(src, dst, k).wait_send()

        @pl.when(quarter < 3)
        def _():
            halo_in(src, dst, k).wait_recv()

        @pl.when(quarter > 1)
        def _():
            dst[:, 288:352] = jnp.zeros((2, 64, D), BF16)

    def at(b):
        i, k = b // 6, b % 6
        return i, pl.ds(pl.multiple_of(64 + BLOCK * k, 16), BLOCK), pl.ds(pl.multiple_of(BLOCK * b, 16), BLOCK)

    def first_norm(b):
        i, slots, rows = at(b)
        normed, _ = norm_parts(xb[i, slots].astype(F32))
        h1[rows] = (normed * param(ATTN_GAIN) + param(ATTN_SHIFT)).astype(BF16)

    def project(low, high):
        rows = jnp.concatenate([h1[SLOT * i + low : SLOT * i + high] for i in range(2)], axis=0)

        def tile_of(tile, _):
            cols = pl.ds(pl.multiple_of(256 * tile, 256), 256)
            result = (dot_nn(rows, win[:, cols]) + qkv_row[:, cols]).astype(BF16)
            result = jnp.where(tile < 3, result * jnp.asarray(0.125, BF16), result)
            for i in range(2):
                qkv[SLOT * i + low : SLOT * i + high, cols] = result[(high - low) * i : (high - low) * (i + 1)]
            return 0

        lax.fori_loop(0, 9, tile_of, 0, unroll=3)

    loads[0].wait()
    for b in (0, 1, 2, 3, 6, 7, 8, 9):
        first_norm(b)
    weights[0].wait()
    project(0, 192)
    take_halo(tok_ref, xb, 0)
    for b in (4, 5, 10, 11):
        first_norm(b)
    project(192, SLOT)

    def pair_at(index):
        i, h = index % 2, index // 2
        rows = pl.ds(pl.multiple_of(SLOT * i, 16), SLOT)
        return i, rows, [pl.ds(pl.multiple_of(D * m + 128 * h, 128), 128) for m in range(3)]

    def attend(index, _):
        i, rows, cols = pair_at(index)
        q, v = qkv[rows, cols[0]], qkv[rows, cols[2]]
        keys = halves(qkv[rows, cols[1]])
        lanes = lax.broadcasted_iota(jnp.int32, (SLOT, 128), 1)
        ones = jnp.ones_like(v)
        parts = []
        for h in range(2):
            s = dot_nt(q, keys[h]) + bias[i]
            e = jnp.exp(s - jnp.max(s, axis=-1, keepdims=True)).astype(BF16)
            part = dot_nn(e, jnp.where((lanes < 64) == (h == 0), v, ones))
            parts.append(part / pltpu.roll(part, 64, 1))
        att[rows, cols[0]] = jnp.where(lanes < 64, parts[0], parts[1]).astype(BF16)
        return 0

    lax.fori_loop(0, 12, attend, 0, unroll=2)

    weights[1].wait()
    for tile in range(3):
        cols = slice(256 * tile, 256 * (tile + 1))
        result = dot_nn(att[...], wproj[:, cols]) + prm[PROJ_BIAS : PROJ_BIAS + 1, cols]
        branch[:, cols] = result.astype(BF16)
        scaled = prm[ATTN_SCALE : ATTN_SCALE + 1, cols] * result
        for i in range(2):
            mid[SLOT * i : SLOT * (i + 1), cols] = (
                xb[i, 64 : 64 + SLOT, cols].astype(F32) + scaled[SLOT * i : SLOT * (i + 1)]
            )

    loads[1].wait()
    take_halo(og_ref, db, 1)

    def second_norm(b, _):
        i, slots, rows = at(b)
        low = (db[i, slots].astype(F32) * param(MLP_SCALE)).astype(BF16)
        dm[rows] = low
        sums[DOWN_BIAS] += fold_rows(low.astype(F32))
        normed, _ = norm_parts(mid[rows])
        h2[rows] = (normed * param(MLP_GAIN) + param(MLP_SHIFT)).astype(BF16)
        return 0

    lax.fori_loop(0, BLOCKS, second_norm, 0, unroll=3)

    def transpose_into(dst, src):
        for k in range(6):
            dst[128 * k : 128 * (k + 1)] = src[:, 128 * k : 128 * (k + 1)].T

    def copy(src, dst, unit, stage, axis):
        return pltpu.make_async_remote_copy(
            src_ref=src, dst_ref=dst,
            send_sem=ssem.at[unit % ssem.shape[0], stage], recv_sem=rsem.at[unit % rsem.shape[0], stage],
            device_id=partner[axis], device_id_type=MESH,
        )

    bits = {CORE: c, Y: y, X: x, Z1: z1, Z2: z2}
    over = {Y_WHOLE: Y, Y_BACK: Y, CORE_BACK: CORE}
    landing = (r0, r1, r2, r3, r4)

    def share(u, letter, k, mine):
        stages = STAGES[letter]
        index = [u]
        for axis in bits:
            if axis in stages[:k]:
                index.append(bits[axis])
            elif axis == stages[k]:
                index.append(bits[axis] if mine else 1 - bits[axis])
            else:
                index.append(slice(None))
        return gbuf.at[tuple(index)]

    def transfer(u, letter, k):
        stage = STAGES[letter][k]
        slot = u % fin.shape[0]
        if stage == CORE_BACK:
            return copy(fin.at[slot, c], fin.at[slot, c], u, k, CORE)
        if stage == Y_BACK:
            return copy(fin.at[slot, c, y], fin.at[slot, c, y], u, k, Y)
        dst = landing[k].at[u % landing[k].shape[0]]
        if k == 4 and stage != Y_WHOLE:
            dst = dst.at[0]
        return copy(share(u, letter, k, False), dst, u, k, over.get(stage, stage))

    def add(dst, src):
        dst[...] = (dst[...].astype(F32) + src[...].astype(F32)).astype(BF16)

    def land(u, letter, k):
        stage = STAGES[letter][k]
        if stage in (Y_BACK, CORE_BACK):
            return
        slot = u % fin.shape[0]
        src = landing[k].at[u % landing[k].shape[0]]
        own = share(u, letter, k, True)
        if k == 0:

            def body(index, _):
                add(own.at[index // 2, index % 2], src.at[index // 2, index % 2])
                return 0

            lax.fori_loop(0, 4, body, 0)
        elif k < 4:
            add(own, src)
        elif stage == Y_WHOLE:
            fin[slot, c] = (own[...].astype(F32) + src[...].astype(F32)).astype(BF16)
        else:
            fin[slot, c, y] = (own[...].astype(F32) + src[0].astype(F32)).astype(BF16)

    def in_tile(index):
        return 3 * ((index - 3) % 3) + (index - 3) // 3

    def write_out(u):
        p, a = u // 2, u % 2
        slot = u % fin.shape[0]
        for sub in range(4):
            block = fin[slot, sub // 2, sub % 2]
            if p >= 6:
                index = 2 * (u - 12) + sub // 2
                dst, tile = (gproj_ref, index) if index < 3 else (gin_ref, in_tile(index))
                start = 256 * tile + 128 * (sub % 2)
                dst[:, start : start + 128] = block
            elif p % 2 == 1:
                start = 128 * (3 * (4 * a + sub) + p // 2)
                gup_ref[:, start : start + 128] = block
            else:
                wdt[384 * a + 96 * sub : 384 * a + 96 * (sub + 1), 64 * p : 64 * p + 128] = block

    def vector_event(buf, arrived, which, k):
        def exchange(stage):
            return pltpu.make_async_remote_copy(
                src_ref=buf.at[stage], dst_ref=arrived.at[stage], send_sem=vssem.at[which, stage],
                recv_sem=vrsem.at[which, stage], device_id=partner[AXES[stage]], device_id_type=MESH,
            )

        if k >= 0:
            exchange(k).wait()
            buf[k + 1] = (buf[k].astype(F32) + arrived[k].astype(F32)).astype(buf.dtype)
        if k < 4:
            exchange(k + 1).start()

    def event(u, k):
        if u >= UNITS:
            vector_event((early, late)[u - UNITS], (early_in, late_in)[u - UNITS], u - UNITS, k)
            return
        letter = KINDS[u]
        if k >= 0:
            transfer(u, letter, k).wait()
            land(u, letter, k)
        if k + 1 < len(STAGES[letter]):
            transfer(u, letter, k + 1).start()
        else:
            write_out(u)

    polls = iter(PLAN)

    def poll():
        for u, k in next(polls):
            event(u, k)

    transpose_into(t1, dm)

    def gelu_block(j, tile, b):
        _, _, rows = at(b)
        cols = pl.ds(pl.multiple_of(256 * tile, 256), 256)
        u = ub[rows] + prm[pl.ds(UP_BIAS + j, 1), cols]
        phi = 0.5 * (1.0 + lax.erf(u * 0.7071067811865476))
        gact[rows, cols] = (u * phi).astype(BF16)
        slope = phi + u * (jnp.exp(u * u * -0.5) * 0.3989422804014327)
        low = (gb[rows] * slope).astype(BF16)
        dhid[rows, cols] = low
        usums[:, pl.ds(pl.multiple_of(1024 * j + 256 * tile, 256), 256)] += fold_rows(low.astype(F32))

    def mlp(j):
        part = wup.at[:, 1024 * j : 1024 * (j + 1)]
        pltpu.make_async_copy(up_hbm.at[:, 0:1024], part, upsem.at[j]).wait()
        downs[j].wait()

        def hidden_tile(tile, _):
            cols = pl.ds(pl.multiple_of(1024 * j + 256 * tile, 256), 256)
            ub[...] = dot_nn(h2[...], wup[:, cols])
            down = wdown[j, pl.ds(2 * tile, 2)].reshape(256, D)
            gb[...] = dot_nt(dm[...], down)

            def block(b, _):
                gelu_block(j, tile, b)
                return 0

            lax.fori_loop(0, BLOCKS, block, 0, unroll=3)
            return 0

        def down_grad(nt, _):
            result = dot_nn(t1[...], gact[:, pl.ds(pl.multiple_of(256 * nt, 256), 256)])
            for ss in range(2):
                for sub in range(8):
                    gbuf[4 * j + sub // 4, (sub // 2) % 2, sub % 2, ss, nt % 2, nt // 2] = result[
                        96 * sub : 96 * (sub + 1), 128 * ss : 128 * (ss + 1)
                    ].astype(BF16)
            return 0

        def up_grad(nt, _):
            result = dot_nn(t2[...], dhid[:, pl.ds(pl.multiple_of(256 * nt, 256), 256)])
            for s in range(8):
                for yy in range(2):
                    gbuf[4 * j + 2 + nt // 2, nt % 2, yy, s % 2, (s // 2) % 2, s // 4] = result[
                        96 * s : 96 * (s + 1), 128 * yy : 128 * (yy + 1)
                    ].astype(BF16)
            return 0

        def combine(nt):
            cols = slice(256 * nt, 256 * (nt + 1))
            more = dot_nn(gact[...], wdown[j, :, :, cols].reshape(1024, 256))
            more_d = dot_nt(dhid[...], wup[cols, 1024 * j : 1024 * (j + 1)])
            macc[:, cols] = more if j == 0 else macc[:, cols] + more
            dacc[:, cols] = more_d if j == 0 else dacc[:, cols] + more_d

        lax.fori_loop(0, 2, hidden_tile, 0)
        poll()
        lax.fori_loop(2, 4, hidden_tile, 0)
        poll()
        lax.fori_loop(0, 4, down_grad, 0, unroll=2)
        poll()
        if j == 0:
            transpose_into(t2, h2)
        lax.fori_loop(0, 4, up_grad, 0, unroll=2)
        poll()
        for nt in range(3):
            combine(nt)
            poll()

    for j in range(3):
        mlp(j)

    transpose_into(t1, h1)
    transpose_into(t2, att)

    def second_back(b, _):
        i, slots, rows = at(b)
        grad = db[i, slots].astype(F32)
        y_rows = mid[rows]
        outcome = macc[rows] + param(DOWN_BIAS)
        ob[i, slots] = (y_rows + param(MLP_SCALE) * outcome).astype(BF16)
        sums[MLP_SCALE] += fold_rows(grad * outcome)
        normed, rstd = norm_parts(y_rows)
        dh = dacc[rows]
        sums[MLP_GAIN] += fold_rows(dh * normed)
        sums[MLP_SHIFT] += fold_rows(dh)
        e = dh * param(MLP_GAIN)
        mean_e = jnp.sum(e, axis=-1, keepdims=True) * (1.0 / D)
        mean_en = jnp.sum(e * normed, axis=-1, keepdims=True) * (1.0 / D)
        dy = grad + rstd * (e - mean_e - normed * mean_en)
        dacc[rows] = dy
        sums[ATTN_SCALE] += fold_rows(dy * branch[rows].astype(F32))
        low = (dy * param(ATTN_SCALE)).astype(BF16)
        dm[rows] = low
        sums[PROJ_BIAS] += fold_rows(low.astype(F32))
        return 0

    lax.fori_loop(0, 6, second_back, 0, unroll=2)
    poll()
    lax.fori_loop(6, BLOCKS, second_back, 0, unroll=2)

    def give_back(buf, k):
        @pl.when(quarter % 2 == 0)
        def _():
            halo_back(buf, k, 32).start()

        @pl.when(quarter == 1)
        def _():
            halo_back(buf, k, 64).start()

    def take_back(buf, k):
        @pl.when(quarter % 2 == 0)
        def _():
            halo_back(buf, k, 32).wait_send()

        @pl.when(quarter == 1)
        def _():
            halo_back(buf, k, 64).wait_send()

        @pl.when(quarter % 2 == 1)
        def _():
            halo_back(buf, k, 32).wait_recv()

        @pl.when(quarter == 2)
        def _():
            halo_back(buf, k, 64).wait_recv()

    give_back(ob, 2)
    rows = [jnp.sum(sums[row], axis=0, keepdims=True) for row in EARLY_ROWS]
    for index, row in enumerate(rows):
        early[0, index : index + 1, 0:D] = row.astype(BF16)
    for j in range(3):
        early[0, 6 + j : 7 + j] = jnp.sum(usums[:, 1024 * j : 1024 * (j + 1)], axis=0, keepdims=True).astype(BF16)
    poll()

    for tile in range(3):
        cols = slice(256 * tile, 256 * (tile + 1))
        h2[:, cols] = dot_nt(dm[...], wproj[cols]).astype(BF16)

    def attend_back(index, _):
        i, rows, cols = pair_at(index)
        k, v = qkv[rows, cols[1]], qkv[rows, cols[2]]
        queries, keys, grads = halves(qkv[rows, cols[0]]), halves(k), halves(h2[rows, cols[0]])
        dq = dk = dv = None
        for h in range(2):
            s = dot_nt(k, queries[h]) + bias_t[i]
            e = jnp.exp(s - jnp.max(s, axis=0, keepdims=True))
            p = e * (1.0 / jnp.sum(e, axis=0, keepdims=True))
            dp = dot_nt(v, grads[h])
            ds = (p * (dp - jnp.sum(p * dp, axis=0, keepdims=True))).astype(BF16)
            parts = dot_tn(ds, keys[h]), dot_nn(ds, queries[h]), dot_nn(p.astype(BF16), grads[h])
            dq, dk, dv = parts if dq is None else (dq + parts[0], dk + parts[1], dv + parts[2])
        low_q, low_v = (dq * 0.125).astype(BF16), dv.astype(BF16)
        qkv[rows, cols[0]] = low_q
        qkv[rows, cols[1]] = dk.astype(BF16)
        qkv[rows, cols[2]] = low_v
        sums[Q_BIAS, :, cols[0]] += fold_rows(low_q.astype(F32))
        sums[V_BIAS, :, cols[0]] += fold_rows(low_v.astype(F32))
        return 0

    def attn_grad(u):
        for half in range(2):
            index = 2 * (u - 12) + half
            if index < 3:
                result = dot_nn(t2[...], dm[:, 256 * index : 256 * (index + 1)])
            else:
                result = dot_nn(t1[...], qkv[:, 256 * in_tile(index) : 256 * (in_tile(index) + 1)])
            for s in range(8):
                for yy in range(2):
                    gbuf[u, half, yy, s % 2, (s // 2) % 2, s // 4] = result[
                        96 * s : 96 * (s + 1), 128 * yy : 128 * (yy + 1)
                    ].astype(BF16)
        poll()

    poll()
    attn_grad(12)
    for m in range(3):
        lax.fori_loop(4 * m, 4 * m + 2, attend_back, 0)
        poll()
        lax.fori_loop(4 * m + 2, 4 * m + 4, attend_back, 0)
        poll()
        for u in ((13, 14), (15,), (16, 17))[m]:
            attn_grad(u)

    for tile in range(3):
        cols = slice(256 * tile, 256 * (tile + 1))
        macc[:, cols] = dot_nt(qkv[...], win[cols])
        poll()

    def first_back(b, _):
        i, slots, rows = at(b)
        normed, rstd = norm_parts(xb[i, slots].astype(F32))
        dh = macc[rows]
        sums[ATTN_GAIN] += fold_rows(dh * normed)
        sums[ATTN_SHIFT] += fold_rows(dh)
        e = dh * param(ATTN_GAIN)
        mean_e = jnp.sum(e, axis=-1, keepdims=True) * (1.0 / D)
        mean_en = jnp.sum(e * normed, axis=-1, keepdims=True) * (1.0 / D)
        db[i, slots] = (dacc[rows] + rstd * (e - mean_e - normed * mean_en)).astype(BF16)
        return 0

    lax.fori_loop(0, 6, first_back, 0, unroll=2)
    poll()
    lax.fori_loop(6, BLOCKS, first_back, 0, unroll=2)
    give_back(db, 3)

    late[0] = jnp.zeros_like(late[0])
    for index, row in enumerate(LATE_ROWS):
        late[0, index : index + 1] = jnp.sum(sums[row], axis=0, keepdims=True)
    poll()
    poll()

    turn = (D - 96 * w) % D
    vout_ref[0:6] = pltpu.roll(early[5, :, 0:D].astype(F32), turn, 1)[0:6, 0:128]
    vout_ref[6:9] = early[5, 6:9, pl.ds(pl.multiple_of(128 * w, 128), 128)].astype(F32)
    vout_ref[16:24] = pltpu.roll(late[5], turn, 1)[:, 0:128]

    for a in range(3):
        for b in range(6):
            gdown_ref[128 * a : 128 * (a + 1), 128 * b : 128 * (b + 1)] = wdt[
                128 * b : 128 * (b + 1), 128 * a : 128 * (a + 1)
            ].T

    take_back(ob, 2)
    take_back(db, 3)
    stores = [
        pltpu.make_async_copy(ob.at[:, own], out_hbm, lsem.at[0]),
        pltpu.make_async_copy(db.at[:, own], ig_hbm, lsem.at[1]),
    ]
    for store in stores:
        store.start()
    for store in stores:
        store.wait()


def layer(tokens, out_grad, lengths, vectors, weights):
    vm = pl.BlockSpec(memory_space=pltpu.VMEM)
    hbm = pl.BlockSpec(memory_space=pl.ANY)
    dma = pltpu.SemaphoreType.DMA
    slots = pltpu.VMEM((2, 384, D), BF16)
    square = pltpu.VMEM((ROWS, D), BF16)
    wide_square = pltpu.VMEM((ROWS, D), F32)
    block = (96, 128)
    return pl.pallas_call(
        layer_kernel,
        out_shape=(
            jax.ShapeDtypeStruct((2, 256, D), BF16),
            jax.ShapeDtypeStruct((2, 256, D), BF16),
            jax.ShapeDtypeStruct((96, 3 * D), BF16),
            jax.ShapeDtypeStruct((96, D), BF16),
            jax.ShapeDtypeStruct((96, 4 * D), BF16),
            jax.ShapeDtypeStruct((384, D), BF16),
            jax.ShapeDtypeStruct((24, 128), F32),
        ),
        in_specs=[hbm, hbm, pl.BlockSpec(memory_space=pltpu.SMEM)] + [vm] * 10 + [hbm] * 4,
        out_specs=(hbm, hbm, vm, vm, vm, vm, vm),
        scratch_shapes=[
            pltpu.VMEM((D, 3 * D), BF16),
            pltpu.VMEM((D, D), BF16),
            pltpu.VMEM((D, 4 * D), BF16),
            pltpu.VMEM((3, 8, 128, D), BF16),
            slots, slots, slots,
            square,
            pltpu.VMEM((D, ROWS), BF16),
            pltpu.VMEM((D, ROWS), BF16),
            pltpu.VMEM((ROWS, 3 * D), BF16),
            square, square,
            wide_square,
            square, square,
            pltpu.VMEM((ROWS, 1024), BF16),
            pltpu.VMEM((ROWS, 1024), BF16),
            wide_square, wide_square,
            pltpu.VMEM((ROWS, 256), F32),
            pltpu.VMEM((ROWS, 256), F32),
            pltpu.VMEM((2, SLOT, SLOT), F32),
            pltpu.VMEM((2, SLOT, SLOT), F32),
            pltpu.VMEM((16, 1024), F32),
            pltpu.VMEM((1, 3 * D), F32),
            pltpu.VMEM((10, 8, D), F32),
            pltpu.VMEM((8, 4 * D), F32),
            pltpu.VMEM((UNITS, 2, 2, 2, 2, 2) + block, BF16),
            pltpu.VMEM((8, 2, 2, 2, 2) + block, BF16),
            pltpu.VMEM((12, 2, 2, 2) + block, BF16),
            pltpu.VMEM((8, 2, 2) + block, BF16),
            pltpu.VMEM((12, 2) + block, BF16),
            pltpu.VMEM((12, 2) + block, BF16),
            pltpu.VMEM((12, 2, 2) + block, BF16),
            pltpu.VMEM((D, 384), BF16),
            pltpu.VMEM((6, 16, 1024), BF16),
            pltpu.VMEM((5, 16, 1024), BF16),
            pltpu.VMEM((6, 8, D), F32),
            pltpu.VMEM((5, 8, D), F32),
            dma((5,)), dma((3,)), dma((2,)), dma((4,)), dma((4,)),
            dma((12, 7)), dma((12, 7)), dma((2, 5)), dma((2, 5)),
        ],
        compiler_params=pltpu.CompilerParams(collective_id=0, has_side_effects=True, vmem_limit_bytes=64 << 20),
        name="layer",
    )(tokens, out_grad, lengths, *vectors, *weights)


def finish_kernel(
    out_in, ig_in, in_ref, proj_ref, up_ref, down_ref, v_ref,
    out_ref, ig_ref, ag_ref, as_ref, gin_ref, qv_ref, gproj_ref, pb_ref, sc_ref, mg_ref, ms_ref, gup_ref, ub_ref,
    gdown_ref, bd_ref, sm_ref,
):
    out_ref[...] = out_in[...]
    ig_ref[...] = ig_in[...]
    for src, dst in ((in_ref, gin_ref), (proj_ref, gproj_ref), (up_ref, gup_ref), (down_ref, gdown_ref)):
        dst[...] = src[...].astype(F32)
    for row, dst in zip((0, 1, 2, 3, 4, 5, 16, 17), (pb_ref, sc_ref, mg_ref, ms_ref, bd_ref, sm_ref, ag_ref, as_ref)):
        dst[...] = v_ref[row, 0:96]
    qv_ref[...] = v_ref[18:20, 0:96]
    for j in range(3):
        ub_ref[128 * j : 128 * (j + 1)] = v_ref[6 + j]


def finish(output, input_grad, g_in, g_proj, g_up, g_down, v):
    vm = pl.BlockSpec(memory_space=pltpu.VMEM)
    row = jax.ShapeDtypeStruct((96,), F32)

    def wide(shape):
        return jax.ShapeDtypeStruct(shape, F32)

    rows = jax.ShapeDtypeStruct((TOK_DEV, D), BF16)
    return pl.pallas_call(
        finish_kernel,
        out_shape=(
            rows, rows, row, row, wide((96, 3 * D)), wide((2, 96)), wide((96, D)), row, row, row, row, wide((96, 4 * D)),
            wide((384,)), wide((384, D)), row, row,
        ),
        in_specs=[vm] * 7,
        out_specs=(vm,) * 16,
        name="finish",
    )(output.reshape(TOK_DEV, D), input_grad.reshape(TOK_DEV, D), g_in, g_proj, g_up, g_down, v)


def on_device_local(
    tokens, attn_gain, attn_shift, in_weight, query_value_bias, proj_weight, proj_bias, attn_scale,
    mlp_gain, mlp_shift, up_weight, up_bias, down_weight, down_bias, mlp_scale, crop_lengths, out_grad,
):
    output, input_grad, g_in, g_proj, g_up, g_down, v = layer(
        tokens.reshape(2, 256, D), out_grad.reshape(2, 256, D), crop_lengths,
        (attn_gain, attn_shift, query_value_bias, proj_bias, attn_scale, mlp_gain, mlp_shift, up_bias, down_bias, mlp_scale),
        (in_weight, proj_weight, up_weight, down_weight.reshape(8, 3, 128, D)),
    )
    return finish(output, input_grad, g_in, g_proj, g_up, g_down, v)


def solution(mesh):
    local = mesh.shape["wide"] == 8 and mesh.shape["narrow"] == 4
    return jax.shard_map(
        on_device_local if local else on_device,
        mesh=mesh,
        in_specs=(
            P(("narrow", "wide"), None),
            P(),
            P(),
            P(),
            P(),
            P(),
            P(),
            P(),
            P(),
            P(),
            P(),
            P(),
            P(),
            P(),
            P(),
            P("narrow", None),
            P(("narrow", "wide"), None),
        ),
        out_specs=(
            P(("narrow", "wide"), None),
            P(("narrow", "wide"), None),
            P("wide"),
            P("wide"),
            P("wide", None),
            P(None, "wide"),
            P("wide", None),
            P("wide"),
            P("wide"),
            P("wide"),
            P("wide"),
            P("wide", None),
            P("wide"),
            P("wide", None),
            P("wide"),
            P("wide"),
        ),
        check_vma=False,
    )
```

```python
import jax
import jax.numpy as jnp
from jax import lax
from jax.experimental import pallas as pl
from jax.experimental.pallas import tpu as pltpu
from jax.sharding import PartitionSpec as P

D = 768
HEAD_DIM = 64
HEAD_GROUPS = 4
GSLOT = 288
LSLOT = 56
GROUP_IMG = 2
IMG_ROWS = 1024
STREAM = 2048
TOK_DEV = 512


NORM_EPSILON = 1e-06
MASKED = -1e30


def layer_norm(values, gain_row, shift_row):
    row_mean = jnp.mean(values, axis=-1, keepdims=True)
    centered = values - row_mean
    variance = jnp.mean(centered * centered, axis=-1, keepdims=True)
    return centered * lax.rsqrt(variance + NORM_EPSILON) * gain_row + shift_row


def gelu_exact(values):
    return 0.5 * values * (1.0 + jax.scipy.special.erf(values * 0.7071067811865476))


def key_masks(lengths):
    positions = jnp.arange(GSLOT, dtype=jnp.int32)
    global_valid = positions[None, None, :] < lengths[:, :2, None]
    global_valid = global_valid.reshape(GROUP_IMG * 2, 1, 1, GSLOT)
    row_ids = jnp.arange(8 * LSLOT, dtype=jnp.int32)
    crop_ids = row_ids // LSLOT
    offsets = row_ids % LSLOT
    local_lengths = jnp.repeat(lengths[:, 2:], LSLOT, axis=1)
    same_crop = crop_ids[:, None] == crop_ids[None, :]
    local_valid = same_crop[None] & (offsets[None, None, :] < local_lengths[:, None, :])
    return (global_valid, local_valid[:, None])


def split_crops(values):
    global_part = values[:, : 2 * GSLOT].reshape(
        GROUP_IMG * 2, GSLOT, values.shape[2], values.shape[3]
    )
    return (global_part, values[:, 2 * GSLOT :])


def join_crops(global_part, local_part):
    widened = global_part.reshape(GROUP_IMG, 2 * GSLOT, local_part.shape[2], local_part.shape[3])
    return jnp.concatenate([widened, local_part], axis=1)


def unpack_heads(packed):
    per_group = packed.shape[2] // HEAD_DIM
    return [packed[which].reshape(GROUP_IMG, IMG_ROWS, per_group, HEAD_DIM) for which in range(3)]


def tile_logits(queries, key_rows, key_mask, score_scale):
    raw = (
        jnp.einsum("bqhk,bshk->bhqs", queries, key_rows, preferred_element_type=jnp.float32)
        * score_scale
    )
    return jnp.where(key_mask, raw, MASKED)


def forward_tile(queries, key_rows, values, key_mask, score_scale):
    logits = tile_logits(queries, key_rows, key_mask, score_scale)
    row_max = jnp.max(logits, axis=-1, keepdims=True)
    exponent = jnp.exp(logits - row_max)
    row_total = jnp.sum(exponent, axis=-1, keepdims=True)
    weights = (exponent / row_total).astype(jnp.bfloat16)
    result = jnp.einsum("bhqs,bshk->bqhk", weights, values, preferred_element_type=jnp.float32)
    return (result.astype(jnp.bfloat16), row_max + jnp.log(row_total))


def backward_tile(queries, key_rows, values, grad_out, key_mask, logsum, score_scale):
    logits = tile_logits(queries, key_rows, key_mask, score_scale)
    probabilities = jnp.exp(logits - logsum)
    grad_probs = jnp.einsum("bqhk,bshk->bhqs", grad_out, values, preferred_element_type=jnp.float32)
    inner = jnp.sum(probabilities * grad_probs, axis=-1, keepdims=True)
    grad_logits = (probabilities * (grad_probs - inner)).astype(jnp.bfloat16)
    grad_queries = (
        jnp.einsum("bhqs,bshk->bqhk", grad_logits, key_rows, preferred_element_type=jnp.float32)
        * score_scale
    )
    grad_keys = (
        jnp.einsum("bhqs,bqhk->bshk", grad_logits, queries, preferred_element_type=jnp.float32)
        * score_scale
    )
    grad_values = jnp.einsum(
        "bhqs,bqhk->bshk",
        probabilities.astype(jnp.bfloat16),
        grad_out,
        preferred_element_type=jnp.float32,
    )
    return (
        grad_queries.astype(jnp.bfloat16),
        grad_keys.astype(jnp.bfloat16),
        grad_values.astype(jnp.bfloat16),
    )


def attention_forward(packed, masks, score_scale):
    members = [split_crops(member) for member in unpack_heads(packed)]
    results = []
    logsums = []
    for which in range(2):
        result, logsum = forward_tile(
            members[0][which], members[1][which], members[2][which], masks[which], score_scale
        )
        results.append(result)
        logsums.append(logsum)
    return (join_crops(results[0], results[1]).reshape(STREAM, packed.shape[2]), logsums)


def attention_backward(packed, grad_attended, logsums, masks, score_scale):
    members = [split_crops(member) for member in unpack_heads(packed)]
    grad_parts = split_crops(grad_attended.reshape(GROUP_IMG, IMG_ROWS, -1, HEAD_DIM))
    tile_grads = [
        backward_tile(
            members[0][which],
            members[1][which],
            members[2][which],
            grad_parts[which],
            masks[which],
            logsums[which],
            score_scale,
        )
        for which in range(2)
    ]
    joined = [
        join_crops(tile_grads[0][member], tile_grads[1][member]).reshape(STREAM, packed.shape[2])
        for member in range(3)
    ]
    return jnp.stack(joined)


def on_device(
    tokens,
    attn_gain,
    attn_shift,
    in_weight,
    query_value_bias,
    proj_weight,
    proj_bias,
    attn_scale,
    mlp_gain,
    mlp_shift,
    up_weight,
    up_bias,
    down_weight,
    down_bias,
    mlp_scale,
    crop_lengths,
    out_grad,
):
    wide_size = lax.axis_size("wide")
    crop_groups = wide_size // HEAD_GROUPS
    block_rows = TOK_DEV // crop_groups
    head_width = D // HEAD_GROUPS
    score_scale = HEAD_DIM ** (-0.5)
    own_group = lax.axis_index("wide") // HEAD_GROUPS
    own_lengths = lax.dynamic_slice_in_dim(crop_lengths, own_group * GROUP_IMG, GROUP_IMG, 0)
    masks = key_masks(own_lengths)
    inputs = tokens.astype(jnp.float32)
    first_gain = attn_gain.astype(jnp.float32)
    first_shift = attn_shift.astype(jnp.float32)
    normed, first_back = jax.vjp(layer_norm, inputs, first_gain, first_shift)
    normed_low = normed.astype(jnp.bfloat16)
    normed_blocks = normed_low.reshape(crop_groups, block_rows, D)
    weight_in = in_weight.reshape(D, 3, HEAD_GROUPS, head_width)
    qv_rows = query_value_bias.astype(jnp.float32)
    full_bias = jnp.stack([qv_rows[0], jnp.zeros_like(qv_rows[0]), qv_rows[1]]).reshape(
        3, 1, HEAD_GROUPS, 1, head_width
    )
    projected = (
        jnp.einsum("gbd,dchk->cghbk", normed_blocks, weight_in, preferred_element_type=jnp.float32)
        + full_bias
    )
    send_heads = projected.astype(jnp.bfloat16).reshape(3, wide_size, block_rows, head_width)
    arrived = lax.all_to_all(send_heads, "wide", split_axis=1, concat_axis=1, tiled=True)
    packed = arrived.reshape(3, STREAM, head_width)
    attended, logsums = attention_forward(packed, masks, score_scale)
    returned = lax.all_to_all(
        attended.reshape(wide_size, block_rows, head_width),
        "wide",
        split_axis=0,
        concat_axis=0,
        tiled=True,
    )
    mixed_rows = returned.reshape(crop_groups, HEAD_GROUPS, block_rows, head_width)
    weight_proj = proj_weight.reshape(HEAD_GROUPS, head_width, D)
    branch = jnp.einsum(
        "ghbk,hkd->gbd", mixed_rows, weight_proj, preferred_element_type=jnp.float32
    )
    branch = branch.reshape(TOK_DEV, D) + proj_bias.astype(jnp.float32)
    first_scale = attn_scale.astype(jnp.float32)
    middle = inputs + first_scale * branch
    second, second_back = jax.vjp(
        layer_norm, middle, mlp_gain.astype(jnp.float32), mlp_shift.astype(jnp.float32)
    )
    second_low = second.astype(jnp.bfloat16)
    hidden = jnp.dot(second_low, up_weight, preferred_element_type=jnp.float32) + up_bias.astype(
        jnp.float32
    )
    activated, gelu_back = jax.vjp(gelu_exact, hidden)
    activated_low = activated.astype(jnp.bfloat16)
    outcome = jnp.dot(
        activated_low, down_weight, preferred_element_type=jnp.float32
    ) + down_bias.astype(jnp.float32)
    second_scale = mlp_scale.astype(jnp.float32)
    output = (middle + second_scale * outcome).astype(jnp.bfloat16)
    cotangent = out_grad.astype(jnp.float32)
    grad_mlp_scale = jnp.sum(cotangent * outcome, axis=0)
    grad_outcome = (cotangent * second_scale).astype(jnp.bfloat16)
    grad_down_weight = jnp.einsum(
        "tf,td->fd", activated_low, grad_outcome, preferred_element_type=jnp.float32
    )
    grad_down_bias = jnp.sum(grad_outcome.astype(jnp.float32), axis=0)
    grad_activated = jnp.einsum(
        "td,fd->tf", grad_outcome, down_weight, preferred_element_type=jnp.float32
    )
    grad_hidden = gelu_back(grad_activated)[0].astype(jnp.bfloat16)
    grad_up_weight = jnp.einsum(
        "td,tf->df", second_low, grad_hidden, preferred_element_type=jnp.float32
    )
    grad_up_bias = jnp.sum(grad_hidden.astype(jnp.float32), axis=0)
    grad_second = jnp.einsum(
        "tf,df->td", grad_hidden, up_weight, preferred_element_type=jnp.float32
    )
    grad_middle, grad_mlp_gain, grad_mlp_shift = second_back(grad_second)
    grad_middle = grad_middle + cotangent
    grad_attn_scale = jnp.sum(grad_middle * branch, axis=0)
    grad_branch = (grad_middle * first_scale).astype(jnp.bfloat16)
    branch_blocks = grad_branch.reshape(crop_groups, block_rows, D)
    grad_proj_weight = jnp.einsum(
        "ghbk,gbd->hkd", mixed_rows, branch_blocks, preferred_element_type=jnp.float32
    ).reshape(D, D)
    grad_proj_bias = jnp.sum(grad_branch.astype(jnp.float32), axis=0)
    grad_mixed = jnp.einsum(
        "gbd,hkd->ghbk", branch_blocks, weight_proj, preferred_element_type=jnp.float32
    )
    grad_mixed = grad_mixed.astype(jnp.bfloat16).reshape(wide_size, block_rows, head_width)
    again, grad_arrived = (
        lax.all_to_all(send_heads, "wide", split_axis=1, concat_axis=1, tiled=True),
        lax.all_to_all(grad_mixed[None], "wide", split_axis=1, concat_axis=1, tiled=True),
    )
    packed_back = again.reshape(3, STREAM, head_width)
    grad_attended = grad_arrived.reshape(STREAM, head_width)
    grad_packed = attention_backward(packed_back, grad_attended, logsums, masks, score_scale)
    grad_sent = lax.all_to_all(
        grad_packed.reshape(3, wide_size, block_rows, head_width),
        "wide",
        split_axis=1,
        concat_axis=1,
        tiled=True,
    )
    grad_heads = grad_sent.reshape(3, crop_groups, HEAD_GROUPS, block_rows, head_width)
    grad_in_weight = jnp.einsum(
        "gbd,cghbk->dchk", normed_blocks, grad_heads, preferred_element_type=jnp.float32
    ).reshape(D, 3 * D)
    bias_sums = jnp.sum(grad_heads.astype(jnp.float32), axis=(1, 3)).reshape(3, D)
    grad_query_value_bias = jnp.stack([bias_sums[0], bias_sums[2]])
    grad_normed = jnp.einsum(
        "cghbk,dchk->gbd", grad_heads, weight_in, preferred_element_type=jnp.float32
    ).reshape(TOK_DEV, D)
    grad_inputs, grad_attn_gain, grad_attn_shift = first_back(grad_normed)
    input_grad = (grad_inputs + grad_middle).astype(jnp.bfloat16)
    shares = (
        lax.psum_scatter(
            grad_attn_gain.astype(jnp.bfloat16), "wide", scatter_dimension=0, tiled=True
        ).astype(jnp.float32),
        lax.psum_scatter(
            grad_attn_shift.astype(jnp.bfloat16), "wide", scatter_dimension=0, tiled=True
        ).astype(jnp.float32),
        lax.psum_scatter(
            grad_in_weight.astype(jnp.bfloat16), "wide", scatter_dimension=0, tiled=True
        ).astype(jnp.float32),
        lax.psum_scatter(
            grad_query_value_bias.astype(jnp.bfloat16), "wide", scatter_dimension=1, tiled=True
        ).astype(jnp.float32),
        lax.psum_scatter(
            grad_proj_weight.astype(jnp.bfloat16), "wide", scatter_dimension=0, tiled=True
        ).astype(jnp.float32),
        lax.psum_scatter(
            grad_proj_bias.astype(jnp.bfloat16), "wide", scatter_dimension=0, tiled=True
        ).astype(jnp.float32),
        lax.psum_scatter(
            grad_attn_scale.astype(jnp.bfloat16), "wide", scatter_dimension=0, tiled=True
        ).astype(jnp.float32),
        lax.psum_scatter(
            grad_mlp_gain.astype(jnp.bfloat16), "wide", scatter_dimension=0, tiled=True
        ).astype(jnp.float32),
        lax.psum_scatter(
            grad_mlp_shift.astype(jnp.bfloat16), "wide", scatter_dimension=0, tiled=True
        ).astype(jnp.float32),
        lax.psum_scatter(
            grad_up_weight.astype(jnp.bfloat16), "wide", scatter_dimension=0, tiled=True
        ).astype(jnp.float32),
        lax.psum_scatter(
            grad_up_bias.astype(jnp.bfloat16), "wide", scatter_dimension=0, tiled=True
        ).astype(jnp.float32),
        lax.psum_scatter(
            grad_down_weight.astype(jnp.bfloat16), "wide", scatter_dimension=0, tiled=True
        ).astype(jnp.float32),
        lax.psum_scatter(
            grad_down_bias.astype(jnp.bfloat16), "wide", scatter_dimension=0, tiled=True
        ).astype(jnp.float32),
        lax.psum_scatter(
            grad_mlp_scale.astype(jnp.bfloat16), "wide", scatter_dimension=0, tiled=True
        ).astype(jnp.float32),
    )
    results = (
        lax.psum(shares[0].astype(jnp.bfloat16), "narrow").astype(jnp.float32),
        lax.psum(shares[1].astype(jnp.bfloat16), "narrow").astype(jnp.float32),
        lax.psum(shares[2].astype(jnp.bfloat16), "narrow").astype(jnp.float32),
        lax.psum(shares[3].astype(jnp.bfloat16), "narrow").astype(jnp.float32),
        lax.psum(shares[4].astype(jnp.bfloat16), "narrow").astype(jnp.float32),
        lax.psum(shares[5].astype(jnp.bfloat16), "narrow").astype(jnp.float32),
        lax.psum(shares[6].astype(jnp.bfloat16), "narrow").astype(jnp.float32),
        lax.psum(shares[7].astype(jnp.bfloat16), "narrow").astype(jnp.float32),
        lax.psum(shares[8].astype(jnp.bfloat16), "narrow").astype(jnp.float32),
        lax.psum(shares[9].astype(jnp.bfloat16), "narrow").astype(jnp.float32),
        lax.psum(shares[10].astype(jnp.bfloat16), "narrow").astype(jnp.float32),
        lax.psum(shares[11].astype(jnp.bfloat16), "narrow").astype(jnp.float32),
        lax.psum(shares[12].astype(jnp.bfloat16), "narrow").astype(jnp.float32),
        lax.psum(shares[13].astype(jnp.bfloat16), "narrow").astype(jnp.float32),
    )
    return (
        output,
        input_grad,
        results[0],
        results[1],
        results[2],
        results[3],
        results[4],
        results[5],
        results[6],
        results[7],
        results[8],
        results[9],
        results[10],
        results[11],
        results[12],
        results[13],
    )


MESH = pl.DeviceIdType.MESH
F32 = jnp.float32
BF16 = jnp.bfloat16
SLOT = 288
ROWS = 576
UNITS = 18
PAIRS = 9
BLOCK = 48
BLOCKS = ROWS // BLOCK
CORE, Y, X, Z1, Z2, Y_WHOLE, Y_BACK, CORE_BACK, DIAGONAL = range(9)
STAGES = {
    "A": (CORE, X, Z1, Z2, Y_WHOLE, CORE_BACK),
    "B": (CORE, Y, X, Z1, Z2, Y_BACK, CORE_BACK),
    "C": (CORE, Z1, Z2, X, Y_WHOLE, CORE_BACK),
    "D": (CORE, Y, Z1, Z2, X, Y_BACK, CORE_BACK),
    "E": (CORE, X, Y, Z1, Z2, Y_BACK, CORE_BACK),
}
AXES = (CORE, X, Y, Z1, Z2)
KINDS = "BBCADBEADBEBEEBEEE"
PLAN = (
    (),
    (),
    ((0, -1), (1, -1),),
    ((2, -1), (3, -1),),
    (),
    ((0, 0),),
    ((1, 0), (2, 0),),
    ((3, 0),),
    ((0, 1),),
    ((4, -1), (5, -1),),
    ((6, -1), (7, -1), (2, 1),),
    (),
    ((4, 0), (5, 0), (1, 1), (3, 1),),
    ((6, 0), (7, 0), (0, 2),),
    ((1, 2), (2, 2),),
    ((4, 1), (3, 2), (0, 3),),
    ((8, -1), (9, -1), (1, 3),),
    ((10, -1), (11, -1), (6, 1),),
    ((5, 1), (8, 0), (4, 2),),
    ((9, 0),),
    ((10, 0), (11, 0), (7, 1), (6, 2), (2, 3), (3, 3), (0, 4),),
    ((5, 2), (1, 4),),
    ((18, -1), (8, 1), (4, 3),),
    (),
    ((12, -1), (7, 2),),
    ((18, 0), (9, 1), (10, 1), (12, 0), (5, 3), (6, 3),),
    (),
    ((13, -1), (4, 4),),
    ((14, -1), (11, 1), (18, 1),),
    ((13, 0), (14, 0), (8, 2), (9, 2), (2, 4), (3, 4), (0, 5), (1, 5),),
    ((10, 2), (7, 3), (5, 4), (6, 4), (2, 5), (3, 5), (4, 5), (0, 6), (1, 6), (12, 1),),
    ((15, -1), (18, 2),),
    ((11, 2), (8, 3), (9, 3), (10, 3), (4, 6), (15, 0),),
    ((14, 1), (11, 3), (18, 3), (7, 4),),
    ((16, -1), (13, 1), (8, 4), (9, 4), (5, 5), (6, 5),),
    ((17, -1), (7, 5), (10, 4),),
    ((12, 2), (16, 0), (11, 4), (5, 6), (6, 6),),
    ((17, 0), (15, 1), (13, 2), (8, 5),),
    ((12, 3), (18, 4), (9, 5), (14, 2), (10, 5), (11, 5),),
    ((13, 3), (8, 6), (9, 6), (10, 6), (11, 6), (15, 2),),
    ((19, -1), (16, 1), (14, 3), (12, 4),),
    ((13, 4), (15, 3), (19, 0), (16, 2), (17, 1), (12, 5), (13, 5), (12, 6), (13, 6), (14, 4), (17, 2), (15, 4), (14, 5), (16, 3), (19, 1), (15, 5), (14, 6), (17, 3), (19, 2), (15, 6), (16, 4), (17, 4), (19, 3), (16, 5), (17, 5), (16, 6), (19, 4), (17, 6),),
)
ATTN_GAIN, ATTN_SHIFT, Q_BIAS, V_BIAS, PROJ_BIAS, ATTN_SCALE, MLP_GAIN, MLP_SHIFT, DOWN_BIAS, MLP_SCALE = range(10)
UP_BIAS = 10
EARLY_ROWS = (PROJ_BIAS, ATTN_SCALE, MLP_GAIN, MLP_SHIFT, DOWN_BIAS, MLP_SCALE)
LATE_ROWS = (ATTN_GAIN, ATTN_SHIFT, Q_BIAS, V_BIAS)


def dot_nn(a, b):
    return jnp.dot(a, b, preferred_element_type=F32)


def dot_nt(a, b):
    return lax.dot_general(a, b, (((1,), (1,)), ((), ())), preferred_element_type=F32)


def dot_tn(a, b):
    return lax.dot_general(a, b, (((0,), (0,)), ((), ())), preferred_element_type=F32)


def halves(block):
    lanes = lax.broadcasted_iota(jnp.int32, block.shape, 1)
    zero = jnp.zeros_like(block)
    return [jnp.where((lanes < 64) == (h == 0), block, zero) for h in range(2)]


def fold_rows(values):
    return jnp.sum(values.reshape(values.shape[0] // 8, 8, values.shape[1]), axis=0)


def norm_parts(values):
    mean = jnp.sum(values, axis=-1, keepdims=True) * (1.0 / D)
    centered = values - mean
    variance = jnp.sum(centered * centered, axis=-1, keepdims=True) * (1.0 / D)
    rstd = lax.rsqrt(variance + NORM_EPSILON)
    return centered * rstd, rstd


def layer_kernel(
    tok_ref, og_ref, len_ref,
    attn_gain_ref, attn_shift_ref, qv_ref, proj_bias_ref, attn_scale_ref, mlp_gain_ref, mlp_shift_ref,
    up_bias_ref, down_bias_ref, mlp_scale_ref,
    in_hbm, proj_hbm, up_hbm, down_hbm,
    out_hbm, ig_hbm, gin_ref, gproj_ref, gup_ref, gdown_ref, vout_ref,
    win, wproj, wup, wdown,
    xb, db, ob, h1, t1, t2, qkv, att, branch, mid, h2, dm, gact, dhid, macc, dacc, ub, gb, bias, bias_t,
    prm, qkv_row, sums, usums,
    gbuf, r0, r1, r2, r3, r4, fin, wdt, early, early_in, late, late_in,
    wsem, upsem, lsem, hsend, hrecv, ssem, rsem, vssem, vrsem,
):
    n = lax.axis_index("narrow")
    w = lax.axis_index("wide")
    c = n % 2
    y = n // 2
    x = w % 2
    z1 = (w // 2) % 2
    z2 = w // 4
    quarter = w % 4
    shift = 32 * (quarter % 2) + 32 * (quarter // 2) * (2 - 2 * (quarter % 2)) + 0 * quarter
    partner = {
        CORE: (n + 1 - 2 * c, w),
        Y: (n + 2 - 4 * y, w),
        X: (n, w + 1 - 2 * x),
        Z1: (n, w + 2 - 4 * z1),
        Z2: (n, w + 4 - 8 * z2),
        DIAGONAL: (n, w + 3 - 2 * quarter),
    }

    weights = [
        pltpu.make_async_copy(in_hbm, win, wsem.at[0]),
        pltpu.make_async_copy(proj_hbm, wproj, wsem.at[1]),
    ]
    downs = [pltpu.make_async_copy(down_hbm.at[:, j], wdown.at[j], wsem.at[2 + j]) for j in range(3)]
    ups = [
        [
            pltpu.make_async_copy(
                up_hbm.at[:, 128 * (3 * s + j) : 128 * (3 * s + j + 1)],
                wup.at[:, 128 * (8 * j + s) : 128 * (8 * j + s + 1)],
                upsem.at[j],
            )
            for s in range(8)
        ]
        for j in range(3)
    ]
    own = pl.ds(pl.multiple_of(64 - shift, 32), 256)
    loads = [
        pltpu.make_async_copy(tok_ref, xb.at[:, own], lsem.at[0]),
        pltpu.make_async_copy(og_ref, db.at[:, own], lsem.at[1]),
    ]
    loads[0].start()
    weights[0].start()
    loads[1].start()
    weights[1].start()
    for j in range(3):
        for s in range(8):
            ups[j][s].start()
        downs[j].start()

    barrier = pltpu.get_barrier_semaphore()
    for target in partner.values():
        pl.semaphore_signal(barrier, inc=1, device_id=target, device_id_type=MESH)

    before_shift = 32 * ((quarter + 3) % 2) + 32 * ((quarter - 1) // 2) * (2 - 2 * ((quarter + 3) % 2))
    before = (n, w - 1)
    after = (n, w + 1)

    def halo_in(src, dst, i, k):
        return pltpu.make_async_remote_copy(
            src_ref=src.at[i, 0:64],
            dst_ref=dst.at[i, pl.ds(pl.multiple_of(320 - before_shift, 32), 64)],
            send_sem=hsend.at[k + i], recv_sem=hrecv.at[k + i], device_id=before, device_id_type=MESH,
        )

    def halo_back(buf, k, size):
        return pltpu.make_async_remote_copy(
            src_ref=buf.at[:, pl.ds(pl.multiple_of(320 - shift, 32), size)],
            dst_ref=buf.at[:, 64 - size : 64],
            send_sem=hsend.at[k], recv_sem=hrecv.at[k], device_id=after, device_id_type=MESH,
        )

    for row, ref in (
        (ATTN_GAIN, attn_gain_ref), (ATTN_SHIFT, attn_shift_ref), (PROJ_BIAS, proj_bias_ref), (ATTN_SCALE, attn_scale_ref),
        (MLP_GAIN, mlp_gain_ref), (MLP_SHIFT, mlp_shift_ref), (DOWN_BIAS, down_bias_ref), (MLP_SCALE, mlp_scale_ref),
    ):
        prm[row : row + 1, 0:D] = ref[...].astype(F32).reshape(1, D)
    qv = qv_ref[...].astype(F32)
    qkv_row[:, 0:D] = qv[0:1]
    qkv_row[:, D : 2 * D] = jnp.zeros((1, D), F32)
    qkv_row[:, 2 * D : 3 * D] = qv[1:2]
    up_row = up_bias_ref[...].astype(F32).reshape(1, 4 * D)
    for j in range(3):
        for s in range(8):
            prm[UP_BIAS + j : UP_BIAS + j + 1, 128 * s : 128 * (s + 1)] = up_row[:, 128 * (3 * s + j) : 128 * (3 * s + j + 1)]
    sums[...] = jnp.zeros_like(sums)
    usums[...] = jnp.zeros_like(usums)

    def param(row):
        return prm[row : row + 1, 0:D]

    is_local = quarter // 2
    for i in range(2):
        image = 2 * i + z2

        def crop_of(axis, valid_only):
            shape = (1, SLOT) if axis == 1 else (SLOT, 1)
            place = lax.broadcasted_iota(jnp.int32, shape, axis)
            ids = jnp.full(shape, -1 if valid_only else 4, jnp.int32)
            for m in range(4):
                start = 56 * m * is_local
                if valid_only:
                    local_length = len_ref[image, 2 + 4 * (quarter % 2) + m]
                    global_length = len_ref[image, quarter % 2] if m == 0 else 0
                    size = is_local * local_length + (1 - is_local) * global_length
                else:
                    size = 56 * is_local + (1 - is_local) * (SLOT if m == 0 else 0)
                inside = jnp.logical_and(place >= start, place < start + size)
                ids = jnp.where(inside, m, ids)
            return ids

        bias[i] = jnp.where(crop_of(0, False) == crop_of(1, True), 0.0, MASKED)
        bias_t[i] = jnp.where(crop_of(1, False) == crop_of(0, True), 0.0, MASKED)

    pl.semaphore_wait(barrier, 6)

    @pl.when(quarter > 0)
    def _():
        for i in range(2):
            halo_in(tok_ref, xb, i, 0).start()
        for i in range(2):
            halo_in(og_ref, db, i, 2).start()

    def take_halo(src, dst, i, k):
        @pl.when(quarter > 0)
        def _():
            halo_in(src, dst, i, k).wait_send()

        @pl.when(quarter < 3)
        def _():
            halo_in(src, dst, i, k).wait_recv()

        @pl.when(quarter > 1)
        def _():
            dst[i, 288:352] = jnp.zeros((64, D), BF16)

    def at(b):
        i, k = b // 6, b % 6
        return i, pl.ds(pl.multiple_of(64 + BLOCK * k, 16), BLOCK), pl.ds(pl.multiple_of(BLOCK * b, 16), BLOCK)

    def first_norm(b):
        i, slots, rows = at(b)
        normed, _ = norm_parts(xb[i, slots].astype(F32))
        h1[rows] = (normed * param(ATTN_GAIN) + param(ATTN_SHIFT)).astype(BF16)

    def project(pieces):
        rows = jnp.concatenate([h1[piece] for piece, _ in pieces], axis=0)

        def tile_of(tile, _):
            cols = pl.ds(pl.multiple_of(256 * tile, 256), 256)
            result = (dot_nn(rows, win[:, cols]) + qkv_row[:, cols]).astype(BF16)
            result = jnp.where(tile < 3, result * jnp.asarray(0.125, BF16), result)
            done = 0
            for piece, size in pieces:
                qkv[piece, cols] = result[done : done + size]
                done += size
            return 0

        lax.fori_loop(0, 9, tile_of, 0, unroll=3)

    def pair_at(index):
        i, h = index % 2, index // 2
        rows = pl.ds(pl.multiple_of(SLOT * i, 16), SLOT)
        return i, rows, [pl.ds(pl.multiple_of(D * m + 128 * h, 128), 128) for m in range(3)]

    def attend(index, _):
        i, rows, cols = pair_at(index)
        q, v = qkv[rows, cols[0]], qkv[rows, cols[2]]
        keys = halves(qkv[rows, cols[1]])
        lanes = lax.broadcasted_iota(jnp.int32, (SLOT, 128), 1)
        ones = jnp.ones_like(v)
        parts = []
        for h in range(2):
            s = dot_nt(q, keys[h]) + bias[i]
            e = jnp.exp(s - jnp.max(s, axis=-1, keepdims=True)).astype(BF16)
            part = dot_nn(e, jnp.where((lanes < 64) == (h == 0), v, ones))
            parts.append(part / pltpu.roll(part, 64, 1))
        att[rows, cols[0]] = jnp.where(lanes < 64, parts[0], parts[1]).astype(BF16)
        return 0

    loads[0].wait()
    for b in (0, 1, 2, 3, 6, 7, 8, 9):
        first_norm(b)
    weights[0].wait()
    project([(slice(SLOT * i, SLOT * i + 192), 192) for i in range(2)])

    def attend_image(i, _):
        take_halo(tok_ref, xb, i, 0)
        for k in (4, 5):
            first_norm(6 * i + k)
        project([(pl.ds(pl.multiple_of(SLOT * i + 192, 16), 96), 96)])

        def heads(h, _):
            return attend(2 * h + i, 0)

        lax.fori_loop(0, 6, heads, 0, unroll=2)
        return 0

    lax.fori_loop(0, 2, attend_image, 0)

    weights[1].wait()
    for tile in range(3):
        cols = slice(256 * tile, 256 * (tile + 1))
        result = dot_nn(att[...], wproj[:, cols]) + prm[PROJ_BIAS : PROJ_BIAS + 1, cols]
        branch[:, cols] = result.astype(BF16)
        scaled = prm[ATTN_SCALE : ATTN_SCALE + 1, cols] * result
        for i in range(2):
            mid[SLOT * i : SLOT * (i + 1), cols] = (
                xb[i, 64 : 64 + SLOT, cols].astype(F32) + scaled[SLOT * i : SLOT * (i + 1)]
            )

    loads[1].wait()
    for i in range(2):
        take_halo(og_ref, db, i, 2)

    def second_norm(b, _):
        i, slots, rows = at(b)
        low = (db[i, slots].astype(F32) * param(MLP_SCALE)).astype(BF16)
        dm[rows] = low
        sums[DOWN_BIAS] += fold_rows(low.astype(F32))
        normed, _ = norm_parts(mid[rows])
        h2[rows] = (normed * param(MLP_GAIN) + param(MLP_SHIFT)).astype(BF16)
        return 0

    lax.fori_loop(0, BLOCKS, second_norm, 0, unroll=3)

    def transpose_into(dst, src):
        for k in range(6):
            dst[128 * k : 128 * (k + 1)] = src[:, 128 * k : 128 * (k + 1)].T

    def copy(src, dst, unit, stage, axis):
        return pltpu.make_async_remote_copy(
            src_ref=src, dst_ref=dst,
            send_sem=ssem.at[unit % ssem.shape[0]], recv_sem=rsem.at[unit % rsem.shape[0], stage],
            device_id=partner[axis], device_id_type=MESH,
        )

    bits = {CORE: c, Y: y, X: x, Z1: z1, Z2: z2}
    over = {Y_WHOLE: Y, Y_BACK: Y, CORE_BACK: CORE}
    landing = (r0, r1, r2, r3, r4)

    def share(u, letter, k, mine):
        stages = STAGES[letter]
        index = [u]
        for axis in bits:
            if axis in stages[:k]:
                index.append(bits[axis])
            elif axis == stages[k]:
                index.append(bits[axis] if mine else 1 - bits[axis])
            else:
                index.append(slice(None))
        return gbuf.at[tuple(index)]

    def transfer(u, letter, k):
        stage = STAGES[letter][k]
        slot = u % fin.shape[0]
        if stage == CORE_BACK:
            return copy(fin.at[slot, c], fin.at[slot, c], u, k, CORE)
        if stage == Y_BACK:
            return copy(fin.at[slot, c, y], fin.at[slot, c, y], u, k, Y)
        dst = landing[k].at[u % landing[k].shape[0]]
        if k == 4 and stage != Y_WHOLE:
            dst = dst.at[0]
        return copy(share(u, letter, k, False), dst, u, k, over.get(stage, stage))

    def add(dst, src):
        dst[...] = (dst[...].astype(F32) + src[...].astype(F32)).astype(BF16)

    def land(u, letter, k):
        stage = STAGES[letter][k]
        if stage in (Y_BACK, CORE_BACK):
            return
        slot = u % fin.shape[0]
        src = landing[k].at[u % landing[k].shape[0]]
        own = share(u, letter, k, True)
        if k == 0:

            def body(index, _):
                add(own.at[index // 2, index % 2], src.at[index // 2, index % 2])
                return 0

            lax.fori_loop(0, 4, body, 0)
        elif k < 4:
            add(own, src)
        elif stage == Y_WHOLE:
            fin[slot, c] = (own[...].astype(F32) + src[...].astype(F32)).astype(BF16)
        else:
            fin[slot, c, y] = (own[...].astype(F32) + src[0].astype(F32)).astype(BF16)

    def in_tile(index):
        return 3 * ((index - 3) % 3) + (index - 3) // 3

    def write_out(u):
        p, a = u // 2, u % 2
        slot = u % fin.shape[0]
        for sub in range(4):
            block = fin[slot, sub // 2, sub % 2]
            if p >= 6:
                index = 2 * (u - 12) + sub // 2
                dst, tile = (gproj_ref, index) if index < 3 else (gin_ref, in_tile(index))
                start = 256 * tile + 128 * (sub % 2)
                dst[:, start : start + 128] = block
            elif p % 2 == 1:
                start = 128 * (3 * (4 * a + sub) + p // 2)
                gup_ref[:, start : start + 128] = block
            else:
                wdt[384 * a + 96 * sub : 384 * a + 96 * (sub + 1), 64 * p : 64 * p + 128] = block

    def vector_event(buf, arrived, which, k):
        def exchange(stage):
            return pltpu.make_async_remote_copy(
                src_ref=buf.at[stage], dst_ref=arrived.at[stage], send_sem=vssem.at[which],
                recv_sem=vrsem.at[which, stage], device_id=partner[AXES[stage]], device_id_type=MESH,
            )

        if k >= 0:
            exchange(k).wait()
            buf[k + 1] = (buf[k].astype(F32) + arrived[k].astype(F32)).astype(buf.dtype)
        if k < 4:
            exchange(k + 1).start()

    def event(u, k):
        if u >= UNITS:
            vector_event((early, late)[u - UNITS], (early_in, late_in)[u - UNITS], u - UNITS, k)
            return
        letter = KINDS[u]
        if k >= 0:
            transfer(u, letter, k).wait()
            land(u, letter, k)
        if k + 1 < len(STAGES[letter]):
            transfer(u, letter, k + 1).start()
        else:
            write_out(u)

    polls = iter(PLAN)

    def poll():
        for u, k in next(polls):
            event(u, k)

    transpose_into(t1, dm)

    def gelu_block(j, tile, b):
        _, _, rows = at(b)
        cols = pl.ds(pl.multiple_of(256 * tile, 256), 256)
        u = ub[rows] + prm[pl.ds(UP_BIAS + j, 1), cols]
        phi = 0.5 * (1.0 + lax.erf(u * 0.7071067811865476))
        gact[rows, cols] = (u * phi).astype(BF16)
        slope = phi + u * (jnp.exp(u * u * -0.5) * 0.3989422804014327)
        low = (gb[rows] * slope).astype(BF16)
        dhid[rows, cols] = low
        usums[:, pl.ds(pl.multiple_of(1024 * j + 256 * tile, 256), 256)] += fold_rows(low.astype(F32))

    def mlp(j):
        part = wup.at[:, 1024 * j : 1024 * (j + 1)]
        pltpu.make_async_copy(up_hbm.at[:, 0:1024], part, upsem.at[j]).wait()
        downs[j].wait()

        def hidden_tile(tile, _):
            cols = pl.ds(pl.multiple_of(1024 * j + 256 * tile, 256), 256)
            ub[...] = dot_nn(h2[...], wup[:, cols])
            down = wdown[j, pl.ds(2 * tile, 2)].reshape(256, D)
            gb[...] = dot_nt(dm[...], down)

            def block(b, _):
                gelu_block(j, tile, b)
                return 0

            lax.fori_loop(0, BLOCKS, block, 0, unroll=3)
            return 0

        def down_grad(nt, _):
            result = dot_nn(t1[...], gact[:, pl.ds(pl.multiple_of(256 * nt, 256), 256)])
            for ss in range(2):
                for sub in range(8):
                    gbuf[4 * j + sub // 4, (sub // 2) % 2, sub % 2, ss, nt % 2, nt // 2] = result[
                        96 * sub : 96 * (sub + 1), 128 * ss : 128 * (ss + 1)
                    ].astype(BF16)
            return 0

        def up_grad(nt, _):
            result = dot_nn(t2[...], dhid[:, pl.ds(pl.multiple_of(256 * nt, 256), 256)])
            for s in range(8):
                for yy in range(2):
                    gbuf[4 * j + 2 + nt // 2, nt % 2, yy, s % 2, (s // 2) % 2, s // 4] = result[
                        96 * s : 96 * (s + 1), 128 * yy : 128 * (yy + 1)
                    ].astype(BF16)
            return 0

        def combine(nt):
            cols = slice(256 * nt, 256 * (nt + 1))
            more = dot_nn(gact[...], wdown[j, :, :, cols].reshape(1024, 256))
            more_d = dot_nt(dhid[...], wup[cols, 1024 * j : 1024 * (j + 1)])
            macc[:, cols] = more if j == 0 else macc[:, cols] + more
            dacc[:, cols] = more_d if j == 0 else dacc[:, cols] + more_d

        lax.fori_loop(0, 2, hidden_tile, 0)
        poll()
        lax.fori_loop(2, 4, hidden_tile, 0)
        poll()
        lax.fori_loop(0, 4, down_grad, 0, unroll=2)
        poll()
        if j == 0:
            transpose_into(t2, h2)
        lax.fori_loop(0, 4, up_grad, 0, unroll=2)
        poll()
        for nt in range(3):
            combine(nt)
            poll()

    for j in range(3):
        mlp(j)

    transpose_into(t1, h1)
    transpose_into(t2, att)

    def second_back(b, _):
        i, slots, rows = at(b)
        grad = db[i, slots].astype(F32)
        y_rows = mid[rows]
        outcome = macc[rows] + param(DOWN_BIAS)
        ob[i, slots] = (y_rows + param(MLP_SCALE) * outcome).astype(BF16)
        sums[MLP_SCALE] += fold_rows(grad * outcome)
        normed, rstd = norm_parts(y_rows)
        dh = dacc[rows]
        sums[MLP_GAIN] += fold_rows(dh * normed)
        sums[MLP_SHIFT] += fold_rows(dh)
        e = dh * param(MLP_GAIN)
        mean_e = jnp.sum(e, axis=-1, keepdims=True) * (1.0 / D)
        mean_en = jnp.sum(e * normed, axis=-1, keepdims=True) * (1.0 / D)
        dy = grad + rstd * (e - mean_e - normed * mean_en)
        dacc[rows] = dy
        sums[ATTN_SCALE] += fold_rows(dy * branch[rows].astype(F32))
        low = (dy * param(ATTN_SCALE)).astype(BF16)
        dm[rows] = low
        sums[PROJ_BIAS] += fold_rows(low.astype(F32))
        return 0

    lax.fori_loop(0, 6, second_back, 0, unroll=2)
    poll()
    lax.fori_loop(6, BLOCKS, second_back, 0, unroll=2)

    def give_back(buf, k):
        @pl.when(quarter % 2 == 0)
        def _():
            halo_back(buf, k, 32).start()

        @pl.when(quarter == 1)
        def _():
            halo_back(buf, k, 64).start()

    def take_back(buf, k):
        @pl.when(quarter % 2 == 0)
        def _():
            halo_back(buf, k, 32).wait_send()

        @pl.when(quarter == 1)
        def _():
            halo_back(buf, k, 64).wait_send()

        @pl.when(quarter % 2 == 1)
        def _():
            halo_back(buf, k, 32).wait_recv()

        @pl.when(quarter == 2)
        def _():
            halo_back(buf, k, 64).wait_recv()

    give_back(ob, 4)
    rows = [jnp.sum(sums[row], axis=0, keepdims=True) for row in EARLY_ROWS]
    for index, row in enumerate(rows):
        early[0, index : index + 1, 0:D] = row.astype(BF16)
    for j in range(3):
        early[0, 6 + j : 7 + j] = jnp.sum(usums[:, 1024 * j : 1024 * (j + 1)], axis=0, keepdims=True).astype(BF16)
    poll()

    for tile in range(3):
        cols = slice(256 * tile, 256 * (tile + 1))
        h2[:, cols] = dot_nt(dm[...], wproj[cols]).astype(BF16)

    def attend_back(index, _):
        i, rows, cols = pair_at(index)
        k, v = qkv[rows, cols[1]], qkv[rows, cols[2]]
        queries, keys, grads = halves(qkv[rows, cols[0]]), halves(k), halves(h2[rows, cols[0]])
        dq = dk = dv = None
        for h in range(2):
            s = dot_nt(k, queries[h]) + bias_t[i]
            e = jnp.exp(s - jnp.max(s, axis=0, keepdims=True))
            p = e * (1.0 / jnp.sum(e, axis=0, keepdims=True))
            dp = dot_nt(v, grads[h])
            ds = (p * (dp - jnp.sum(p * dp, axis=0, keepdims=True))).astype(BF16)
            parts = dot_tn(ds, keys[h]), dot_nn(ds, queries[h]), dot_nn(p.astype(BF16), grads[h])
            dq, dk, dv = parts if dq is None else (dq + parts[0], dk + parts[1], dv + parts[2])
        low_q, low_v = (dq * 0.125).astype(BF16), dv.astype(BF16)
        qkv[rows, cols[0]] = low_q
        qkv[rows, cols[1]] = dk.astype(BF16)
        qkv[rows, cols[2]] = low_v
        sums[Q_BIAS, :, cols[0]] += fold_rows(low_q.astype(F32))
        sums[V_BIAS, :, cols[0]] += fold_rows(low_v.astype(F32))
        return 0

    def attn_grad(u):
        for half in range(2):
            index = 2 * (u - 12) + half
            if index < 3:
                result = dot_nn(t2[...], dm[:, 256 * index : 256 * (index + 1)])
            else:
                result = dot_nn(t1[...], qkv[:, 256 * in_tile(index) : 256 * (in_tile(index) + 1)])
            for s in range(8):
                for yy in range(2):
                    gbuf[u, half, yy, s % 2, (s // 2) % 2, s // 4] = result[
                        96 * s : 96 * (s + 1), 128 * yy : 128 * (yy + 1)
                    ].astype(BF16)
        poll()

    poll()
    attn_grad(12)
    for m in range(3):
        lax.fori_loop(4 * m, 4 * m + 2, attend_back, 0)
        poll()
        lax.fori_loop(4 * m + 2, 4 * m + 4, attend_back, 0)
        poll()
        for u in ((13, 14), (15,), (16, 17))[m]:
            attn_grad(u)

    for tile in range(3):
        cols = slice(256 * tile, 256 * (tile + 1))
        macc[:, cols] = dot_nt(qkv[...], win[cols])
        poll()

    def first_back(b, _):
        i, slots, rows = at(b)
        normed, rstd = norm_parts(xb[i, slots].astype(F32))
        dh = macc[rows]
        sums[ATTN_GAIN] += fold_rows(dh * normed)
        sums[ATTN_SHIFT] += fold_rows(dh)
        e = dh * param(ATTN_GAIN)
        mean_e = jnp.sum(e, axis=-1, keepdims=True) * (1.0 / D)
        mean_en = jnp.sum(e * normed, axis=-1, keepdims=True) * (1.0 / D)
        db[i, slots] = (dacc[rows] + rstd * (e - mean_e - normed * mean_en)).astype(BF16)
        return 0

    lax.fori_loop(0, 6, first_back, 0, unroll=2)
    poll()
    lax.fori_loop(6, BLOCKS, first_back, 0, unroll=2)
    give_back(db, 5)

    late[0] = jnp.zeros_like(late[0])
    for index, row in enumerate(LATE_ROWS):
        late[0, index : index + 1] = jnp.sum(sums[row], axis=0, keepdims=True)
    poll()
    poll()

    turn = (D - 96 * w) % D
    vout_ref[0:6] = pltpu.roll(early[5, :, 0:D].astype(F32), turn, 1)[0:6, 0:128]
    vout_ref[6:9] = early[5, 6:9, pl.ds(pl.multiple_of(128 * w, 128), 128)].astype(F32)
    vout_ref[16:24] = pltpu.roll(late[5], turn, 1)[:, 0:128]

    for a in range(3):
        for b in range(6):
            gdown_ref[128 * a : 128 * (a + 1), 128 * b : 128 * (b + 1)] = wdt[
                128 * b : 128 * (b + 1), 128 * a : 128 * (a + 1)
            ].T

    take_back(ob, 4)
    take_back(db, 5)
    stores = [
        pltpu.make_async_copy(ob.at[:, own], out_hbm, lsem.at[0]),
        pltpu.make_async_copy(db.at[:, own], ig_hbm, lsem.at[1]),
    ]
    for store in stores:
        store.start()
    for store in stores:
        store.wait()


def layer(tokens, out_grad, lengths, vectors, weights):
    vm = pl.BlockSpec(memory_space=pltpu.VMEM)
    hbm = pl.BlockSpec(memory_space=pl.ANY)
    dma = pltpu.SemaphoreType.DMA
    slots = pltpu.VMEM((2, 384, D), BF16)
    square = pltpu.VMEM((ROWS, D), BF16)
    wide_square = pltpu.VMEM((ROWS, D), F32)
    block = (96, 128)
    return pl.pallas_call(
        layer_kernel,
        out_shape=(
            jax.ShapeDtypeStruct((2, 256, D), BF16),
            jax.ShapeDtypeStruct((2, 256, D), BF16),
            jax.ShapeDtypeStruct((96, 3 * D), BF16),
            jax.ShapeDtypeStruct((96, D), BF16),
            jax.ShapeDtypeStruct((96, 4 * D), BF16),
            jax.ShapeDtypeStruct((384, D), BF16),
            jax.ShapeDtypeStruct((24, 128), F32),
        ),
        in_specs=[hbm, hbm, pl.BlockSpec(memory_space=pltpu.SMEM)] + [vm] * 10 + [hbm] * 4,
        out_specs=(hbm, hbm, vm, vm, vm, vm, vm),
        scratch_shapes=[
            pltpu.VMEM((D, 3 * D), BF16),
            pltpu.VMEM((D, D), BF16),
            pltpu.VMEM((D, 4 * D), BF16),
            pltpu.VMEM((3, 8, 128, D), BF16),
            slots, slots, slots,
            square,
            pltpu.VMEM((D, ROWS), BF16),
            pltpu.VMEM((D, ROWS), BF16),
            pltpu.VMEM((ROWS, 3 * D), BF16),
            square, square,
            wide_square,
            square, square,
            pltpu.VMEM((ROWS, 1024), BF16),
            pltpu.VMEM((ROWS, 1024), BF16),
            wide_square, wide_square,
            pltpu.VMEM((ROWS, 256), F32),
            pltpu.VMEM((ROWS, 256), F32),
            pltpu.VMEM((2, SLOT, SLOT), F32),
            pltpu.VMEM((2, SLOT, SLOT), F32),
            pltpu.VMEM((16, 1024), F32),
            pltpu.VMEM((1, 3 * D), F32),
            pltpu.VMEM((10, 8, D), F32),
            pltpu.VMEM((8, 4 * D), F32),
            pltpu.VMEM((UNITS, 2, 2, 2, 2, 2) + block, BF16),
            pltpu.VMEM((8, 2, 2, 2, 2) + block, BF16),
            pltpu.VMEM((12, 2, 2, 2) + block, BF16),
            pltpu.VMEM((8, 2, 2) + block, BF16),
            pltpu.VMEM((12, 2) + block, BF16),
            pltpu.VMEM((12, 2) + block, BF16),
            pltpu.VMEM((12, 2, 2) + block, BF16),
            pltpu.VMEM((D, 384), BF16),
            pltpu.VMEM((6, 16, 1024), BF16),
            pltpu.VMEM((5, 16, 1024), BF16),
            pltpu.VMEM((6, 8, D), F32),
            pltpu.VMEM((5, 8, D), F32),
            dma((5,)), dma((3,)), dma((2,)), dma((6,)), dma((6,)),
            dma((12,)), dma((12, 7)), dma((2,)), dma((2, 5)),
        ],
        compiler_params=pltpu.CompilerParams(collective_id=0, has_side_effects=True, vmem_limit_bytes=64 << 20),
        name="layer",
    )(tokens, out_grad, lengths, *vectors, *weights)


def finish_kernel(
    out_in, ig_in, in_ref, proj_ref, up_ref, down_ref, v_ref,
    out_ref, ig_ref, ag_ref, as_ref, gin_ref, qv_ref, gproj_ref, pb_ref, sc_ref, mg_ref, ms_ref, gup_ref, ub_ref,
    gdown_ref, bd_ref, sm_ref,
):
    out_ref[...] = out_in[...]
    ig_ref[...] = ig_in[...]
    for src, dst in ((in_ref, gin_ref), (proj_ref, gproj_ref), (up_ref, gup_ref), (down_ref, gdown_ref)):
        dst[...] = src[...].astype(F32)
    for row, dst in zip((0, 1, 2, 3, 4, 5, 16, 17), (pb_ref, sc_ref, mg_ref, ms_ref, bd_ref, sm_ref, ag_ref, as_ref)):
        dst[...] = v_ref[row, 0:96]
    qv_ref[...] = v_ref[18:20, 0:96]
    for j in range(3):
        ub_ref[128 * j : 128 * (j + 1)] = v_ref[6 + j]


def finish(output, input_grad, g_in, g_proj, g_up, g_down, v):
    vm = pl.BlockSpec(memory_space=pltpu.VMEM)
    row = jax.ShapeDtypeStruct((96,), F32)

    def wide(shape):
        return jax.ShapeDtypeStruct(shape, F32)

    rows = jax.ShapeDtypeStruct((TOK_DEV, D), BF16)
    return pl.pallas_call(
        finish_kernel,
        out_shape=(
            rows, rows, row, row, wide((96, 3 * D)), wide((2, 96)), wide((96, D)), row, row, row, row, wide((96, 4 * D)),
            wide((384,)), wide((384, D)), row, row,
        ),
        in_specs=[vm] * 7,
        out_specs=(vm,) * 16,
        name="finish",
    )(output.reshape(TOK_DEV, D), input_grad.reshape(TOK_DEV, D), g_in, g_proj, g_up, g_down, v)


def on_device_local(
    tokens, attn_gain, attn_shift, in_weight, query_value_bias, proj_weight, proj_bias, attn_scale,
    mlp_gain, mlp_shift, up_weight, up_bias, down_weight, down_bias, mlp_scale, crop_lengths, out_grad,
):
    output, input_grad, g_in, g_proj, g_up, g_down, v = layer(
        tokens.reshape(2, 256, D), out_grad.reshape(2, 256, D), crop_lengths,
        (attn_gain, attn_shift, query_value_bias, proj_bias, attn_scale, mlp_gain, mlp_shift, up_bias, down_bias, mlp_scale),
        (in_weight, proj_weight, up_weight, down_weight.reshape(8, 3, 128, D)),
    )
    return finish(output, input_grad, g_in, g_proj, g_up, g_down, v)


def solution(mesh):
    local = mesh.shape["wide"] == 8 and mesh.shape["narrow"] == 4
    return jax.shard_map(
        on_device_local if local else on_device,
        mesh=mesh,
        in_specs=(
            P(("narrow", "wide"), None),
            P(),
            P(),
            P(),
            P(),
            P(),
            P(),
            P(),
            P(),
            P(),
            P(),
            P(),
            P(),
            P(),
            P(),
            P("narrow", None),
            P(("narrow", "wide"), None),
        ),
        out_specs=(
            P(("narrow", "wide"), None),
            P(("narrow", "wide"), None),
            P("wide"),
            P("wide"),
            P("wide", None),
            P(None, "wide"),
            P("wide", None),
            P("wide"),
            P("wide"),
            P("wide"),
            P("wide"),
            P("wide", None),
            P("wide"),
            P("wide", None),
            P("wide"),
            P("wide"),
        ),
        check_vma=False,
    )
```
